32 devices in a mesh: gx: 2 (over x), gy: 4 (over y, core), gz: 4 (over z).
Axes of the slice: x: 2, y: 2, z: 4, core: 2. Of those that a mesh axis runs over, the one named last changes fastest.
Arguments:
- t_matrix: float32 [1, 2, 4, 16, 1024], P(None, 'gx', 'gy', 'gz'), may hold values from -3 to 3
- structure: float32 [1, 1440, 1440], replicated, may hold values from -0.0390625 to 0.0390625
- species: int32 [2, 4, 16], P('gx', 'gy', 'gz'), may hold values from 0 to 3
- members: int32 [2, 4, 16, 45], P('gx', 'gy', 'gz'), may hold values from -1 to 44, as said below
- delta_table: float32 [4, 1024], replicated, may hold values from -4 to 4
Outputs:
- site_tau: float32 [1, 2, 4, 16, 1024], P(None, 'gx', 'gy', 'gz')
- pair_terms: float32 [2, 4, 16, 45], P('gx', 'gy', 'gz')
The draws below stay inside these ranges and needn't reach their ends.
Inputs may be any that keep to these rules, and one draw needn't show every extreme that they name: `members`: each site's list names distinct window cells, the centre cell first, 27 to 45 of them, then -1 in the remaining slots; in every draw some site lists all 45 cells.
All inputs are finite; a program needn't handle non-finite values.
Results may differ from the reference program's by a relative error of at most 0.00013.
Values sent between devices are 32-bit elements; how exact they have to be, the bound alone decides.
No kernel may reach another device: no remote copies, remote signals or barrier semaphores. Data moves between devices by JAX's collectives and lax.ppermute only.
A program may use at most 192 MiB of HBM per device.

```python
import jax
import jax.numpy as jnp
from jax import lax

L2 = 32
WINDOW = 45
ITERS = 4
ENERGIES = 1
SPECIES = 4
NX = 2
NY = 4
NZ = 16


def draw_members(key, part):
    window_cells = jnp.arange(WINDOW, dtype=jnp.int32)
    score_key = jax.random.fold_in(key, 11)
    count_key = jax.random.fold_in(key, 23)
    scores = jax.random.randint(score_key, (NX, NY, NZ, WINDOW), 0, 1 << 20, dtype=jnp.int32)
    scores = scores * 64 + window_cells
    scores = jnp.where(window_cells == WINDOW // 2, -1, scores)
    ordered = jnp.argsort(scores, axis=-1, stable=True).astype(jnp.int32)
    counts = jax.random.randint(count_key, (NX * NY * NZ,), 27, WINDOW + 1, dtype=jnp.int32)
    counts = counts.at[0].set(WINDOW).reshape(NX, NY, NZ, 1)
    return jnp.where(window_cells < counts, ordered, -1).astype(jnp.int32)


def with_ends(drawn, key, least, largest):
    spot = [jax.random.randint(jax.random.fold_in(key, axis), (), 0, length) for axis, length in enumerate(drawn.shape)]
    widest = drawn.shape.index(max(drawn.shape))
    neighbour = spot[:widest] + [(spot[widest] + 1) % drawn.shape[widest]] + spot[widest + 1:]
    return drawn.at[tuple(spot)].set(least).at[tuple(neighbour)].set(largest)


def shard_levels(key, dims, cuts, least, top_value):
    level, own = 1.0, jax.random.fold_in(key, 6)
    for position, parts in cuts:
        draws = jnp.exp(jax.random.uniform(jax.random.fold_in(own, position), (parts,), jnp.float32, least / len(cuts), top_value / len(cuts)))
        level = level * jnp.repeat(draws, dims[position] // parts).reshape([-1 if axis == position else 1 for axis in range(len(dims))])
    return level


def bell_draw(own_key, dims, spread, limit, cuts=(), kind=jnp.bfloat16):
    entries = jax.random.normal(own_key, dims, jnp.float32) * spread
    if len(cuts) > 0:
        entries = shard_levels(own_key, dims, cuts, -0.22, 0.18) * entries
    return jnp.clip(entries, min=-limit, max=limit).astype(kind)


def setup_inputs(seed: int = 0) -> dict:
    key_of = jax.random.split(jax.random.key(seed), 6)
    return {
        "t_matrix": bell_draw(key_of[0], (ENERGIES, NX, NY, NZ, L2 * L2), 0.5, 3.0, ((1, 2), (2, 4), (3, 4)), jnp.float32),
        "structure": bell_draw(key_of[1], (ENERGIES, WINDOW * L2, WINDOW * L2), (16 * WINDOW * L2) ** -0.5, 0.0390625, (), jnp.float32),
        "species": with_ends(jax.random.randint(key_of[2], (NX, NY, NZ), 0, SPECIES), jax.random.fold_in(key_of[2], 1), 0, SPECIES - 1).astype(jnp.int32),
        "members": draw_members(jax.random.fold_in(key_of[5], 71), 0),
        "delta_table": bell_draw(key_of[4], (SPECIES, L2 * L2), 0.6, 4.0, (), jnp.float32),
    }


highest = lax.Precision.HIGHEST


def cell_offset(cell_index):
    return cell_index // 15 - 1, (cell_index // 5) % 3 - 1, cell_index % 5 - 2


def reference(t_matrix, structure, species, members, delta_table):
    site_count = NX * NY * NZ
    centre = WINDOW // 2
    window_cells = jnp.arange(WINDOW, dtype=jnp.int32)
    member = jnp.any(members[..., None] == window_cells, axis=-2).astype(jnp.float32)
    member = member.reshape(site_count, WINDOW).T
    onehot = (species.reshape(site_count, 1) == jnp.arange(SPECIES, dtype=jnp.int32)).astype(jnp.float32)
    delta_site = jnp.dot(onehot, delta_table, precision=highest, preferred_element_type=jnp.float32)
    delta_site = delta_site.reshape(site_count, L2, L2)
    tau_list = []
    pair_sums = jnp.zeros((WINDOW, site_count), jnp.float32)
    for energy in range(ENERGIES):
        site_matrices = t_matrix[energy].reshape(NX, NY, NZ, L2, L2)
        shifted = []
        for cell_index in range(WINDOW):
            shift_x, shift_y, shift_z = cell_offset(cell_index)
            rolled = jnp.roll(site_matrices, (-shift_x, -shift_y, -shift_z), axis=(0, 1, 2))
            shifted.append(rolled.reshape(site_count, L2, L2))
        window_matrices = jnp.stack(shifted)
        own_rows = jnp.transpose(site_matrices.reshape(site_count, L2, L2), (1, 0, 2))
        start_column = jnp.zeros((WINDOW, L2, site_count, L2), jnp.float32).at[centre].set(own_rows)
        column = start_column
        for sweep_index in range(ITERS):
            image_rows = jnp.dot(structure[energy], column.reshape(WINDOW * L2, site_count * L2),
                                 precision=highest, preferred_element_type=jnp.float32)
            image_rows = image_rows.reshape(WINDOW, L2, site_count, L2)
            moved_rows = jnp.einsum('psab,pbsc->pasc', window_matrices, image_rows, precision=highest)
            column = start_column + member[:, None, :, None] * moved_rows
        tau_list.append(jnp.transpose(column[centre], (1, 0, 2)).reshape(NX, NY, NZ, L2 * L2))
        right_blocks = jnp.einsum('carb,rbd->crad', column, delta_site, precision=highest)
        right_grid = right_blocks.reshape(WINDOW, NX, NY, NZ, L2, L2)
        terms = []
        for cell_index in range(WINDOW):
            shift_x, shift_y, shift_z = cell_offset(cell_index)
            incoming = jnp.roll(right_grid[WINDOW - 1 - cell_index], (-shift_x, -shift_y, -shift_z), axis=(0, 1, 2))
            incoming = incoming.reshape(site_count, L2, L2)
            left_blocks = jnp.einsum('sab,sbd->sad', delta_site, incoming, precision=highest)
            terms.append(jnp.einsum('sad,dsa->s', left_blocks, column[cell_index], precision=highest))
        pair_sums = pair_sums + jnp.stack(terms)
    site_tau = jnp.stack(tau_list)
    pair_terms = pair_sums.T.reshape(NX, NY, NZ, WINDOW)
    return site_tau, pair_terms
```

```python
import functools

import jax
import jax.numpy as jnp
import numpy as np
from jax import lax
from jax.experimental import pallas as pl
from jax.experimental.pallas import tpu as pltpu
from jax.sharding import PartitionSpec as P

L2 = 32
WINDOW = 45
ITERS = 4
SPECIES = 4
DEPTH = 4
LANES = DEPTH * L2
ROWS = WINDOW * L2
CENTRE = WINDOW // 2
GROUP = 9
CHUNK = GROUP * L2
CHUNKS = WINDOW // GROUP
MESH_AXES = ("gx", "gy", "gz")

bf16 = jnp.bfloat16
f32 = jnp.float32
highest = lax.Precision.HIGHEST
MIB = 1 << 20


def shifted(x, shift):
    sizes = [lax.axis_size(axis) for axis in MESH_AXES]
    pairs = []
    for source in np.ndindex(*sizes):
        target = [(i + d) % n for i, d, n in zip(source, shift, sizes)]
        pairs.append(
            (int(np.ravel_multi_index(source, sizes)), int(np.ravel_multi_index(target, sizes)))
        )
    return lax.ppermute(x, MESH_AXES, pairs)


def in_vmem(count):
    return [pl.BlockSpec(memory_space=pltpu.VMEM)] * count


def halves(x):
    high = x.astype(bf16)
    return high, (x - high.astype(f32)).astype(bf16)


def lane_index(shape):
    return lax.broadcasted_iota(jnp.int32, shape, len(shape) - 1)


def tile_kernel(flat_ref, tile_ref):
    row = lax.broadcasted_iota(jnp.int32, (DEPTH, LANES), 0)
    diagonal = lane_index((DEPTH, LANES)) // L2 == row
    for j in range(L2 // DEPTH):
        part = flat_ref[:, j * LANES : (j + 1) * LANES]
        rolled = [part] + [pltpu.roll(part, m * L2, 1) for m in range(1, DEPTH)]
        for k in range(DEPTH):
            picked = jnp.zeros((DEPTH, LANES), f32)
            for m in range(DEPTH):
                picked = jnp.where(diagonal & (row == (m + k) % DEPTH), rolled[m], picked)
            a = j * DEPTH + k
            tile_ref[a : a + 1, :] = jnp.sum(picked, axis=0, keepdims=True)


def own_tile(flat):
    return pl.pallas_call(
        tile_kernel,
        out_shape=jax.ShapeDtypeStruct((L2, LANES), f32),
        in_specs=in_vmem(1),
        out_specs=in_vmem(1)[0],
        compiler_params=pltpu.CompilerParams(vmem_limit_bytes=4 * MIB),
        name="own_tile",
    )(flat)


def split_kernel(structure_ref, own_ref, high_ref, low_ref, image_ref, buffer, sems):
    def fetch(step):
        return pltpu.make_async_copy(
            structure_ref.at[pl.ds(step * CHUNK, CHUNK), :],
            buffer.at[step % 2],
            sems.at[step % 2],
        )

    fetch(0).start()
    own_high, own_low = halves(own_ref[...])
    for step in range(CHUNKS):
        if step + 1 < CHUNKS:
            fetch(step + 1).start()
        fetch(step).wait()
        rows = pl.ds(step * CHUNK, CHUNK)
        for q in range(GROUP):
            part = pl.ds(q * L2, L2)
            high, low = halves(buffer[step % 2, part, :])
            high_ref[pl.ds(step * CHUNK + q * L2, L2), :] = high
            low_ref[pl.ds(step * CHUNK + q * L2, L2), :] = low
        columns = pl.ds(CENTRE * L2, L2)
        centre_high, centre_low = halves(buffer[step % 2, :, columns])
        image_ref[rows, :] = (
            jnp.dot(centre_high, own_high, preferred_element_type=f32)
            + jnp.dot(centre_high, own_low, preferred_element_type=f32)
            + jnp.dot(centre_low, own_high, preferred_element_type=f32)
        )


def split_structure(structure, own):
    return pl.pallas_call(
        split_kernel,
        out_shape=(
            jax.ShapeDtypeStruct((ROWS, ROWS), bf16),
            jax.ShapeDtypeStruct((ROWS, ROWS), bf16),
            jax.ShapeDtypeStruct((ROWS, LANES), f32),
        ),
        in_specs=[pl.BlockSpec(memory_space=pl.ANY)] + in_vmem(1),
        out_specs=tuple(in_vmem(3)),
        scratch_shapes=[pltpu.VMEM((2, CHUNK, ROWS), f32), pltpu.SemaphoreType.DMA((2,))],
        compiler_params=pltpu.CompilerParams(vmem_limit_bytes=24 * MIB),
        cost_estimate=pl.CostEstimate(
            flops=2 * 3 * ROWS * L2 * LANES, bytes_accessed=4 * ROWS * ROWS, transcendentals=0
        ),
        name="split_structure",
    )(structure, own)


def window_tile(near_ref, cell):
    dx, dy, dz = cell // 15, cell // 5 % 3, cell % 5 - 2
    dx = dx % near_ref.shape[1]
    own = near_ref[dy, dx, 0]
    if dz == 0:
        return own
    lane = lane_index((L2, LANES))
    if dz > 0:
        joined = jnp.where(lane < dz * L2, near_ref[dy, dx, 2], own)
        return pltpu.roll(joined, LANES - dz * L2, 1)
    joined = jnp.where(lane >= LANES + dz * L2, near_ref[dy, dx, 1], own)
    return pltpu.roll(joined, -dz * L2, 1)


def sweep_kernel(
    groups, high_ref, low_ref, image_ref, near_ref, member_ref, own_ref, delta_ref, *rest
):
    sent = rest[: len(groups)]
    tau_ref, window, column = rest[len(groups) :]
    lane = lane_index((L2, LANES))
    masks = [(lane // L2 == s).astype(f32).astype(bf16) for s in range(DEPTH)]

    def apply(cell, image):
        high, low = halves(image)
        high_blocks = jnp.concatenate([high * mask for mask in masks], axis=0)
        low_blocks = jnp.concatenate([low * mask for mask in masks], axis=0)
        both = jnp.concatenate([high_blocks, low_blocks], axis=1)
        rows = pl.ds(cell * L2, L2)
        first = jnp.dot(window[rows, :LANES], both, preferred_element_type=f32)
        second = jnp.dot(window[rows, LANES:], high_blocks, preferred_element_type=f32)
        return first[:, :LANES] + first[:, LANES:] + second

    def keep(slot, cell, value):
        high, low = halves(value)
        rows = pl.ds(cell * L2, L2)
        column[slot, rows, :LANES] = high
        column[slot, rows, LANES:] = low

    for cell in range(WINDOW):
        value = window_tile(near_ref, cell) * member_ref[cell : cell + 1, :]
        high, low = halves(value)
        window[cell * L2 : (cell + 1) * L2, :LANES] = high
        window[cell * L2 : (cell + 1) * L2, LANES:] = low
    for cell in range(WINDOW):
        value = apply(cell, image_ref[cell * L2 : (cell + 1) * L2, :])
        if cell == CENTRE:
            value = value + own_ref[...]
        keep(0, cell, value)

    for sweep in range(1, ITERS):
        now, later = (sweep - 1) % 2, sweep % 2

        def chunk_step(chunk, carry, now=now, later=later, last=sweep == ITERS - 1):
            rows = pl.ds(pl.multiple_of(chunk * CHUNK, CHUNK), CHUNK)
            first = jnp.dot(high_ref[rows, :], column[now], preferred_element_type=f32)
            second = jnp.dot(low_ref[rows, :], column[now, :, :LANES], preferred_element_type=f32)
            image = first[:, :LANES] + first[:, LANES:] + second
            for q in range(GROUP):
                cell = chunk * GROUP + q
                value = apply(cell, image[q * L2 : (q + 1) * L2])
                if q == CENTRE % GROUP:
                    value = value + jnp.where(chunk == CENTRE // GROUP, own_ref[...], 0.0)
                    if last:
                        @pl.when(chunk == CENTRE // GROUP)
                        def _():
                            tau_ref[...] = value
                keep(later, cell, value)
            return carry

        lax.fori_loop(0, CHUNKS, chunk_step, 0)

    final = (ITERS - 1) % 2
    high, low = halves(delta_ref[...])
    delta = jnp.concatenate(
        [
            jnp.concatenate([high, low], axis=1),
            jnp.concatenate([high, jnp.zeros_like(high)], axis=1),
        ],
        axis=0,
    )
    for group, ref in zip(groups, sent):
        for place, (ox, oy) in enumerate(group):
            base = ((ox + 1) * 3 + oy + 1) * 5 * L2
            rows = slice(base, base + 5 * L2)
            product = jnp.dot(column[final, rows, :], delta, preferred_element_type=f32)
            value = product[:, :LANES] + product[:, LANES:]
            ref[place * 5 : place * 5 + 5] = value.reshape(5, L2, LANES)


def sweeps(groups, high, low, image, near, member, own, delta):
    out_shape = [jax.ShapeDtypeStruct((5 * len(group), L2, LANES), f32) for group in groups]
    out_shape.append(jax.ShapeDtypeStruct((L2, LANES), f32))
    flops = 2 * 3 * (ITERS - 1) * ROWS * ROWS * LANES
    return pl.pallas_call(
        functools.partial(sweep_kernel, groups),
        out_shape=tuple(out_shape),
        in_specs=in_vmem(7),
        out_specs=tuple(in_vmem(len(out_shape))),
        scratch_shapes=[
            pltpu.VMEM((ROWS, 2 * LANES), bf16),
            pltpu.VMEM((2, ROWS, 2 * LANES), bf16),
        ],
        compiler_params=pltpu.CompilerParams(vmem_limit_bytes=32 * MIB),
        cost_estimate=pl.CostEstimate(flops=flops, bytes_accessed=10 * MIB, transcendentals=0),
        name="sweeps",
    )(high, low, image, near, member, own, delta)


def find_tile(groups, refs, ox, oy, oz):
    for group, ref in zip(groups, refs):
        if (ox, oy) in group:
            return ref[group.index((ox, oy)) * 5 + oz + 2]
    raise ValueError("no tile")


def turn_kernel(groups, *refs):
    own, out = refs[:-1], refs[-1]
    lane = lane_index((L2, LANES))

    def cell_tile(cell):
        cell = min(cell, WINDOW - 1)
        return find_tile(groups, own, cell // 15 - 1, cell // 5 % 3 - 1, cell % 5 - 2)

    for base in range(0, WINDOW, DEPTH):
        block = jnp.concatenate([cell_tile(base + k) for k in range(DEPTH)], axis=0)
        turned = block.T
        pieces = [turned[s * L2 : (s + 1) * L2] for s in range(DEPTH)]
        for k in range(min(DEPTH, WINDOW - base)):
            value = pieces[0] if k == 0 else pltpu.roll(pieces[0], (-k % DEPTH) * L2, 1)
            for s in range(1, DEPTH):
                move = (s - k) % DEPTH
                piece = pieces[s] if move == 0 else pltpu.roll(pieces[s], move * L2, 1)
                value = jnp.where(lane // L2 == s, piece, value)
            out[base + k] = value


def turned_tiles(groups, own):
    return pl.pallas_call(
        functools.partial(turn_kernel, groups),
        out_shape=jax.ShapeDtypeStruct((WINDOW, L2, LANES), f32),
        in_specs=in_vmem(len(own)),
        out_specs=in_vmem(1)[0],
        compiler_params=pltpu.CompilerParams(vmem_limit_bytes=8 * MIB),
        cost_estimate=pl.CostEstimate(flops=MIB, bytes_accessed=2 * MIB, transcendentals=0),
        name="turned_tiles",
    )(*own)


def plane_offsets():
    return [(ox, oy) for ox in (-1, 0, 1) for oy in (-1, 0, 1)]


def pack_kernel(groups, *refs):
    got = refs[:-2]
    down_ref, up_ref = refs[-2:]
    lane = lane_index((L2, LANES))
    for place, (ox, oy) in enumerate(plane_offsets()):
        far = pltpu.roll(find_tile(groups, got, ox, oy, -2), 2 * L2, 1)
        down_ref[place] = jnp.where(lane >= 2 * L2, far, find_tile(groups, got, ox, oy, -1))
        far = pltpu.roll(find_tile(groups, got, ox, oy, 2), 2 * L2, 1)
        up_ref[place] = jnp.where(lane < 2 * L2, far, find_tile(groups, got, ox, oy, 1))


def packed_edges(groups, got):
    shape = jax.ShapeDtypeStruct((9, L2, LANES), f32)
    return pl.pallas_call(
        functools.partial(pack_kernel, groups),
        out_shape=(shape, shape),
        in_specs=in_vmem(len(got)),
        out_specs=tuple(in_vmem(2)),
        compiler_params=pltpu.CompilerParams(vmem_limit_bytes=8 * MIB),
        name="packed_edges",
    )(*got)


def pair_kernel(groups, *refs):
    got = refs[: len(groups)]
    above_ref, below_ref, turned_ref, out_ref, sums = refs[len(groups) :]
    lane = lane_index((L2, LANES))
    for place, (ox, oy) in enumerate(plane_offsets()):
        above, below = above_ref[place], below_ref[place]
        for dz in range(-2, 3):
            tile = find_tile(groups, got, ox, oy, -dz)
            if dz == 1:
                tile = pltpu.roll(jnp.where(lane >= L2, tile, above), 3 * L2, 1)
            elif dz == 2:
                tile = jnp.where(lane < 2 * L2, pltpu.roll(tile, 2 * L2, 1), above)
            elif dz == -1:
                tile = pltpu.roll(jnp.where(lane < 3 * L2, tile, below), L2, 1)
            elif dz == -2:
                tile = jnp.where(lane >= 2 * L2, pltpu.roll(tile, 2 * L2, 1), below)
            cell = ((1 - ox) * 3 + 1 - oy) * 5 + dz + 2
            sums[cell : cell + 1, :] = jnp.sum(tile * turned_ref[cell], axis=0, keepdims=True)
    site = lax.broadcasted_iota(jnp.int32, (8, LANES), 0)
    pick = (lane_index((8, LANES)) // L2 == site).astype(f32)
    total = lax.dot_general(
        pick, sums[...], (((1,), (1,)), ((), ())), precision=highest, preferred_element_type=f32
    )
    out_ref[...] = total[:DEPTH, :WINDOW]


def pair_sums(groups, got, above, below, turned):
    return pl.pallas_call(
        functools.partial(pair_kernel, groups),
        out_shape=jax.ShapeDtypeStruct((DEPTH, WINDOW), f32),
        in_specs=in_vmem(len(got) + 3),
        out_specs=in_vmem(1)[0],
        scratch_shapes=[pltpu.VMEM((48, LANES), f32)],
        compiler_params=pltpu.CompilerParams(vmem_limit_bytes=8 * MIB),
        name="pair_sums",
    )(*got, above, below, turned)


def plane_groups():
    counts = (lax.axis_size("gx"), lax.axis_size("gy"))
    groups = {}
    for ox, oy in plane_offsets():
        groups.setdefault((ox % counts[0], oy % counts[1]), []).append((ox, oy))
    return groups


def near_tiles(own):
    column = jnp.stack([own, shifted(own, (0, 0, 1)), shifted(own, (0, 0, -1))])
    if lax.axis_size("gx") == 2:
        sides = [shifted(column, (1, 0, 0)), column]
    else:
        sides = [shifted(column, (1, 0, 0)), column, shifted(column, (-1, 0, 0))]
    plane = jnp.stack(sides)
    planes = [shifted(plane, (0, 1, 0)), plane, shifted(plane, (0, -1, 0))]
    return jnp.stack(planes)


def body(t_matrix, structure, species, members, delta_table):
    own = own_tile(t_matrix.reshape(DEPTH, L2 * L2))
    near = near_tiles(own)
    high, low, image = split_structure(structure[0], own)

    window_cells = jnp.arange(WINDOW, dtype=jnp.int32)
    member = jnp.any(members[0, 0][..., None] == window_cells, axis=-2).astype(f32).T
    member = jnp.repeat(member, L2, axis=1)
    onehot = (species.reshape(DEPTH, 1) == jnp.arange(SPECIES, dtype=jnp.int32)).astype(f32)
    delta = jnp.dot(onehot, delta_table, precision=highest, preferred_element_type=f32)
    delta = delta.reshape(DEPTH, L2, 1, L2) * jnp.eye(DEPTH, dtype=f32)[:, None, :, None]
    delta = delta.reshape(LANES, LANES)

    table = plane_groups()
    shifts, groups = list(table), list(table.values())
    *sent, tau = sweeps(groups, high, low, image, near, member, own, delta)
    got = [
        block if shift == (0, 0) else shifted(block, shift + (0,))
        for shift, block in zip(shifts, sent)
    ]
    turned = turned_tiles(groups, sent)
    down, up = packed_edges(groups, got)
    above = shifted(down, (0, 0, -1))
    below = shifted(up, (0, 0, 1))
    pairs = pair_sums(groups, got, above, below, turned)
    site_tau = jnp.transpose(tau.reshape(L2, DEPTH, L2), (1, 0, 2))
    return (
        site_tau.reshape(1, 1, 1, DEPTH, L2 * L2),
        pairs.reshape(1, 1, DEPTH, WINDOW),
    )


def solution(mesh):
    placed = (
        P(None, "gx", "gy", "gz", None),
        P(),
        P("gx", "gy", "gz"),
        P("gx", "gy", "gz", None),
        P(),
    )
    return jax.shard_map(
        body,
        mesh=mesh,
        in_specs=placed,
        out_specs=(P(None, "gx", "gy", "gz", None), P("gx", "gy", "gz", None)),
        check_vma=False,
    )
```

```python
import functools

import jax
import jax.numpy as jnp
import numpy as np
from jax import lax
from jax.experimental import pallas as pl
from jax.experimental.pallas import tpu as pltpu
from jax.sharding import PartitionSpec as P

L2 = 32
WINDOW = 45
ITERS = 4
SPECIES = 4
DEPTH = 4
LANES = DEPTH * L2
ROWS = WINDOW * L2
CENTRE = WINDOW // 2
GROUP = 9
CHUNK = GROUP * L2
CHUNKS = WINDOW // GROUP
MESH_AXES = ("gx", "gy", "gz")

bf16 = jnp.bfloat16
f32 = jnp.float32
highest = lax.Precision.HIGHEST
MIB = 1 << 20


def shifted(x, shift):
    sizes = [lax.axis_size(axis) for axis in MESH_AXES]
    pairs = []
    for source in np.ndindex(*sizes):
        target = [(i + d) % n for i, d, n in zip(source, shift, sizes)]
        pairs.append(
            (int(np.ravel_multi_index(source, sizes)), int(np.ravel_multi_index(target, sizes)))
        )
    return lax.ppermute(x, MESH_AXES, pairs)


def in_vmem(count):
    return [pl.BlockSpec(memory_space=pltpu.VMEM)] * count


def in_hbm(x):
    return pltpu.with_memory_space_constraint(x, pltpu.HBM)


def halves(x):
    high = x.astype(bf16)
    return high, (x - high.astype(f32)).astype(bf16)


def lane_index(shape):
    return lax.broadcasted_iota(jnp.int32, shape, len(shape) - 1)


def tile_kernel(flat_ref, tile_ref):
    row = lax.broadcasted_iota(jnp.int32, (DEPTH, LANES), 0)
    diagonal = lane_index((DEPTH, LANES)) // L2 == row
    for j in range(L2 // DEPTH):
        part = flat_ref[:, j * LANES : (j + 1) * LANES]
        rolled = [part] + [pltpu.roll(part, m * L2, 1) for m in range(1, DEPTH)]
        for k in range(DEPTH):
            picked = jnp.zeros((DEPTH, LANES), f32)
            for m in range(DEPTH):
                picked = jnp.where(diagonal & (row == (m + k) % DEPTH), rolled[m], picked)
            a = j * DEPTH + k
            tile_ref[a : a + 1, :] = jnp.sum(picked, axis=0, keepdims=True)


def flat_kernel(tile_ref, flat_ref):
    row = lax.broadcasted_iota(jnp.int32, (DEPTH, LANES), 0)
    diagonal = lane_index((DEPTH, LANES)) // L2 == row
    for j in range(L2 // DEPTH):
        spread = []
        for k in range(DEPTH):
            a = j * DEPTH + k
            line = jnp.broadcast_to(tile_ref[a : a + 1, :], (DEPTH, LANES))
            spread.append(jnp.where(diagonal, line, 0.0))
        value = jnp.zeros((DEPTH, LANES), f32)
        for m in range(DEPTH):
            picked = jnp.zeros((DEPTH, LANES), f32)
            for k in range(DEPTH):
                picked = jnp.where(row == (k - m) % DEPTH, spread[k], picked)
            value = value + (picked if m == 0 else pltpu.roll(picked, m * L2, 1))
        flat_ref[:, j * LANES : (j + 1) * LANES] = value


def own_tile(flat):
    return pl.pallas_call(
        tile_kernel,
        out_shape=jax.ShapeDtypeStruct((L2, LANES), f32),
        in_specs=in_vmem(1),
        out_specs=in_vmem(1)[0],
        compiler_params=pltpu.CompilerParams(vmem_limit_bytes=4 * MIB),
        name="own_tile",
    )(flat)


def split_kernel(
    structure_hbm,
    own_ref,
    species_hbm,
    members_hbm,
    table_hbm,
    high_ref,
    low_ref,
    image_ref,
    member_ref,
    delta_ref,
    buffer,
    species_ref,
    members_ref,
    table_ref,
    table_tile,
    sems,
    small_sems,
):
    def fetch(step):
        return pltpu.make_async_copy(
            structure_hbm.at[pl.ds(step * CHUNK, CHUNK), :], buffer.at[step], sems.at[step]
        )

    small = [
        pltpu.make_async_copy(source, target, small_sems.at[i])
        for i, (source, target) in enumerate(
            [
                (species_hbm, species_ref),
                (members_hbm, members_ref),
                (table_hbm, table_ref),
            ]
        )
    ]
    for step in range(CHUNKS):
        fetch(step).start()
    for copy in small:
        copy.start()
    own_high, own_low = halves(own_ref[...])
    for copy in small:
        copy.wait()
    split_small(species_ref, members_ref, table_ref, table_tile, member_ref, delta_ref)

    for step in range(CHUNKS):
        fetch(step).wait()

        def cell_step(q, carry, step=step):
            source = pl.ds(pl.multiple_of(q * L2, L2), L2)
            rows = pl.ds(pl.multiple_of(step * CHUNK + q * L2, L2), L2)
            high, low = halves(buffer[step, source, :])
            high_ref[rows, :] = high
            low_ref[rows, :] = low
            columns = slice(CENTRE * L2, CENTRE * L2 + L2)
            image_ref[rows, :] = (
                jnp.dot(high[:, columns], own_high, preferred_element_type=f32)
                + jnp.dot(high[:, columns], own_low, preferred_element_type=f32)
                + jnp.dot(low[:, columns], own_high, preferred_element_type=f32)
            )
            return carry

        lax.fori_loop(0, GROUP, cell_step, 0, unroll=3)


def split_small(species_ref, members_ref, table_ref, table_tile, member_ref, delta_ref):
    tile_kernel(table_ref, table_tile)
    table = table_tile[...]
    moved = [table] + [pltpu.roll(table, m * L2, 1) for m in range(1, SPECIES)]
    group = lane_index((L2, LANES)) // L2
    delta = jnp.zeros((L2, LANES), f32)
    for s in range(DEPTH):
        for kind in range(SPECIES):
            here = (group == s) & (species_ref[0, s] == kind)
            delta = jnp.where(here, moved[(s - kind) % SPECIES], delta)
    delta_ref[...] = delta

    cells = lax.broadcasted_iota(jnp.int32, (WINDOW, WINDOW), 0)
    group = lane_index((WINDOW, LANES)) // L2
    member = jnp.zeros((WINDOW, LANES), f32)
    for s in range(DEPTH):
        found = (members_ref[s : s + 1, :] == cells).astype(f32)
        found = jnp.max(found, axis=1, keepdims=True)
        member = jnp.where(group == s, found, member)
    member_ref[...] = member


def split_structure(structure, own, species, members, table):
    specs = [pl.BlockSpec(memory_space=pltpu.HBM)] * 5
    specs[1] = in_vmem(1)[0]
    return pl.pallas_call(
        split_kernel,
        out_shape=(
            jax.ShapeDtypeStruct((ROWS, ROWS), bf16),
            jax.ShapeDtypeStruct((ROWS, ROWS), bf16),
            jax.ShapeDtypeStruct((ROWS, LANES), f32),
            jax.ShapeDtypeStruct((WINDOW, LANES), f32),
            jax.ShapeDtypeStruct((L2, LANES), f32),
        ),
        in_specs=specs,
        out_specs=tuple(in_vmem(5)),
        scratch_shapes=[
            pltpu.VMEM((CHUNKS, CHUNK, ROWS), f32),
            pltpu.SMEM((1, DEPTH), jnp.int32),
            pltpu.VMEM((DEPTH, WINDOW), jnp.int32),
            pltpu.VMEM((SPECIES, L2 * L2), f32),
            pltpu.VMEM((L2, LANES), f32),
            pltpu.SemaphoreType.DMA((CHUNKS,)),
            pltpu.SemaphoreType.DMA((3,)),
        ],
        compiler_params=pltpu.CompilerParams(vmem_limit_bytes=16 * MIB),
        cost_estimate=pl.CostEstimate(
            flops=2 * 3 * ROWS * L2 * LANES, bytes_accessed=4 * ROWS * ROWS, transcendentals=0
        ),
        name="split_structure",
    )(in_hbm(structure), own, in_hbm(species), in_hbm(members), in_hbm(table))


def window_tile(near_ref, cell):
    dx, dy, dz = cell // 15, cell // 5 % 3, cell % 5 - 2
    dx = dx % near_ref.shape[1]
    own = near_ref[dy, dx, 0]
    if dz == 0:
        return own
    lane = lane_index((L2, LANES))
    if dz > 0:
        joined = jnp.where(lane < dz * L2, near_ref[dy, dx, 2], own)
        return pltpu.roll(joined, LANES - dz * L2, 1)
    joined = jnp.where(lane >= LANES + dz * L2, near_ref[dy, dx, 1], own)
    return pltpu.roll(joined, -dz * L2, 1)


def sweep_kernel(
    groups, high_ref, low_ref, image_ref, near_ref, member_ref, own_ref, delta_ref, *rest
):
    sent = rest[: len(groups)]
    tau_ref, window, column = rest[len(groups) :]
    lane = lane_index((L2, LANES))
    masks = [(lane // L2 == s).astype(f32).astype(bf16) for s in range(DEPTH)]

    def site_blocks(tile):
        return jnp.concatenate([tile * mask for mask in masks], axis=0)

    def apply(cell, image):
        high_blocks, low_blocks = (site_blocks(part) for part in halves(image))
        both = jnp.concatenate([high_blocks, low_blocks], axis=1)
        rows = pl.ds(cell * L2, L2)
        first = jnp.dot(window[rows, :LANES], both, preferred_element_type=f32)
        second = jnp.dot(window[rows, LANES:], high_blocks, preferred_element_type=f32)
        return first[:, :LANES] + first[:, LANES:] + second

    def keep(slot, cell, value):
        high, low = halves(value)
        rows = pl.ds(cell * L2, L2)
        column[slot, rows, :LANES] = high
        column[slot, rows, LANES:] = low

    for cell in range(WINDOW):
        value = window_tile(near_ref, cell) * member_ref[cell : cell + 1, :]
        high, low = halves(value)
        window[cell * L2 : (cell + 1) * L2, :LANES] = high
        window[cell * L2 : (cell + 1) * L2, LANES:] = low
    for cell in range(WINDOW):
        value = apply(cell, image_ref[cell * L2 : (cell + 1) * L2, :])
        if cell == CENTRE:
            value = value + own_ref[...]
        keep(0, cell, value)

    for sweep in range(1, ITERS):
        now, later = (sweep - 1) % 2, sweep % 2

        def chunk_step(chunk, carry, now=now, later=later, last=sweep == ITERS - 1):
            rows = pl.ds(pl.multiple_of(chunk * CHUNK, CHUNK), CHUNK)
            first = jnp.dot(high_ref[rows, :], column[now], preferred_element_type=f32)
            second = jnp.dot(low_ref[rows, :], column[now, :, :LANES], preferred_element_type=f32)
            image = first[:, :LANES] + first[:, LANES:] + second
            for q in range(GROUP):
                cell = chunk * GROUP + q
                value = apply(cell, image[q * L2 : (q + 1) * L2])
                if q == CENTRE % GROUP:
                    value = value + jnp.where(chunk == CENTRE // GROUP, own_ref[...], 0.0)
                    if last:
                        @pl.when(chunk == CENTRE // GROUP)
                        def _():
                            tau_ref[...] = value
                keep(later, cell, value)
            return carry

        lax.fori_loop(0, CHUNKS, chunk_step, 0)

    final = (ITERS - 1) % 2
    high, low = (site_blocks(part) for part in halves(delta_ref[...]))
    delta = jnp.concatenate(
        [
            jnp.concatenate([high, low], axis=1),
            jnp.concatenate([high, jnp.zeros_like(high)], axis=1),
        ],
        axis=0,
    )
    for group, ref in zip(groups, sent):
        for place, (ox, oy) in enumerate(group):
            base = ((ox + 1) * 3 + oy + 1) * 5 * L2
            rows = slice(base, base + 5 * L2)
            product = jnp.dot(column[final, rows, :], delta, preferred_element_type=f32)
            value = product[:, :LANES] + product[:, LANES:]
            ref[place * 5 : place * 5 + 5] = value.reshape(5, L2, LANES)


def sweeps(groups, high, low, image, near, member, own, delta):
    out_shape = [jax.ShapeDtypeStruct((5 * len(group), L2, LANES), f32) for group in groups]
    out_shape.append(jax.ShapeDtypeStruct((L2, LANES), f32))
    flops = 2 * 3 * (ITERS - 1) * ROWS * ROWS * LANES
    return pl.pallas_call(
        functools.partial(sweep_kernel, groups),
        out_shape=tuple(out_shape),
        in_specs=in_vmem(7),
        out_specs=tuple(in_vmem(len(out_shape))),
        scratch_shapes=[
            pltpu.VMEM((ROWS, 2 * LANES), bf16),
            pltpu.VMEM((2, ROWS, 2 * LANES), bf16),
        ],
        compiler_params=pltpu.CompilerParams(vmem_limit_bytes=32 * MIB),
        cost_estimate=pl.CostEstimate(flops=flops, bytes_accessed=10 * MIB, transcendentals=0),
        name="sweeps",
    )(high, low, image, near, member, own, delta)


def find_tile(groups, refs, ox, oy, oz):
    for group, ref in zip(groups, refs):
        if (ox, oy) in group:
            return ref[group.index((ox, oy)) * 5 + oz + 2]
    raise ValueError("no tile")


def plane_offsets():
    return [(ox, oy) for ox in (-1, 0, 1) for oy in (-1, 0, 1)]


def cell_of(dx, dy, dz):
    return ((dx + 1) * 3 + dy + 1) * 5 + dz + 2


def turn_kernel(groups, *refs):
    own = refs[: len(groups)]
    out, up_ref, down_ref = refs[len(groups) :]
    lane = lane_index((L2, LANES))

    def cell_tile(cell):
        cell = min(cell, WINDOW - 1)
        return find_tile(groups, own, cell // 15 - 1, cell // 5 % 3 - 1, cell % 5 - 2)

    for base in range(0, WINDOW, DEPTH):
        block = jnp.concatenate([cell_tile(base + k) for k in range(DEPTH)], axis=0)
        turned = block.T
        pieces = [turned[s * L2 : (s + 1) * L2] for s in range(DEPTH)]
        for k in range(min(DEPTH, WINDOW - base)):
            value = pieces[0] if k == 0 else pltpu.roll(pieces[0], (-k % DEPTH) * L2, 1)
            for s in range(1, DEPTH):
                move = (s - k) % DEPTH
                piece = pieces[s] if move == 0 else pltpu.roll(pieces[s], move * L2, 1)
                value = jnp.where(lane // L2 == s, piece, value)
            out[base + k] = value
    for place, (dx, dy) in enumerate(plane_offsets()):
        far = pltpu.roll(out[cell_of(dx, dy, 2)], 2 * L2, 1)
        up_ref[place] = jnp.where(lane < 2 * L2, far, out[cell_of(dx, dy, 1)])
        far = pltpu.roll(out[cell_of(dx, dy, -2)], 2 * L2, 1)
        down_ref[place] = jnp.where(lane >= 2 * L2, far, out[cell_of(dx, dy, -1)])


def turned_tiles(groups, own):
    edge = jax.ShapeDtypeStruct((9, L2, LANES), f32)
    return pl.pallas_call(
        functools.partial(turn_kernel, groups),
        out_shape=(jax.ShapeDtypeStruct((WINDOW, L2, LANES), f32), edge, edge),
        in_specs=in_vmem(len(own)),
        out_specs=tuple(in_vmem(3)),
        compiler_params=pltpu.CompilerParams(vmem_limit_bytes=8 * MIB),
        cost_estimate=pl.CostEstimate(flops=MIB, bytes_accessed=2 * MIB, transcendentals=0),
        name="turned_tiles",
    )(*own)


def edge_kernel(groups, *refs):
    got = refs[: len(groups)]
    from_below, from_above, to_below, to_above = refs[len(groups) :]
    lane = lane_index((L2, LANES))
    for ref in (to_below, to_above):
        ref[...] = jnp.zeros_like(ref)
    for place, (dx, dy) in enumerate(plane_offsets()):
        far = find_tile(groups, got, -dx, -dy, -2)
        close = pltpu.roll(find_tile(groups, got, -dx, -dy, -1), 3 * L2, 1)
        value = jnp.where(lane < 2 * L2, far, close) * from_below[place]
        to_below[place : place + 1, :] = jnp.sum(value, axis=0, keepdims=True)
        far = find_tile(groups, got, -dx, -dy, 2)
        close = pltpu.roll(find_tile(groups, got, -dx, -dy, 1), L2, 1)
        value = jnp.where(lane >= 2 * L2, far, close) * from_above[place]
        to_above[place : place + 1, :] = jnp.sum(value, axis=0, keepdims=True)


def edge_sums(groups, got, from_below, from_above):
    shape = jax.ShapeDtypeStruct((16, LANES), f32)
    return pl.pallas_call(
        functools.partial(edge_kernel, groups),
        out_shape=(shape, shape),
        in_specs=in_vmem(len(got) + 2),
        out_specs=tuple(in_vmem(2)),
        compiler_params=pltpu.CompilerParams(vmem_limit_bytes=8 * MIB),
        name="edge_sums",
    )(*got, from_below, from_above)


def slab_kernel(groups, *refs):
    got = refs[: len(groups)]
    turned_ref, tau_ref, sums, flat_ref = refs[len(groups) :]
    flat_kernel(tau_ref, flat_ref)
    lane = lane_index((1, LANES))
    for dx, dy in plane_offsets():
        for dz in range(-2, 3):
            cell = cell_of(dx, dy, dz)
            tile = find_tile(groups, got, -dx, -dy, -dz)
            if dz != 0:
                tile = pltpu.roll(tile, -dz % DEPTH * L2, 1)
            row = jnp.sum(tile * turned_ref[cell], axis=0, keepdims=True)
            if dz > 0:
                row = jnp.where(lane < (DEPTH - dz) * L2, row, 0.0)
            elif dz < 0:
                row = jnp.where(lane >= -dz * L2, row, 0.0)
            sums[cell : cell + 1, :] = row


def slab_sums(groups, got, turned, tau):
    return pl.pallas_call(
        functools.partial(slab_kernel, groups),
        out_shape=(
            jax.ShapeDtypeStruct((WINDOW, LANES), f32),
            jax.ShapeDtypeStruct((DEPTH, L2 * L2), f32),
        ),
        in_specs=in_vmem(len(got) + 2),
        out_specs=tuple(in_vmem(2)),
        compiler_params=pltpu.CompilerParams(vmem_limit_bytes=8 * MIB),
        cost_estimate=pl.CostEstimate(flops=MIB, bytes_accessed=2 * MIB, transcendentals=0),
        name="slab_sums",
    )(*got, turned, tau)


def total_kernel(slab_ref, above_ref, below_ref, out_ref, sums):
    lane = lane_index((1, LANES))
    sums[...] = jnp.zeros_like(sums)
    sums[:WINDOW, :] = slab_ref[...]
    for place, (dx, dy) in enumerate(plane_offsets()):
        above = above_ref[place : place + 1, :]
        below = below_ref[place : place + 1, :]
        edges = {
            1: jnp.where(lane >= 3 * L2, above, 0.0),
            2: jnp.where(lane >= 2 * L2, pltpu.roll(above, 2 * L2, 1), 0.0),
            -1: jnp.where(lane < L2, below, 0.0),
            -2: jnp.where(lane < 2 * L2, pltpu.roll(below, 2 * L2, 1), 0.0),
        }
        for dz, row in edges.items():
            cell = cell_of(dx, dy, dz)
            sums[cell : cell + 1, :] = sums[cell : cell + 1, :] + row
    site = lax.broadcasted_iota(jnp.int32, (8, LANES), 0)
    pick = (lane_index((8, LANES)) // L2 == site).astype(f32)
    total = lax.dot_general(
        pick, sums[...], (((1,), (1,)), ((), ())), precision=highest, preferred_element_type=f32
    )
    out_ref[...] = total[:DEPTH, :WINDOW]


def total_sums(slab, above, below):
    return pl.pallas_call(
        total_kernel,
        out_shape=jax.ShapeDtypeStruct((DEPTH, WINDOW), f32),
        in_specs=in_vmem(3),
        out_specs=in_vmem(1)[0],
        scratch_shapes=[pltpu.VMEM((48, LANES), f32)],
        compiler_params=pltpu.CompilerParams(vmem_limit_bytes=4 * MIB),
        name="total_sums",
    )(slab, above, below)


def plane_groups():
    counts = (lax.axis_size("gx"), lax.axis_size("gy"))
    groups = {}
    for ox, oy in plane_offsets():
        groups.setdefault((ox % counts[0], oy % counts[1]), []).append((ox, oy))
    return groups


def near_tiles(own, ready):
    column = jnp.stack([own, shifted(own, (0, 0, 1)), shifted(own, (0, 0, -1))])
    column, *ready = lax.optimization_barrier((column, *ready))
    if lax.axis_size("gx") == 2:
        sides = [shifted(column, (1, 0, 0)), column]
    else:
        sides = [shifted(column, (1, 0, 0)), column, shifted(column, (-1, 0, 0))]
    plane = jnp.stack(sides)
    planes = [shifted(plane, (0, 1, 0)), plane, shifted(plane, (0, -1, 0))]
    return jnp.stack(planes), ready


def body(t_matrix, structure, species, members, delta_table):
    own = own_tile(t_matrix.reshape(DEPTH, L2 * L2))
    near, (high, low, image, member, delta) = near_tiles(
        own,
        split_structure(
            structure[0],
            own,
            species.reshape(1, DEPTH),
            members.reshape(DEPTH, WINDOW),
            delta_table,
        ),
    )
    table = plane_groups()
    shifts, groups = list(table), list(table.values())
    *sent, tau = sweeps(groups, high, low, image, near, member, own, delta)
    got = [
        block if shift == (0, 0) else shifted(block, shift + (0,))
        for shift, block in zip(shifts, sent)
    ]
    turned, up, down = turned_tiles(groups, sent)
    from_below = shifted(up, (0, 0, 1))
    from_above = shifted(down, (0, 0, -1))
    to_below, to_above = edge_sums(groups, got, from_below, from_above)
    above = shifted(to_below, (0, 0, -1))
    below = shifted(to_above, (0, 0, 1))
    slab, site_tau = slab_sums(groups, got, turned, tau)
    pairs = total_sums(slab, above, below)
    return (
        site_tau.reshape(1, 1, 1, DEPTH, L2 * L2),
        pairs.reshape(1, 1, DEPTH, WINDOW),
    )


def solution(mesh):
    placed = (
        P(None, "gx", "gy", "gz", None),
        P(),
        P("gx", "gy", "gz"),
        P("gx", "gy", "gz", None),
        P(),
    )
    return jax.shard_map(
        body,
        mesh=mesh,
        in_specs=placed,
        out_specs=(P(None, "gx", "gy", "gz", None), P("gx", "gy", "gz", None)),
        check_vma=False,
    )
```

```python
import functools

import jax
import jax.numpy as jnp
import numpy as np
from jax import lax
from jax.experimental import pallas as pl
from jax.experimental.pallas import tpu as pltpu
from jax.sharding import PartitionSpec as P

L2 = 32
WINDOW = 45
ITERS = 4
SPECIES = 4
DEPTH = 4
LANES = DEPTH * L2
ROWS = WINDOW * L2
CENTRE = WINDOW // 2
SUM_ROWS = 48
PIECES = 3
PIECE = WINDOW // PIECES
PIECE_ROWS = PIECE * L2
SPLIT_STEPS = 3
CHUNK = 15
MESH_AXES = ("gx", "gy", "gz")

bf16 = jnp.bfloat16
f32 = jnp.float32
highest = lax.Precision.HIGHEST
MIB = 1 << 20


def shifted(x, shift):
    sizes = [lax.axis_size(axis) for axis in MESH_AXES]
    pairs = []
    for source in np.ndindex(*sizes):
        target = [(i + d) % n for i, d, n in zip(source, shift, sizes)]
        pairs.append(
            (int(np.ravel_multi_index(source, sizes)), int(np.ravel_multi_index(target, sizes)))
        )
    return lax.ppermute(x, MESH_AXES, pairs)


def in_vmem(count):
    return [pl.BlockSpec(memory_space=pltpu.VMEM)] * count


def in_hbm(x):
    return pltpu.with_memory_space_constraint(x, pltpu.HBM)


def halves(x):
    high = x.astype(bf16)
    return high, (x - high.astype(f32)).astype(bf16)


def lane_index(shape):
    return lax.broadcasted_iota(jnp.int32, shape, len(shape) - 1)


def tile_kernel(flat_ref, tile_ref):
    row = lax.broadcasted_iota(jnp.int32, (DEPTH, LANES), 0)
    diagonal = lane_index((DEPTH, LANES)) // L2 == row
    for j in range(L2 // DEPTH):
        part = flat_ref[:, j * LANES : (j + 1) * LANES]
        rolled = [part] + [pltpu.roll(part, m * L2, 1) for m in range(1, DEPTH)]
        for k in range(DEPTH):
            picked = jnp.zeros((DEPTH, LANES), f32)
            for m in range(DEPTH):
                picked = jnp.where(diagonal & (row == (m + k) % DEPTH), rolled[m], picked)
            a = j * DEPTH + k
            tile_ref[a : a + 1, :] = jnp.sum(picked, axis=0, keepdims=True)


def flat_kernel(tile_ref, flat_ref):
    row = lax.broadcasted_iota(jnp.int32, (DEPTH, LANES), 0)
    diagonal = lane_index((DEPTH, LANES)) // L2 == row
    for j in range(L2 // DEPTH):
        spread = []
        for k in range(DEPTH):
            a = j * DEPTH + k
            line = jnp.broadcast_to(tile_ref[a : a + 1, :], (DEPTH, LANES))
            spread.append(jnp.where(diagonal, line, 0.0))
        value = jnp.zeros((DEPTH, LANES), f32)
        for m in range(DEPTH):
            picked = jnp.zeros((DEPTH, LANES), f32)
            for k in range(DEPTH):
                picked = jnp.where(row == (k - m) % DEPTH, spread[k], picked)
            value = value + (picked if m == 0 else pltpu.roll(picked, m * L2, 1))
        flat_ref[:, j * LANES : (j + 1) * LANES] = value


def own_tile(flat):
    return pl.pallas_call(
        tile_kernel,
        out_shape=jax.ShapeDtypeStruct((L2, LANES), f32),
        in_specs=in_vmem(1),
        out_specs=in_vmem(1)[0],
        compiler_params=pltpu.CompilerParams(vmem_limit_bytes=4 * MIB),
        name="own_tile",
    )(flat)


def split_kernel(piece, structure_hbm, own_ref, *refs):
    parts_ref, image_ref, buffer, sems = refs
    step_rows = PIECE_ROWS // SPLIT_STEPS

    def fetch(step):
        rows = pl.ds(piece * PIECE_ROWS + step * step_rows, step_rows)
        return pltpu.make_async_copy(structure_hbm.at[rows, :], buffer.at[step], sems.at[step])

    for step in range(SPLIT_STEPS):
        fetch(step).start()
    lane_tile = CENTRE * L2 // LANES * LANES
    before = CENTRE * L2 - lane_tile
    own_parts = jnp.concatenate(halves(own_ref[...]), axis=1)
    own_parts = jnp.concatenate(
        [
            jnp.zeros((before, 2 * LANES), bf16),
            own_parts,
            jnp.zeros((LANES - before - L2, 2 * LANES), bf16),
        ],
        axis=0,
    )
    half = L2 // 2
    for step in range(SPLIT_STEPS):
        fetch(step).wait()

        def half_cell(i, carry, step=step):
            source = pl.ds(pl.multiple_of(i * half, half), half)
            target = step * 2 * step_rows + i // 2 * 2 * L2 + i % 2 * half
            high, low = halves(buffer[step, source, :])
            parts_ref[pl.ds(pl.multiple_of(target, half), half), :] = high
            parts_ref[pl.ds(pl.multiple_of(target + L2, half), half), :] = low
            return carry

        lax.fori_loop(0, step_rows // half, half_cell, 0, unroll=2)
    product = jnp.dot(
        parts_ref[:, lane_tile : lane_tile + LANES], own_parts, preferred_element_type=f32
    )
    image_ref[...] = four_products(product)


def split_piece(piece, structure, own):
    return pl.pallas_call(
        functools.partial(split_kernel, piece),
        out_shape=(
            jax.ShapeDtypeStruct((2 * PIECE_ROWS, ROWS), bf16),
            jax.ShapeDtypeStruct((PIECE, L2, LANES), f32),
        ),
        in_specs=[pl.BlockSpec(memory_space=pltpu.HBM)] + in_vmem(1),
        out_specs=tuple(in_vmem(2)),
        scratch_shapes=[
            pltpu.VMEM((SPLIT_STEPS, PIECE_ROWS // SPLIT_STEPS, ROWS), f32),
            pltpu.SemaphoreType.DMA((SPLIT_STEPS,)),
        ],
        compiler_params=pltpu.CompilerParams(vmem_limit_bytes=8 * MIB),
        cost_estimate=pl.CostEstimate(
            flops=MIB, bytes_accessed=4 * PIECE_ROWS * ROWS, transcendentals=0
        ),
        name="split_piece",
    )(in_hbm(structure), own)


def setup_kernel(
    species_hbm,
    members_hbm,
    table_hbm,
    member_ref,
    delta_ref,
    species_ref,
    members_ref,
    table_ref,
    table_tile,
    sems,
):
    moves = [(species_hbm, species_ref), (members_hbm, members_ref), (table_hbm, table_ref)]
    copies = [
        pltpu.make_async_copy(source, target, sems.at[i])
        for i, (source, target) in enumerate(moves)
    ]
    for copy in copies:
        copy.start()
    for copy in copies:
        copy.wait()
    tile_kernel(table_ref, table_tile)
    table = table_tile[...]
    moved = [table] + [pltpu.roll(table, m * L2, 1) for m in range(1, SPECIES)]
    group = lane_index((L2, LANES)) // L2
    delta = jnp.zeros((L2, LANES), f32)
    for s in range(DEPTH):
        for kind in range(SPECIES):
            here = (group == s) & (species_ref[0, s] == kind)
            delta = jnp.where(here, moved[(s - kind) % SPECIES], delta)
    delta_ref[...] = delta

    cells = lax.broadcasted_iota(jnp.int32, (WINDOW, WINDOW), 0)
    group = lane_index((WINDOW, LANES)) // L2
    member = jnp.zeros((WINDOW, LANES), f32)
    for s in range(DEPTH):
        found = (members_ref[s : s + 1, :] == cells).astype(f32)
        found = jnp.max(found, axis=1, keepdims=True)
        member = jnp.where(group == s, found, member)
    member_ref[...] = member


def setup(species, members, table):
    return pl.pallas_call(
        setup_kernel,
        out_shape=(
            jax.ShapeDtypeStruct((WINDOW, LANES), f32),
            jax.ShapeDtypeStruct((L2, LANES), f32),
        ),
        in_specs=[pl.BlockSpec(memory_space=pltpu.HBM)] * 3,
        out_specs=tuple(in_vmem(2)),
        scratch_shapes=[
            pltpu.SMEM((1, DEPTH), jnp.int32),
            pltpu.VMEM((DEPTH, WINDOW), jnp.int32),
            pltpu.VMEM((SPECIES, L2 * L2), f32),
            pltpu.VMEM((L2, LANES), f32),
            pltpu.SemaphoreType.DMA((3,)),
        ],
        compiler_params=pltpu.CompilerParams(vmem_limit_bytes=2 * MIB),
        name="setup",
    )(in_hbm(species), in_hbm(members), in_hbm(table))


def four_products(product):
    parts = product.reshape(-1, 2, L2, 2 * LANES)
    high, low = parts[:, 0], parts[:, 1]
    return (high[..., :LANES] + high[..., LANES:]) + (low[..., :LANES] + low[..., LANES:])


def site_blocks(tile):
    lane = lane_index((L2, LANES))
    masks = [(lane // L2 == s).astype(f32).astype(bf16) for s in range(DEPTH)]
    return jnp.concatenate([tile * mask for mask in masks], axis=0)


def moved(window, cell, image):
    blocks = jnp.concatenate([site_blocks(part) for part in halves(image)], axis=1)
    product = jnp.dot(window[cell * 2 * L2 : (cell + 1) * 2 * L2, :], blocks, preferred_element_type=f32)
    return four_products(product)[0]


def keep(column, place, value):
    high, low = halves(value)
    rows = slice(place * L2, (place + 1) * L2)
    column[rows, :LANES] = high
    column[rows, LANES:] = low


def images(parts, cells, column):
    rows = []
    for cell in cells:
        base = cell % PIECE * 2 * L2
        if rows and rows[-1][0] == cell // PIECE and rows[-1][2] == base:
            rows[-1][2] = base + 2 * L2
        else:
            rows.append([cell // PIECE, base, base + 2 * L2])
    left = [parts[piece][low:high, :] for piece, low, high in rows]
    left = left[0] if len(left) == 1 else jnp.concatenate(left, axis=0)
    return four_products(jnp.dot(left, column[...], preferred_element_type=f32))


def window_tile(near_ref, cell):
    dx, dy, dz = cell // 15, cell // 5 % 3, cell % 5 - 2
    dx = dx % near_ref.shape[1]
    own = near_ref[dy, dx, 0]
    if dz == 0:
        return own
    lane = lane_index((L2, LANES))
    if dz > 0:
        joined = jnp.where(lane < dz * L2, near_ref[dy, dx, 2], own)
        return pltpu.roll(joined, LANES - dz * L2, 1)
    joined = jnp.where(lane >= LANES + dz * L2, near_ref[dy, dx, 1], own)
    return pltpu.roll(joined, -dz * L2, 1)


def sweep_over(parts, chunks, source, use_image, slots):
    for i, chunk in enumerate(chunks):
        slots[i % 2][: len(chunk)] = images(parts, chunk, source)
        if i > 0:
            use_image(i - 1, slots[(i - 1) % 2])
    use_image(len(chunks) - 1, slots[(len(chunks) - 1) % 2])


def last_sweep(parts, column, window, own_ref, delta_ref, stage, sent, tau_ref, slots, final):
    high, low = (site_blocks(part) for part in halves(delta_ref[...]))
    delta = jnp.concatenate(
        [
            jnp.concatenate([high, low], axis=1),
            jnp.concatenate([high, jnp.zeros_like(high)], axis=1),
        ],
        axis=0,
    )
    chunks = [[cell_of(ox, oy, oz) for ox, oy in group for oz in range(-2, 3)] for group in stage]

    def use_image(i, slot):
        for place, cell in enumerate(chunks[i]):
            value = moved(window, cell, slot[place])
            if cell == CENTRE:
                value = value + own_ref[...]
                tau_ref[...] = value
            keep(final, place, value)
        count = len(chunks[i])
        product = jnp.dot(final[: count * L2, :], delta, preferred_element_type=f32)
        value = product[:, :LANES] + product[:, LANES:]
        sent[i][...] = value.reshape(count, L2, LANES)

    sweep_over(parts, chunks, column, use_image, slots)


def first_kernel(stage, *refs):
    parts, firsts = refs[:PIECES], refs[PIECES : 2 * PIECES]
    near_ref, member_ref, own_ref, delta_ref = refs[2 * PIECES : 2 * PIECES + 4]
    outs = refs[2 * PIECES + 4 :]
    sent = outs[: len(stage)]
    column, window, other, slot_a, slot_b, final = outs[len(stage) :]
    slots = (slot_a, slot_b)
    for cell in range(WINDOW):
        high, low = halves(window_tile(near_ref, cell) * member_ref[cell : cell + 1, :])
        base = cell * 2 * L2
        window[base : base + L2, :] = high
        window[base + L2 : base + 2 * L2, :] = low

    def update(target, cell, image):
        value = moved(window, cell, image)
        if cell == CENTRE:
            value = value + own_ref[...]
        keep(target, cell, value)

    full = [list(range(base, base + CHUNK)) for base in range(0, WINDOW, CHUNK)]
    source, target = (column, other) if ITERS % 2 == 0 else (other, column)
    for cell in range(WINDOW):
        update(source, cell, firsts[cell // PIECE][cell % PIECE])
    for sweep in range(1, ITERS - 1):

        def use_image(i, slot, target=target):
            for place, cell in enumerate(full[i]):
                update(target, cell, slot[place])

        sweep_over(parts, full, source, use_image, slots)
        source, target = target, source
    last_sweep(parts, source, window, own_ref, delta_ref, stage, sent, None, slots, final)


def next_kernel(stage, *refs):
    parts = refs[:PIECES]
    column, window, own_ref, delta_ref = refs[PIECES : PIECES + 4]
    sent = refs[PIECES + 4 : PIECES + 4 + len(stage)]
    rest = refs[PIECES + 4 + len(stage) :]
    tau_ref = rest[0] if len(rest) == 4 else None
    slot_a, slot_b, final = rest[-3:]
    last_sweep(
        parts, column, window, own_ref, delta_ref, stage, sent, tau_ref, (slot_a, slot_b), final
    )


def stage_call(kernel, name, stage, extra_outs, extra_scratch, operands, flops):
    longest = max(CHUNK, 5 * max(len(group) for group in stage))
    out_shape = [jax.ShapeDtypeStruct((5 * len(group), L2, LANES), f32) for group in stage]
    out_shape += extra_outs
    return pl.pallas_call(
        functools.partial(kernel, stage),
        out_shape=tuple(out_shape),
        in_specs=in_vmem(len(operands)),
        out_specs=tuple(in_vmem(len(out_shape))),
        scratch_shapes=extra_scratch
        + [pltpu.VMEM((longest, L2, LANES), f32)] * 2
        + [pltpu.VMEM((longest * L2, 2 * LANES), bf16)],
        compiler_params=pltpu.CompilerParams(vmem_limit_bytes=16 * MIB),
        cost_estimate=pl.CostEstimate(flops=flops, bytes_accessed=MIB, transcendentals=0),
        name=name,
    )(*operands)


def first_stage(stage, parts, firsts, near, member, own, delta):
    return stage_call(
        first_kernel,
        "first_stage",
        stage,
        [
            jax.ShapeDtypeStruct((ROWS, 2 * LANES), bf16),
            jax.ShapeDtypeStruct((2 * ROWS, LANES), bf16),
        ],
        [pltpu.VMEM((ROWS, 2 * LANES), bf16)],
        (*parts, *firsts, near, member, own, delta),
        2 * 4 * (ITERS - 2) * ROWS * ROWS * LANES,
    )


def next_stage(stage, parts, column, window, own, delta):
    tau = [jax.ShapeDtypeStruct((L2, LANES), f32)]
    return stage_call(
        next_kernel,
        "next_stage",
        stage,
        tau if any((0, 0) in group for group in stage) else [],
        [],
        (*parts, column, window, own, delta),
        2 * ROWS * ROWS * LANES,
    )


def find_tile(groups, refs, ox, oy, oz):
    for group, ref in zip(groups, refs):
        if (ox, oy) in group:
            return ref[group.index((ox, oy)) * 5 + oz + 2]
    raise ValueError("no tile")


def plane_offsets():
    return [(ox, oy) for ox in (-1, 0, 1) for oy in (-1, 0, 1)]


def cell_of(dx, dy, dz):
    return ((dx + 1) * 3 + dy + 1) * 5 + dz + 2


def turn_kernel(groups, *refs):
    own = refs[: len(groups)]
    out, up_ref, down_ref = refs[len(groups) :]
    lane = lane_index((L2, LANES))

    def cell_tile(cell):
        cell = min(cell, WINDOW - 1)
        return find_tile(groups, own, cell // 15 - 1, cell // 5 % 3 - 1, cell % 5 - 2)

    for base in range(0, WINDOW, DEPTH):
        block = jnp.concatenate([cell_tile(base + k) for k in range(DEPTH)], axis=0)
        turned = block.T
        pieces = [turned[s * L2 : (s + 1) * L2] for s in range(DEPTH)]
        for k in range(min(DEPTH, WINDOW - base)):
            value = pieces[0] if k == 0 else pltpu.roll(pieces[0], (-k % DEPTH) * L2, 1)
            for s in range(1, DEPTH):
                move = (s - k) % DEPTH
                piece = pieces[s] if move == 0 else pltpu.roll(pieces[s], move * L2, 1)
                value = jnp.where(lane // L2 == s, piece, value)
            out[base + k] = value
    for place, (dx, dy) in enumerate(plane_offsets()):
        far = pltpu.roll(out[cell_of(dx, dy, 2)], 2 * L2, 1)
        up_ref[place] = jnp.where(lane < 2 * L2, far, out[cell_of(dx, dy, 1)])
        far = pltpu.roll(out[cell_of(dx, dy, -2)], 2 * L2, 1)
        down_ref[place] = jnp.where(lane >= 2 * L2, far, out[cell_of(dx, dy, -1)])


def turned_tiles(groups, own):
    edge = jax.ShapeDtypeStruct((9, L2, LANES), f32)
    return pl.pallas_call(
        functools.partial(turn_kernel, groups),
        out_shape=(jax.ShapeDtypeStruct((WINDOW, L2, LANES), f32), edge, edge),
        in_specs=in_vmem(len(own)),
        out_specs=tuple(in_vmem(3)),
        compiler_params=pltpu.CompilerParams(vmem_limit_bytes=8 * MIB),
        cost_estimate=pl.CostEstimate(flops=MIB, bytes_accessed=2 * MIB, transcendentals=0),
        name="turned_tiles",
    )(*own)


def edge_kernel(groups, *refs):
    got = refs[: len(groups)]
    from_below, from_above, to_below, to_above = refs[len(groups) :]
    lane = lane_index((L2, LANES))
    thin = lane_index((1, LANES))
    for ref in (to_below, to_above):
        ref[...] = jnp.zeros_like(ref)
    for place, (dx, dy) in enumerate(plane_offsets()):
        far = find_tile(groups, got, -dx, -dy, -2)
        close = pltpu.roll(find_tile(groups, got, -dx, -dy, -1), 3 * L2, 1)
        value = jnp.where(lane < 2 * L2, far, close) * from_below[place]
        row = jnp.sum(value, axis=0, keepdims=True)
        cell = cell_of(dx, dy, 1)
        to_below[cell : cell + 1, :] = jnp.where(thin >= 3 * L2, row, 0.0)
        cell = cell_of(dx, dy, 2)
        to_below[cell : cell + 1, :] = jnp.where(thin >= 2 * L2, pltpu.roll(row, 2 * L2, 1), 0.0)
        far = find_tile(groups, got, -dx, -dy, 2)
        close = pltpu.roll(find_tile(groups, got, -dx, -dy, 1), L2, 1)
        value = jnp.where(lane >= 2 * L2, far, close) * from_above[place]
        row = jnp.sum(value, axis=0, keepdims=True)
        cell = cell_of(dx, dy, -1)
        to_above[cell : cell + 1, :] = jnp.where(thin < L2, row, 0.0)
        cell = cell_of(dx, dy, -2)
        to_above[cell : cell + 1, :] = jnp.where(thin < 2 * L2, pltpu.roll(row, 2 * L2, 1), 0.0)


def edge_sums(groups, got, from_below, from_above):
    shape = jax.ShapeDtypeStruct((SUM_ROWS, LANES), f32)
    return pl.pallas_call(
        functools.partial(edge_kernel, groups),
        out_shape=(shape, shape),
        in_specs=in_vmem(len(got) + 2),
        out_specs=tuple(in_vmem(2)),
        compiler_params=pltpu.CompilerParams(vmem_limit_bytes=8 * MIB),
        name="edge_sums",
    )(*got, from_below, from_above)


def slab_kernel(groups, *refs):
    got = refs[: len(groups)]
    turned_ref, tau_ref, sums, flat_ref = refs[len(groups) :]
    flat_kernel(tau_ref, flat_ref)
    sums[WINDOW:, :] = jnp.zeros((SUM_ROWS - WINDOW, LANES), f32)
    lane = lane_index((1, LANES))
    for dx, dy in plane_offsets():
        for dz in range(-2, 3):
            cell = cell_of(dx, dy, dz)
            tile = find_tile(groups, got, -dx, -dy, -dz)
            if dz != 0:
                tile = pltpu.roll(tile, -dz % DEPTH * L2, 1)
            row = jnp.sum(tile * turned_ref[cell], axis=0, keepdims=True)
            if dz > 0:
                row = jnp.where(lane < (DEPTH - dz) * L2, row, 0.0)
            elif dz < 0:
                row = jnp.where(lane >= -dz * L2, row, 0.0)
            sums[cell : cell + 1, :] = row


def slab_sums(groups, got, turned, tau):
    return pl.pallas_call(
        functools.partial(slab_kernel, groups),
        out_shape=(
            jax.ShapeDtypeStruct((SUM_ROWS, LANES), f32),
            jax.ShapeDtypeStruct((DEPTH, L2 * L2), f32),
        ),
        in_specs=in_vmem(len(got) + 2),
        out_specs=tuple(in_vmem(2)),
        compiler_params=pltpu.CompilerParams(vmem_limit_bytes=8 * MIB),
        cost_estimate=pl.CostEstimate(flops=MIB, bytes_accessed=2 * MIB, transcendentals=0),
        name="slab_sums",
    )(*got, turned, tau)


def total_kernel(slab_ref, above_ref, below_ref, out_ref):
    sums = slab_ref[...] + (above_ref[...] + below_ref[...])
    site = lax.broadcasted_iota(jnp.int32, (8, LANES), 0)
    pick = (lane_index((8, LANES)) // L2 == site).astype(f32).astype(bf16)
    high = sums.astype(bf16)
    rest = sums - high.astype(f32)
    middle = rest.astype(bf16)
    low = (rest - middle.astype(f32)).astype(bf16)
    total = lax.dot_general(
        pick,
        jnp.concatenate([high, middle, low], axis=0),
        (((1,), (1,)), ((), ())),
        preferred_element_type=f32,
    )
    total = (total[:, :SUM_ROWS] + total[:, SUM_ROWS : 2 * SUM_ROWS]) + total[:, 2 * SUM_ROWS :]
    out_ref[...] = total[:DEPTH, :WINDOW]


def total_sums(slab, above, below):
    return pl.pallas_call(
        total_kernel,
        out_shape=jax.ShapeDtypeStruct((DEPTH, WINDOW), f32),
        in_specs=in_vmem(3),
        out_specs=in_vmem(1)[0],
        compiler_params=pltpu.CompilerParams(vmem_limit_bytes=4 * MIB),
        name="total_sums",
    )(slab, above, below)


def plane_groups():
    counts = (lax.axis_size("gx"), lax.axis_size("gy"))
    groups = {}
    for ox, oy in plane_offsets():
        groups.setdefault((ox % counts[0], oy % counts[1]), []).append((ox, oy))
    return groups


def body(t_matrix, structure, species, members, delta_table):
    own = own_tile(t_matrix.reshape(DEPTH, L2 * L2))
    structure = structure[0]

    below, above = shifted(own, (0, 0, 1)), shifted(own, (0, 0, -1))
    first = split_piece(0, structure, own)
    slabs = jnp.stack([own, below, above])
    slabs, structure, *first = lax.optimization_barrier((slabs, structure, *first))
    if lax.axis_size("gx") == 2:
        sides = [shifted(slabs, (1, 0, 0)), slabs]
    else:
        sides = [shifted(slabs, (1, 0, 0)), slabs, shifted(slabs, (-1, 0, 0))]
    second = split_piece(1, structure, own)
    plane = jnp.stack(sides)
    plane, structure, *second = lax.optimization_barrier((plane, structure, *second))
    planes = [shifted(plane, (0, 1, 0)), plane, shifted(plane, (0, -1, 0))]
    third = split_piece(2, structure, own)
    member, delta = setup(
        species.reshape(1, DEPTH), members.reshape(DEPTH, WINDOW), delta_table
    )
    near = jnp.stack(planes)
    parts, firsts = zip(first, second, third)

    table = plane_groups()
    shifts = list(table)
    stages = [
        [shift for shift in shifts if shift[0] != 0 and shift[1] == 0],
        [shift for shift in shifts if shift[0] != 0 and shift[1] != 0],
        [shift for shift in shifts if shift[0] == 0],
    ]
    *tiles, column, window = first_stage(
        [table[shift] for shift in stages[0]], parts, firsts, near, member, own, delta
    )
    blocks = dict(zip(stages[0], tiles))
    for stage in stages[1:]:
        *tiles, tau = next_stage(
            [table[shift] for shift in stage], parts, column, window, own, delta
        ) + ((None,) if (0, 0) not in stage else ())
        blocks.update(zip(stage, tiles))
    groups = [table[shift] for shift in shifts]
    sent = [blocks[shift] for shift in shifts]
    got = [
        block if shift == (0, 0) else shifted(block, shift + (0,))
        for shift, block in zip(shifts, sent)
    ]
    turned, up, down = turned_tiles(groups, sent)
    from_below = shifted(up, (0, 0, 1))
    from_above = shifted(down, (0, 0, -1))
    to_below, to_above = edge_sums(groups, got, from_below, from_above)
    above = shifted(to_below, (0, 0, -1))
    below = shifted(to_above, (0, 0, 1))
    slab, site_tau = slab_sums(groups, got, turned, tau)
    pairs = total_sums(slab, above, below)
    return (
        site_tau.reshape(1, 1, 1, DEPTH, L2 * L2),
        pairs.reshape(1, 1, DEPTH, WINDOW),
    )


def solution(mesh):
    placed = (
        P(None, "gx", "gy", "gz", None),
        P(),
        P("gx", "gy", "gz"),
        P("gx", "gy", "gz", None),
        P(),
    )
    return jax.shard_map(
        body,
        mesh=mesh,
        in_specs=placed,
        out_specs=(P(None, "gx", "gy", "gz", None), P("gx", "gy", "gz", None)),
        check_vma=False,
    )
```

```python
import functools

import jax
import jax.numpy as jnp
import numpy as np
from jax import lax
from jax.experimental import pallas as pl
from jax.experimental.pallas import tpu as pltpu
from jax.sharding import PartitionSpec as P


L2 = 32
WINDOW = 45
ITERS = 4
SPECIES = 4
DEPTH = 4
LANES = DEPTH * L2
ROWS = WINDOW * L2
CENTRE = WINDOW // 2
SUM_ROWS = 48
PIECES = 3
PIECE = WINDOW // PIECES
PIECE_ROWS = PIECE * L2
SPLIT_STEPS = 3
CHUNK = 15
MESH_AXES = ("gx", "gy", "gz")


bf16 = jnp.bfloat16
f32 = jnp.float32
MIB = 1 << 20


def shifted(x, shift):
    sizes = [lax.axis_size(axis) for axis in MESH_AXES]
    pairs = []
    for source in np.ndindex(*sizes):
        target = [(i + d) % n for i, d, n in zip(source, shift, sizes)]
        pairs.append(
            (int(np.ravel_multi_index(source, sizes)), int(np.ravel_multi_index(target, sizes)))
        )
    return lax.ppermute(x, MESH_AXES, pairs)


def in_vmem(count):
    return [pl.BlockSpec(memory_space=pltpu.VMEM)] * count


def in_hbm(x):
    return pltpu.with_memory_space_constraint(x, pltpu.HBM)


def halves(x):
    high = x.astype(bf16)
    return high, (x - high.astype(f32)).astype(bf16)


def lane_index(shape):
    return lax.broadcasted_iota(jnp.int32, shape, len(shape) - 1)


def tile_kernel(flat_ref, tile_ref):
    row = lax.broadcasted_iota(jnp.int32, (DEPTH, LANES), 0)
    diagonal = lane_index((DEPTH, LANES)) // L2 == row
    for j in range(L2 // DEPTH):
        part = flat_ref[:, j * LANES : (j + 1) * LANES]
        rolled = [part] + [pltpu.roll(part, m * L2, 1) for m in range(1, DEPTH)]
        for k in range(DEPTH):
            picked = jnp.zeros((DEPTH, LANES), f32)
            for m in range(DEPTH):
                picked = jnp.where(diagonal & (row == (m + k) % DEPTH), rolled[m], picked)
            a = j * DEPTH + k
            tile_ref[a : a + 1, :] = jnp.sum(picked, axis=0, keepdims=True)


def flat_kernel(tile_ref, flat_ref):
    row = lax.broadcasted_iota(jnp.int32, (DEPTH, LANES), 0)
    diagonal = lane_index((DEPTH, LANES)) // L2 == row
    for j in range(L2 // DEPTH):
        spread = []
        for k in range(DEPTH):
            a = j * DEPTH + k
            line = jnp.broadcast_to(tile_ref[a : a + 1, :], (DEPTH, LANES))
            spread.append(jnp.where(diagonal, line, 0.0))
        value = jnp.zeros((DEPTH, LANES), f32)
        for m in range(DEPTH):
            picked = jnp.zeros((DEPTH, LANES), f32)
            for k in range(DEPTH):
                picked = jnp.where(row == (k - m) % DEPTH, spread[k], picked)
            value = value + (picked if m == 0 else pltpu.roll(picked, m * L2, 1))
        flat_ref[:, j * LANES : (j + 1) * LANES] = value


def own_tile(flat):
    return pl.pallas_call(
        tile_kernel,
        out_shape=jax.ShapeDtypeStruct((L2, LANES), f32),
        in_specs=in_vmem(1),
        out_specs=in_vmem(1)[0],
        compiler_params=pltpu.CompilerParams(vmem_limit_bytes=4 * MIB),
        name="own_tile",
    )(flat)


def split_kernel(piece, structure_hbm, own_ref, *refs):
    parts_ref, image_ref, buffer, sems = refs
    step_rows = PIECE_ROWS // SPLIT_STEPS

    def fetch(step):
        rows = pl.ds(piece * PIECE_ROWS + step * step_rows, step_rows)
        return pltpu.make_async_copy(structure_hbm.at[rows, :], buffer.at[step], sems.at[step])

    for step in range(SPLIT_STEPS):
        fetch(step).start()
    lane_tile = CENTRE * L2 // LANES * LANES
    before = CENTRE * L2 - lane_tile
    own_parts = jnp.concatenate(halves(own_ref[...]), axis=1)
    own_parts = jnp.concatenate(
        [
            jnp.zeros((before, 2 * LANES), bf16),
            own_parts,
            jnp.zeros((LANES - before - L2, 2 * LANES), bf16),
        ],
        axis=0,
    )
    half = L2 // 2
    for step in range(SPLIT_STEPS):
        fetch(step).wait()

        def half_cell(i, carry, step=step):
            source = pl.ds(pl.multiple_of(i * half, half), half)
            target = step * 2 * step_rows + i // 2 * 2 * L2 + i % 2 * half
            high, low = halves(buffer[step, source, :])
            parts_ref[pl.ds(pl.multiple_of(target, half), half), :] = high
            parts_ref[pl.ds(pl.multiple_of(target + L2, half), half), :] = low
            return carry

        lax.fori_loop(0, step_rows // half, half_cell, 0, unroll=2)
    product = jnp.dot(
        parts_ref[:, lane_tile : lane_tile + LANES], own_parts, preferred_element_type=f32
    )
    image_ref[...] = four_products(product)


def split_piece(piece, structure, own):
    return pl.pallas_call(
        functools.partial(split_kernel, piece),
        out_shape=(
            jax.ShapeDtypeStruct((2 * PIECE_ROWS, ROWS), bf16),
            jax.ShapeDtypeStruct((PIECE, L2, LANES), f32),
        ),
        in_specs=[pl.BlockSpec(memory_space=pltpu.HBM)] + in_vmem(1),
        out_specs=tuple(in_vmem(2)),
        scratch_shapes=[
            pltpu.VMEM((SPLIT_STEPS, PIECE_ROWS // SPLIT_STEPS, ROWS), f32),
            pltpu.SemaphoreType.DMA((SPLIT_STEPS,)),
        ],
        compiler_params=pltpu.CompilerParams(vmem_limit_bytes=8 * MIB),
        cost_estimate=pl.CostEstimate(
            flops=MIB, bytes_accessed=4 * PIECE_ROWS * ROWS, transcendentals=0
        ),
        name="split_piece",
    )(in_hbm(structure), own)


def setup_kernel(
    species_hbm,
    members_hbm,
    table_hbm,
    member_ref,
    delta_ref,
    species_ref,
    members_ref,
    table_ref,
    table_tile,
    sems,
):
    moves = [(species_hbm, species_ref), (members_hbm, members_ref), (table_hbm, table_ref)]
    copies = [
        pltpu.make_async_copy(source, target, sems.at[i])
        for i, (source, target) in enumerate(moves)
    ]
    for copy in copies:
        copy.start()
    for copy in copies:
        copy.wait()
    tile_kernel(table_ref, table_tile)
    table = table_tile[...]
    moved = [table] + [pltpu.roll(table, m * L2, 1) for m in range(1, SPECIES)]
    group = lane_index((L2, LANES)) // L2
    delta = jnp.zeros((L2, LANES), f32)
    for s in range(DEPTH):
        for kind in range(SPECIES):
            here = (group == s) & (species_ref[0, s] == kind)
            delta = jnp.where(here, moved[(s - kind) % SPECIES], delta)
    delta_ref[...] = delta

    cells = lax.broadcasted_iota(jnp.int32, (WINDOW, WINDOW), 0)
    group = lane_index((WINDOW, LANES)) // L2
    member = jnp.zeros((WINDOW, LANES), f32)
    for s in range(DEPTH):
        found = (members_ref[s : s + 1, :] == cells).astype(f32)
        found = jnp.max(found, axis=1, keepdims=True)
        member = jnp.where(group == s, found, member)
    member_ref[...] = member


def setup(species, members, table):
    return pl.pallas_call(
        setup_kernel,
        out_shape=(
            jax.ShapeDtypeStruct((WINDOW, LANES), f32),
            jax.ShapeDtypeStruct((L2, LANES), f32),
        ),
        in_specs=[pl.BlockSpec(memory_space=pltpu.HBM)] * 3,
        out_specs=tuple(in_vmem(2)),
        scratch_shapes=[
            pltpu.SMEM((1, DEPTH), jnp.int32),
            pltpu.VMEM((DEPTH, WINDOW), jnp.int32),
            pltpu.VMEM((SPECIES, L2 * L2), f32),
            pltpu.VMEM((L2, LANES), f32),
            pltpu.SemaphoreType.DMA((3,)),
        ],
        compiler_params=pltpu.CompilerParams(vmem_limit_bytes=2 * MIB),
        name="setup",
    )(in_hbm(species), in_hbm(members), in_hbm(table))


def four_products(product):
    parts = product.reshape(-1, 2, L2, 2 * LANES)
    high, low = parts[:, 0], parts[:, 1]
    return (high[..., :LANES] + high[..., LANES:]) + (low[..., :LANES] + low[..., LANES:])


def site_blocks(tile):
    lane = lane_index((L2, LANES))
    masks = [(lane // L2 == s).astype(f32).astype(bf16) for s in range(DEPTH)]
    return jnp.concatenate([tile * mask for mask in masks], axis=0)


def moved(window, cell, image):
    blocks = jnp.concatenate([site_blocks(part) for part in halves(image)], axis=1)
    product = jnp.dot(window[cell * 2 * L2 : (cell + 1) * 2 * L2, :], blocks, preferred_element_type=f32)
    return four_products(product)[0]


def keep(column, place, value):
    high, low = halves(value)
    rows = slice(place * L2, (place + 1) * L2)
    column[rows, :LANES] = high
    column[rows, LANES:] = low


def images(parts, cells, column):
    rows = []
    for cell in cells:
        base = cell % PIECE * 2 * L2
        if rows and rows[-1][0] == cell // PIECE and rows[-1][2] == base:
            rows[-1][2] = base + 2 * L2
        else:
            rows.append([cell // PIECE, base, base + 2 * L2])
    left = [parts[piece][low:high, :] for piece, low, high in rows]
    left = left[0] if len(left) == 1 else jnp.concatenate(left, axis=0)
    return four_products(jnp.dot(left, column[...], preferred_element_type=f32))


def window_tile(near_ref, cell):
    dx, dy, dz = cell // 15, cell // 5 % 3, cell % 5 - 2
    dx = dx % near_ref.shape[1]
    own = near_ref[dy, dx, 0]
    if dz == 0:
        return own
    lane = lane_index((L2, LANES))
    if dz > 0:
        joined = jnp.where(lane < dz * L2, near_ref[dy, dx, 2], own)
        return pltpu.roll(joined, LANES - dz * L2, 1)
    joined = jnp.where(lane >= LANES + dz * L2, near_ref[dy, dx, 1], own)
    return pltpu.roll(joined, -dz * L2, 1)


def sweep_over(parts, chunks, source, use_image, slots):
    for i, chunk in enumerate(chunks):
        slots[i % 2][: len(chunk)] = images(parts, chunk, source)
        if i > 0:
            use_image(i - 1, slots[(i - 1) % 2])
    use_image(len(chunks) - 1, slots[(len(chunks) - 1) % 2])


def last_sweep(parts, column, window, own_ref, delta_ref, stage, sent, tau_ref, slots, final):
    high, low = (site_blocks(part) for part in halves(delta_ref[...]))
    delta = jnp.concatenate(
        [
            jnp.concatenate([high, low], axis=1),
            jnp.concatenate([high, jnp.zeros_like(high)], axis=1),
        ],
        axis=0,
    )
    chunks = [[cell_of(ox, oy, oz) for ox, oy in group for oz in range(-2, 3)] for group in stage]

    def use_image(i, slot):
        for place, cell in enumerate(chunks[i]):
            value = moved(window, cell, slot[place])
            if cell == CENTRE:
                value = value + own_ref[...]
                tau_ref[...] = value
            keep(final, place, value)
        count = len(chunks[i])
        product = jnp.dot(final[: count * L2, :], delta, preferred_element_type=f32)
        value = product[:, :LANES] + product[:, LANES:]
        sent[i][...] = value.reshape(count, L2, LANES)

    sweep_over(parts, chunks, column, use_image, slots)


def first_kernel(stage, *refs):
    parts, firsts = refs[:PIECES], refs[PIECES : 2 * PIECES]
    near_ref, member_ref, own_ref, delta_ref = refs[2 * PIECES : 2 * PIECES + 4]
    outs = refs[2 * PIECES + 4 :]
    sent = outs[: len(stage)]
    column, window, other, slot_a, slot_b, final = outs[len(stage) :]
    slots = (slot_a, slot_b)
    for cell in range(WINDOW):
        high, low = halves(window_tile(near_ref, cell) * member_ref[cell : cell + 1, :])
        base = cell * 2 * L2
        window[base : base + L2, :] = high
        window[base + L2 : base + 2 * L2, :] = low

    def update(target, cell, image):
        value = moved(window, cell, image)
        if cell == CENTRE:
            value = value + own_ref[...]
        keep(target, cell, value)

    full = [list(range(base, base + CHUNK)) for base in range(0, WINDOW, CHUNK)]
    source, target = (column, other) if ITERS % 2 == 0 else (other, column)
    for cell in range(WINDOW):
        update(source, cell, firsts[cell // PIECE][cell % PIECE])
    for _ in range(1, ITERS - 1):

        def use_image(i, slot, target=target):
            for place, cell in enumerate(full[i]):
                update(target, cell, slot[place])

        sweep_over(parts, full, source, use_image, slots)
        source, target = target, source
    last_sweep(parts, source, window, own_ref, delta_ref, stage, sent, None, slots, final)


def next_kernel(stage, *refs):
    parts = refs[:PIECES]
    column, window, own_ref, delta_ref = refs[PIECES : PIECES + 4]
    sent = refs[PIECES + 4 : PIECES + 4 + len(stage)]
    rest = refs[PIECES + 4 + len(stage) :]
    tau_ref = rest[0] if len(rest) == 4 else None
    slot_a, slot_b, final = rest[-3:]
    last_sweep(
        parts, column, window, own_ref, delta_ref, stage, sent, tau_ref, (slot_a, slot_b), final
    )


def stage_call(kernel, stage, extra_outs, extra_scratch, operands, flops):
    longest = max(CHUNK, 5 * max(len(group) for group in stage))
    out_shape = [jax.ShapeDtypeStruct((5 * len(group), L2, LANES), f32) for group in stage]
    out_shape += extra_outs
    return pl.pallas_call(
        functools.partial(kernel, stage),
        out_shape=tuple(out_shape),
        in_specs=in_vmem(len(operands)),
        out_specs=tuple(in_vmem(len(out_shape))),
        scratch_shapes=extra_scratch
        + [pltpu.VMEM((longest, L2, LANES), f32)] * 2
        + [pltpu.VMEM((longest * L2, 2 * LANES), bf16)],
        compiler_params=pltpu.CompilerParams(vmem_limit_bytes=16 * MIB),
        cost_estimate=pl.CostEstimate(flops=flops, bytes_accessed=MIB, transcendentals=0),
    )(*operands)


def first_stage(stage, parts, firsts, near, member, own, delta):
    return stage_call(
        first_kernel,
        stage,
        [
            jax.ShapeDtypeStruct((ROWS, 2 * LANES), bf16),
            jax.ShapeDtypeStruct((2 * ROWS, LANES), bf16),
        ],
        [pltpu.VMEM((ROWS, 2 * LANES), bf16)],
        (*parts, *firsts, near, member, own, delta),
        2 * 4 * (ITERS - 2) * ROWS * ROWS * LANES,
    )


def next_stage(stage, parts, column, window, own, delta):
    tau = [jax.ShapeDtypeStruct((L2, LANES), f32)]
    return stage_call(
        next_kernel,
        stage,
        tau if any((0, 0) in group for group in stage) else [],
        [],
        (*parts, column, window, own, delta),
        2 * ROWS * ROWS * LANES,
    )


def find_tile(groups, refs, ox, oy, oz):
    for group, ref in zip(groups, refs):
        if (ox, oy) in group:
            return ref[group.index((ox, oy)) * 5 + oz + 2]
    raise ValueError("no tile")


def plane_offsets():
    return [(ox, oy) for ox in (-1, 0, 1) for oy in (-1, 0, 1)]


def cell_of(dx, dy, dz):
    return ((dx + 1) * 3 + dy + 1) * 5 + dz + 2


def turn_kernel(groups, *refs):
    own = refs[: len(groups)]
    out, up_ref, down_ref = refs[len(groups) :]
    lane = lane_index((L2, LANES))

    def cell_tile(cell):
        cell = min(cell, WINDOW - 1)
        return find_tile(groups, own, cell // 15 - 1, cell // 5 % 3 - 1, cell % 5 - 2)

    for base in range(0, WINDOW, DEPTH):
        block = jnp.concatenate([cell_tile(base + k) for k in range(DEPTH)], axis=0)
        turned = block.T
        pieces = [turned[s * L2 : (s + 1) * L2] for s in range(DEPTH)]
        for k in range(min(DEPTH, WINDOW - base)):
            value = pieces[0] if k == 0 else pltpu.roll(pieces[0], (-k % DEPTH) * L2, 1)
            for s in range(1, DEPTH):
                move = (s - k) % DEPTH
                piece = pieces[s] if move == 0 else pltpu.roll(pieces[s], move * L2, 1)
                value = jnp.where(lane // L2 == s, piece, value)
            out[base + k] = value
    for place, (dx, dy) in enumerate(plane_offsets()):
        far = pltpu.roll(out[cell_of(dx, dy, 2)], 2 * L2, 1)
        up_ref[place] = jnp.where(lane < 2 * L2, far, out[cell_of(dx, dy, 1)])
        far = pltpu.roll(out[cell_of(dx, dy, -2)], 2 * L2, 1)
        down_ref[place] = jnp.where(lane >= 2 * L2, far, out[cell_of(dx, dy, -1)])


def turned_tiles(groups, own):
    edge = jax.ShapeDtypeStruct((9, L2, LANES), f32)
    return pl.pallas_call(
        functools.partial(turn_kernel, groups),
        out_shape=(jax.ShapeDtypeStruct((WINDOW, L2, LANES), f32), edge, edge),
        in_specs=in_vmem(len(own)),
        out_specs=tuple(in_vmem(3)),
        compiler_params=pltpu.CompilerParams(vmem_limit_bytes=8 * MIB),
        cost_estimate=pl.CostEstimate(flops=MIB, bytes_accessed=2 * MIB, transcendentals=0),
        name="turned_tiles",
    )(*own)


def edge_kernel(groups, *refs):
    got = refs[: len(groups)]
    from_below, from_above, to_below, to_above = refs[len(groups) :]
    lane = lane_index((L2, LANES))
    thin = lane_index((1, LANES))
    for ref in (to_below, to_above):
        ref[...] = jnp.zeros_like(ref)
    for place, (dx, dy) in enumerate(plane_offsets()):
        far = find_tile(groups, got, -dx, -dy, -2)
        close = pltpu.roll(find_tile(groups, got, -dx, -dy, -1), 3 * L2, 1)
        value = jnp.where(lane < 2 * L2, far, close) * from_below[place]
        row = jnp.sum(value, axis=0, keepdims=True)
        cell = cell_of(dx, dy, 1)
        to_below[cell : cell + 1, :] = jnp.where(thin >= 3 * L2, row, 0.0)
        cell = cell_of(dx, dy, 2)
        to_below[cell : cell + 1, :] = jnp.where(thin >= 2 * L2, pltpu.roll(row, 2 * L2, 1), 0.0)
        far = find_tile(groups, got, -dx, -dy, 2)
        close = pltpu.roll(find_tile(groups, got, -dx, -dy, 1), L2, 1)
        value = jnp.where(lane >= 2 * L2, far, close) * from_above[place]
        row = jnp.sum(value, axis=0, keepdims=True)
        cell = cell_of(dx, dy, -1)
        to_above[cell : cell + 1, :] = jnp.where(thin < L2, row, 0.0)
        cell = cell_of(dx, dy, -2)
        to_above[cell : cell + 1, :] = jnp.where(thin < 2 * L2, pltpu.roll(row, 2 * L2, 1), 0.0)


def edge_sums(groups, got, from_below, from_above):
    shape = jax.ShapeDtypeStruct((SUM_ROWS, LANES), f32)
    return pl.pallas_call(
        functools.partial(edge_kernel, groups),
        out_shape=(shape, shape),
        in_specs=in_vmem(len(got) + 2),
        out_specs=tuple(in_vmem(2)),
        compiler_params=pltpu.CompilerParams(vmem_limit_bytes=8 * MIB),
        name="edge_sums",
    )(*got, from_below, from_above)


def slab_kernel(groups, *refs):
    got = refs[: len(groups)]
    turned_ref, tau_ref, sums, flat_ref = refs[len(groups) :]
    flat_kernel(tau_ref, flat_ref)
    sums[WINDOW:, :] = jnp.zeros((SUM_ROWS - WINDOW, LANES), f32)
    lane = lane_index((1, LANES))
    for dx, dy in plane_offsets():
        for dz in range(-2, 3):
            cell = cell_of(dx, dy, dz)
            tile = find_tile(groups, got, -dx, -dy, -dz)
            if dz != 0:
                tile = pltpu.roll(tile, -dz % DEPTH * L2, 1)
            row = jnp.sum(tile * turned_ref[cell], axis=0, keepdims=True)
            if dz > 0:
                row = jnp.where(lane < (DEPTH - dz) * L2, row, 0.0)
            elif dz < 0:
                row = jnp.where(lane >= -dz * L2, row, 0.0)
            sums[cell : cell + 1, :] = row


def slab_sums(groups, got, turned, tau):
    return pl.pallas_call(
        functools.partial(slab_kernel, groups),
        out_shape=(
            jax.ShapeDtypeStruct((SUM_ROWS, LANES), f32),
            jax.ShapeDtypeStruct((DEPTH, L2 * L2), f32),
        ),
        in_specs=in_vmem(len(got) + 2),
        out_specs=tuple(in_vmem(2)),
        compiler_params=pltpu.CompilerParams(vmem_limit_bytes=8 * MIB),
        cost_estimate=pl.CostEstimate(flops=MIB, bytes_accessed=2 * MIB, transcendentals=0),
        name="slab_sums",
    )(*got, turned, tau)


def total_kernel(slab_ref, above_ref, below_ref, out_ref):
    sums = slab_ref[...] + (above_ref[...] + below_ref[...])
    site = lax.broadcasted_iota(jnp.int32, (8, LANES), 0)
    pick = (lane_index((8, LANES)) // L2 == site).astype(f32).astype(bf16)
    high = sums.astype(bf16)
    rest = sums - high.astype(f32)
    middle = rest.astype(bf16)
    low = (rest - middle.astype(f32)).astype(bf16)
    total = lax.dot_general(
        pick,
        jnp.concatenate([high, middle, low], axis=0),
        (((1,), (1,)), ((), ())),
        preferred_element_type=f32,
    )
    total = (total[:, :SUM_ROWS] + total[:, SUM_ROWS : 2 * SUM_ROWS]) + total[:, 2 * SUM_ROWS :]
    out_ref[...] = total[:DEPTH, :WINDOW]


def total_sums(slab, above, below):
    return pl.pallas_call(
        total_kernel,
        out_shape=jax.ShapeDtypeStruct((DEPTH, WINDOW), f32),
        in_specs=in_vmem(3),
        out_specs=in_vmem(1)[0],
        compiler_params=pltpu.CompilerParams(vmem_limit_bytes=4 * MIB),
        name="total_sums",
    )(slab, above, below)


def plane_groups():
    counts = (lax.axis_size("gx"), lax.axis_size("gy"))
    groups = {}
    for ox, oy in plane_offsets():
        groups.setdefault((ox % counts[0], oy % counts[1]), []).append((ox, oy))
    return groups


def body(t_matrix, structure, species, members, delta_table):
    own = own_tile(t_matrix.reshape(DEPTH, L2 * L2))
    structure = structure[0]

    below, above = shifted(own, (0, 0, 1)), shifted(own, (0, 0, -1))
    first = split_piece(0, structure, own)
    slabs = jnp.stack([own, below, above])
    slabs, structure, *first = lax.optimization_barrier((slabs, structure, *first))
    if lax.axis_size("gx") == 2:
        sides = [shifted(slabs, (1, 0, 0)), slabs]
    else:
        sides = [shifted(slabs, (1, 0, 0)), slabs, shifted(slabs, (-1, 0, 0))]
    second = split_piece(1, structure, own)
    plane = jnp.stack(sides)
    plane, structure, *second = lax.optimization_barrier((plane, structure, *second))
    planes = [shifted(plane, (0, 1, 0)), plane, shifted(plane, (0, -1, 0))]
    third = split_piece(2, structure, own)
    member, delta = setup(
        species.reshape(1, DEPTH), members.reshape(DEPTH, WINDOW), delta_table
    )
    near = jnp.stack(planes)
    parts, firsts = zip(first, second, third)

    table = plane_groups()
    shifts = list(table)
    stages = [
        [shift for shift in shifts if shift[0] != 0 and shift[1] == 0],
        [shift for shift in shifts if shift[0] != 0 and shift[1] != 0],
        [shift for shift in shifts if shift[0] == 0],
    ]
    *tiles, column, window = first_stage(
        [table[shift] for shift in stages[0]], parts, firsts, near, member, own, delta
    )
    blocks = dict(zip(stages[0], tiles))
    got = {}
    for number, stage in enumerate(stages):
        if number > 0:
            tiles = next_stage([table[shift] for shift in stage], parts, column, window, own, delta)
            if (0, 0) in stage:
                tau = tiles[-1]
            blocks.update(zip(stage, tiles))
        for shift in stage:
            block = blocks[shift]
            got[shift] = block if shift == (0, 0) else shifted(block, shift + (0,))
    groups = [table[shift] for shift in shifts]
    sent = [blocks[shift] for shift in shifts]
    got = [got[shift] for shift in shifts]
    turned, up, down = turned_tiles(groups, sent)
    from_below = shifted(up, (0, 0, 1))
    from_above = shifted(down, (0, 0, -1))
    to_below, to_above = edge_sums(groups, got, from_below, from_above)
    above = shifted(to_below, (0, 0, -1))
    below = shifted(to_above, (0, 0, 1))
    slab, site_tau = slab_sums(groups, got, turned, tau)
    pairs = total_sums(slab, above, below)
    return (
        site_tau.reshape(1, 1, 1, DEPTH, L2 * L2),
        pairs.reshape(1, 1, DEPTH, WINDOW),
    )


def solution(mesh):
    placed = (
        P(None, "gx", "gy", "gz", None),
        P(),
        P("gx", "gy", "gz"),
        P("gx", "gy", "gz", None),
        P(),
    )
    return jax.shard_map(
        body,
        mesh=mesh,
        in_specs=placed,
        out_specs=(P(None, "gx", "gy", "gz", None), P("gx", "gy", "gz", None)),
        check_vma=False,
    )
```

```python
import functools

import jax
import jax.numpy as jnp
import numpy as np
from jax import lax
from jax.experimental import pallas as pl
from jax.experimental.pallas import tpu as pltpu
from jax.sharding import PartitionSpec as P


L2 = 32
WINDOW = 45
ITERS = 4
SPECIES = 4
DEPTH = 4
LANES = DEPTH * L2
ROWS = WINDOW * L2
CENTRE = WINDOW // 2
SUM_ROWS = 48
PACK_ROWS = L2 + 8
PIECES = 3
PIECE = WINDOW // PIECES
PIECE_ROWS = PIECE * L2
SPLIT_STEPS = 3
CHUNK = 15
MESH_AXES = ("gx", "gy", "gz")


bf16 = jnp.bfloat16
f32 = jnp.float32
MIB = 1 << 20


def shifted(x, shift):
    sizes = [lax.axis_size(axis) for axis in MESH_AXES]
    pairs = []
    for source in np.ndindex(*sizes):
        target = [(i + d) % n for i, d, n in zip(source, shift, sizes)]
        pairs.append(
            (int(np.ravel_multi_index(source, sizes)), int(np.ravel_multi_index(target, sizes)))
        )
    return lax.ppermute(x, MESH_AXES, pairs)


def in_vmem(count):
    return [pl.BlockSpec(memory_space=pltpu.VMEM)] * count


def in_hbm(x):
    return pltpu.with_memory_space_constraint(x, pltpu.HBM)


def halves(x):
    high = x.astype(bf16)
    return high, (x - high.astype(f32)).astype(bf16)


def lane_index(shape):
    return lax.broadcasted_iota(jnp.int32, shape, len(shape) - 1)


def tile_kernel(flat_ref, tile_ref):
    row = lax.broadcasted_iota(jnp.int32, (DEPTH, LANES), 0)
    diagonal = lane_index((DEPTH, LANES)) // L2 == row
    for j in range(L2 // DEPTH):
        part = flat_ref[:, j * LANES : (j + 1) * LANES]
        rolled = [part] + [pltpu.roll(part, m * L2, 1) for m in range(1, DEPTH)]
        for k in range(DEPTH):
            picked = jnp.zeros((DEPTH, LANES), f32)
            for m in range(DEPTH):
                picked = jnp.where(diagonal & (row == (m + k) % DEPTH), rolled[m], picked)
            a = j * DEPTH + k
            tile_ref[a : a + 1, :] = jnp.sum(picked, axis=0, keepdims=True)


def flat_kernel(tile_ref, flat_ref):
    row = lax.broadcasted_iota(jnp.int32, (DEPTH, LANES), 0)
    diagonal = lane_index((DEPTH, LANES)) // L2 == row
    for j in range(L2 // DEPTH):
        spread = []
        for k in range(DEPTH):
            a = j * DEPTH + k
            line = jnp.broadcast_to(tile_ref[a : a + 1, :], (DEPTH, LANES))
            spread.append(jnp.where(diagonal, line, 0.0))
        value = jnp.zeros((DEPTH, LANES), f32)
        for m in range(DEPTH):
            picked = jnp.zeros((DEPTH, LANES), f32)
            for k in range(DEPTH):
                picked = jnp.where(row == (k - m) % DEPTH, spread[k], picked)
            value = value + (picked if m == 0 else pltpu.roll(picked, m * L2, 1))
        flat_ref[:, j * LANES : (j + 1) * LANES] = value


def pack_kernel(flat_hbm, members_hbm, species_hbm, pack_ref, flat_ref, members_ref, species_ref, sems):
    moves = [(flat_hbm, flat_ref), (members_hbm, members_ref), (species_hbm, species_ref)]
    copies = [
        pltpu.make_async_copy(source, target, sems.at[i])
        for i, (source, target) in enumerate(moves)
    ]
    for copy in copies:
        copy.start()
    for copy in copies:
        copy.wait()
    tile_kernel(flat_ref, pack_ref)
    pack_ref[L2:, :] = jnp.full((PACK_ROWS - L2, LANES), -1.0, f32)
    pack_ref[L2 : L2 + DEPTH, :WINDOW] = members_ref[...].astype(f32)
    pack_ref[L2 + DEPTH : L2 + DEPTH + 1, :DEPTH] = species_ref[...].astype(f32)


def packed_own(flat, members, species):
    return pl.pallas_call(
        pack_kernel,
        out_shape=jax.ShapeDtypeStruct((PACK_ROWS, LANES), f32),
        in_specs=[pl.BlockSpec(memory_space=pltpu.HBM)] * 3,
        out_specs=in_vmem(1)[0],
        scratch_shapes=[
            pltpu.VMEM((DEPTH, L2 * L2), f32),
            pltpu.VMEM((DEPTH, WINDOW), jnp.int32),
            pltpu.VMEM((1, DEPTH), jnp.int32),
            pltpu.SemaphoreType.DMA((3,)),
        ],
        compiler_params=pltpu.CompilerParams(vmem_limit_bytes=4 * MIB),
        name="packed_own",
    )(in_hbm(flat), in_hbm(members), in_hbm(species))


def split_kernel(piece, structure_hbm, parts_ref, buffer, sems):
    step_rows = PIECE_ROWS // SPLIT_STEPS

    def fetch(step):
        rows = pl.ds(piece * PIECE_ROWS + step * step_rows, step_rows)
        return pltpu.make_async_copy(structure_hbm.at[rows, :], buffer.at[step], sems.at[step])

    for step in range(SPLIT_STEPS):
        fetch(step).start()
    half = L2 // 2
    for step in range(SPLIT_STEPS):
        fetch(step).wait()

        def half_cell(i, carry, step=step):
            source = pl.ds(pl.multiple_of(i * half, half), half)
            target = step * 2 * step_rows + i // 2 * 2 * L2 + i % 2 * half
            high, low = halves(buffer[step, source, :])
            parts_ref[pl.ds(pl.multiple_of(target, half), half), :] = high
            parts_ref[pl.ds(pl.multiple_of(target + L2, half), half), :] = low
            return carry

        lax.fori_loop(0, step_rows // half, half_cell, 0, unroll=2)


def split_piece(piece, structure):
    return pl.pallas_call(
        functools.partial(split_kernel, piece),
        out_shape=jax.ShapeDtypeStruct((2 * PIECE_ROWS, ROWS), bf16),
        in_specs=[pl.BlockSpec(memory_space=pltpu.HBM)],
        out_specs=in_vmem(1)[0],
        scratch_shapes=[
            pltpu.VMEM((SPLIT_STEPS, PIECE_ROWS // SPLIT_STEPS, ROWS), f32),
            pltpu.SemaphoreType.DMA((SPLIT_STEPS,)),
        ],
        compiler_params=pltpu.CompilerParams(vmem_limit_bytes=8 * MIB),
        cost_estimate=pl.CostEstimate(
            flops=MIB, bytes_accessed=4 * PIECE_ROWS * ROWS, transcendentals=0
        ),
        name="split_piece",
    )(in_hbm(structure))


def both_tiles(own, below, above):
    lane = lane_index(own.shape)
    return [own, jnp.where(lane < 2 * L2, above, below)]


def setup_kernel(own_ref, below_ref, above_ref, table_hbm, member_ref, delta_ref, tile_ref, *rest):
    table_ref, table_tile, sem = rest
    copy = pltpu.make_async_copy(table_hbm, table_ref, sem.at[0])
    copy.start()
    cells = lax.broadcasted_iota(jnp.int32, (WINDOW, LANES), 0).astype(f32)
    group = lane_index((WINDOW, LANES)) // L2
    sources = [[own_ref] * DEPTH, [above_ref, above_ref, below_ref, below_ref]]
    for half, refs in enumerate(sources):
        member = jnp.zeros((WINDOW, LANES), f32)
        for g, ref in enumerate(refs):
            found = (ref[L2 + g : L2 + g + 1, :] == cells).astype(f32)
            found = jnp.max(found, axis=1, keepdims=True)
            member = jnp.where(group == g, found, member)
        member_ref[:, half * LANES : (half + 1) * LANES] = member
    tiles = both_tiles(own_ref[:L2, :], below_ref[:L2, :], above_ref[:L2, :])
    for half, tile in enumerate(tiles):
        tile_ref[:, half * LANES : (half + 1) * LANES] = tile

    copy.wait()
    tile_kernel(table_ref, table_tile)
    table = table_tile[...]
    turns = [table] + [pltpu.roll(table, m * L2, 1) for m in range(1, SPECIES)]
    group = lane_index((L2, LANES)) // L2
    thin = lane_index((1, LANES))
    row = slice(L2 + DEPTH, L2 + DEPTH + 1)
    for half, refs in enumerate(sources):
        delta = jnp.zeros((L2, LANES), f32)
        for g, ref in enumerate(refs):
            kinds = jnp.max(jnp.where(thin == g, ref[row, :], -1.0), axis=1, keepdims=True)
            for kind in range(SPECIES):
                here = (group == g) & (kinds == kind)
                delta = jnp.where(here, turns[(g - kind) % SPECIES], delta)
        delta_ref[:, half * LANES : (half + 1) * LANES] = delta


def setup(own, below, above, table):
    return pl.pallas_call(
        setup_kernel,
        out_shape=(
            jax.ShapeDtypeStruct((WINDOW, 2 * LANES), f32),
            jax.ShapeDtypeStruct((L2, 2 * LANES), f32),
            jax.ShapeDtypeStruct((L2, 2 * LANES), f32),
        ),
        in_specs=in_vmem(3) + [pl.BlockSpec(memory_space=pltpu.HBM)],
        out_specs=tuple(in_vmem(3)),
        scratch_shapes=[
            pltpu.VMEM((SPECIES, L2 * L2), f32),
            pltpu.VMEM((L2, LANES), f32),
            pltpu.SemaphoreType.DMA((1,)),
        ],
        compiler_params=pltpu.CompilerParams(vmem_limit_bytes=4 * MIB),
        name="setup",
    )(own, below, above, in_hbm(table))


def four_products(product):
    parts = product.reshape(-1, 2, L2, 2 * LANES)
    high, low = parts[:, 0], parts[:, 1]
    return (high[..., :LANES] + high[..., LANES:]) + (low[..., :LANES] + low[..., LANES:])


def first_image_kernel(*refs):
    parts, (tile_ref, image_ref) = refs[:PIECES], refs[PIECES:]
    lane_tile = CENTRE * L2 // LANES * LANES
    before = CENTRE * L2 - lane_tile
    for half in range(2):
        lanes = slice(half * LANES, (half + 1) * LANES)
        right = jnp.concatenate(halves(tile_ref[:, lanes]), axis=1)
        right = jnp.concatenate(
            [
                jnp.zeros((before, 2 * LANES), bf16),
                right,
                jnp.zeros((LANES - before - L2, 2 * LANES), bf16),
            ],
            axis=0,
        )
        for piece, ref in enumerate(parts):
            left = ref[:, lane_tile : lane_tile + LANES]
            product = jnp.dot(left, right, preferred_element_type=f32)
            image_ref[piece * PIECE : (piece + 1) * PIECE, :, lanes] = four_products(product)


def first_images(parts, tile):
    return pl.pallas_call(
        first_image_kernel,
        out_shape=jax.ShapeDtypeStruct((WINDOW, L2, 2 * LANES), f32),
        in_specs=in_vmem(PIECES + 1),
        out_specs=in_vmem(1)[0],
        compiler_params=pltpu.CompilerParams(vmem_limit_bytes=8 * MIB),
        name="first_images",
    )(*parts, tile)


def site_blocks(tile):
    lane = lane_index((L2, LANES))
    masks = [(lane // L2 == s).astype(f32).astype(bf16) for s in range(DEPTH)]
    return jnp.concatenate([tile * mask for mask in masks], axis=0)


def moved(window, cell, half, image):
    blocks = jnp.concatenate([site_blocks(part) for part in halves(image)], axis=1)
    left = window[cell * 2 * L2 : (cell + 1) * 2 * L2, half * LANES : (half + 1) * LANES]
    return four_products(jnp.dot(left, blocks, preferred_element_type=f32))[0]


HIGH_AT = (1, 2)
LOW_AT = (0, 3)


def keep(column, place, half, value):
    rows = slice(place * L2, (place + 1) * L2)
    for at, part in zip((HIGH_AT[half], LOW_AT[half]), halves(value)):
        column[rows, at * LANES : (at + 1) * LANES] = part


def set_images(parts, cells, column, slot):
    high, low = [], []
    for cell in cells:
        ref, base = parts[cell // PIECE], cell % PIECE * 2 * L2
        high.append(ref[base : base + L2, :])
        low.append(ref[base + L2 : base + 2 * L2, :])
    high, low = jnp.concatenate(high, axis=0), jnp.concatenate(low, axis=0)
    own = jnp.dot(high, column[:, : 2 * LANES], preferred_element_type=f32)
    other = jnp.dot(high, column[:, 2 * LANES :], preferred_element_type=f32)
    both = jnp.dot(low, column[:, LANES : 3 * LANES], preferred_element_type=f32)
    shape = (len(cells), L2, LANES)
    image = own[:, :LANES] + own[:, LANES:] + both[:, :LANES]
    slot[: len(cells), :, :LANES] = image.reshape(shape)
    image = other[:, :LANES] + other[:, LANES:] + both[:, LANES:]
    slot[: len(cells), :, LANES:] = image.reshape(shape)


def window_tiles(near_ref, cell):
    dx, dy, dz = cell // 15, cell // 5 % 3, cell % 5 - 2
    dx = dx % near_ref.shape[1]
    own, below, above = (near_ref[dy, dx, i] for i in range(3))
    group = lane_index((L2, LANES)) // L2
    first, second = own, jnp.where(group < 2, above, below)
    if dz > 0:
        first = jnp.where(group < dz, above, own)
        second = jnp.where(group < dz, own, jnp.where(group < 2 + dz, above, below))
    elif dz < 0:
        first = jnp.where(group >= DEPTH + dz, below, own)
        second = jnp.where(group >= DEPTH + dz, own, jnp.where(group < 2 + dz, above, below))
    move = -dz % DEPTH * L2
    return [tile if move == 0 else pltpu.roll(tile, move, 1) for tile in (first, second)]


def sweep_over(parts, chunks, source, use_image, slots):
    for i, chunk in enumerate(chunks):
        set_images(parts, chunk, source, slots[i % 2])
        if i > 0:
            use_image(i - 1, slots[(i - 1) % 2])
    use_image(len(chunks) - 1, slots[(len(chunks) - 1) % 2])


def delta_blocks(tile):
    high, low = (site_blocks(part) for part in halves(tile))
    return jnp.concatenate(
        [
            jnp.concatenate([high, low], axis=1),
            jnp.concatenate([high, jnp.zeros_like(high)], axis=1),
        ],
        axis=0,
    )


def last_sweep(parts, column, window, tile_ref, delta_ref, stage, sent, local, tau_ref, slots, final):
    deltas = [delta_blocks(delta_ref[:, half * LANES : (half + 1) * LANES]) for half in range(2)]
    chunks = [[cell_of(ox, oy, oz) for ox, oy in group for oz in range(-2, 3)] for group in stage]
    group_of = lane_index((L2, LANES)) // L2

    def use_image(i, slot):
        count = len(chunks[i])
        values = []
        for half in range(2):
            lanes = slice(half * LANES, (half + 1) * LANES)
            for place, cell in enumerate(chunks[i]):
                value = moved(window, cell, half, slot[place, :, lanes])
                if cell == CENTRE:
                    value = value + tile_ref[:, lanes]
                    if half == 0:
                        tau_ref[...] = value
                rows = slice(place * L2, (place + 1) * L2)
                high, low = halves(value)
                final[half, rows, :LANES] = high
                final[half, rows, LANES:] = low
            product = jnp.dot(
                final[half, : count * L2, :], deltas[half], preferred_element_type=f32
            )
            product = product[:, :LANES] + product[:, LANES:]
            values.append(product.reshape(count, L2, LANES))
        local[i][...] = values[0]
        for place, cell in enumerate(chunks[i]):
            oz = cell % 5 - 2
            value = values[0][place]
            if oz > 0:
                value = jnp.where(group_of >= DEPTH - oz, values[1][place], value)
            elif oz < 0:
                value = jnp.where(group_of < -oz, values[1][place], value)
            if oz != 0:
                value = pltpu.roll(value, oz % DEPTH * L2, 1)
            sent[i][place] = value

    sweep_over(parts, chunks, column, use_image, slots)


def first_kernel(stage, *refs):
    parts, refs = refs[:PIECES], refs[PIECES:]
    image_ref, near_ref, member_ref, tile_ref, delta_ref = refs[:5]
    sent, local = refs[5 : 5 + len(stage)], refs[5 + len(stage) : 5 + 2 * len(stage)]
    column, window, other, slot_a, slot_b, final = refs[5 + 2 * len(stage) :]
    slots = (slot_a, slot_b)
    halves_lanes = [slice(half * LANES, (half + 1) * LANES) for half in range(2)]
    for cell in range(WINDOW):
        base = cell * 2 * L2
        for lanes, tile in zip(halves_lanes, window_tiles(near_ref, cell)):
            high, low = halves(tile * member_ref[cell : cell + 1, lanes])
            window[base : base + L2, lanes] = high
            window[base + L2 : base + 2 * L2, lanes] = low

    def update(target, cell, image):
        for half, lanes in enumerate(halves_lanes):
            value = moved(window, cell, half, image[:, lanes])
            if cell == CENTRE:
                value = value + tile_ref[:, lanes]
            keep(target, cell, half, value)

    full = [list(range(base, base + CHUNK)) for base in range(0, WINDOW, CHUNK)]
    source, target = (column, other) if ITERS % 2 == 0 else (other, column)
    for cell in range(WINDOW):
        update(source, cell, image_ref[cell])
    for _ in range(1, ITERS - 1):

        def use_image(i, slot, target=target):
            for place, cell in enumerate(full[i]):
                update(target, cell, slot[place])

        sweep_over(parts, full, source, use_image, slots)
        source, target = target, source
    last_sweep(
        parts, source, window, tile_ref, delta_ref, stage, sent, local, None, slots, final
    )


def next_kernel(stage, *refs):
    parts, refs = refs[:PIECES], refs[PIECES:]
    column, window, tile_ref, delta_ref = refs[:4]
    sent, local = refs[4 : 4 + len(stage)], refs[4 + len(stage) : 4 + 2 * len(stage)]
    rest = refs[4 + 2 * len(stage) :]
    tau_ref = rest[0] if len(rest) == 4 else None
    slot_a, slot_b, final = rest[-3:]
    last_sweep(
        parts,
        column,
        window,
        tile_ref,
        delta_ref,
        stage,
        sent,
        local,
        tau_ref,
        (slot_a, slot_b),
        final,
    )


def stage_call(kernel, stage, extra_outs, extra_scratch, operands, flops):
    longest = max(CHUNK, 5 * max(len(group) for group in stage))
    out_shape = [jax.ShapeDtypeStruct((5 * len(group), L2, LANES), f32) for group in stage] * 2
    out_shape += extra_outs
    return pl.pallas_call(
        functools.partial(kernel, stage),
        out_shape=tuple(out_shape),
        in_specs=in_vmem(len(operands)),
        out_specs=tuple(in_vmem(len(out_shape))),
        scratch_shapes=extra_scratch
        + [pltpu.VMEM((longest, L2, 2 * LANES), f32)] * 2
        + [pltpu.VMEM((2, longest * L2, 2 * LANES), bf16)],
        compiler_params=pltpu.CompilerParams(vmem_limit_bytes=24 * MIB),
        cost_estimate=pl.CostEstimate(flops=flops, bytes_accessed=MIB, transcendentals=0),
    )(*operands)


def first_stage(stage, parts, images, near, member, tile, delta):
    return stage_call(
        first_kernel,
        stage,
        [
            jax.ShapeDtypeStruct((ROWS, 4 * LANES), bf16),
            jax.ShapeDtypeStruct((2 * ROWS, 2 * LANES), bf16),
        ],
        [pltpu.VMEM((ROWS, 4 * LANES), bf16)],
        (*parts, images, near, member, tile, delta),
        2 * 6 * (ITERS - 2) * ROWS * ROWS * LANES,
    )


def next_stage(stage, parts, column, window, tile, delta):
    tau = [jax.ShapeDtypeStruct((L2, LANES), f32)]
    return stage_call(
        next_kernel,
        stage,
        tau if any((0, 0) in group for group in stage) else [],
        [],
        (*parts, column, window, tile, delta),
        2 * ROWS * ROWS * LANES,
    )


def find_tile(groups, refs, ox, oy, oz):
    for group, ref in zip(groups, refs):
        if (ox, oy) in group:
            return ref[group.index((ox, oy)) * 5 + oz + 2]
    raise ValueError("no tile")


def plane_offsets():
    return [(ox, oy) for ox in (-1, 0, 1) for oy in (-1, 0, 1)]


def cell_of(dx, dy, dz):
    return ((dx + 1) * 3 + dy + 1) * 5 + dz + 2


def turn_kernel(groups, *refs):
    own, out = refs[:-1], refs[-1]
    lane = lane_index((L2, LANES))

    def cell_tile(cell):
        cell = min(cell, WINDOW - 1)
        return find_tile(groups, own, cell // 15 - 1, cell // 5 % 3 - 1, cell % 5 - 2)

    for base in range(0, WINDOW, DEPTH):
        block = jnp.concatenate([cell_tile(base + k) for k in range(DEPTH)], axis=0)
        turned = block.T
        pieces = [turned[s * L2 : (s + 1) * L2] for s in range(DEPTH)]
        for k in range(min(DEPTH, WINDOW - base)):
            value = pieces[0] if k == 0 else pltpu.roll(pieces[0], (-k % DEPTH) * L2, 1)
            for s in range(1, DEPTH):
                move = (s - k) % DEPTH
                piece = pieces[s] if move == 0 else pltpu.roll(pieces[s], move * L2, 1)
                value = jnp.where(lane // L2 == s, piece, value)
            out[base + k] = value


def turned_tiles(groups, own):
    return pl.pallas_call(
        functools.partial(turn_kernel, groups),
        out_shape=jax.ShapeDtypeStruct((WINDOW, L2, LANES), f32),
        in_specs=in_vmem(len(own)),
        out_specs=in_vmem(1)[0],
        compiler_params=pltpu.CompilerParams(vmem_limit_bytes=8 * MIB),
        cost_estimate=pl.CostEstimate(flops=MIB, bytes_accessed=2 * MIB, transcendentals=0),
        name="turned_tiles",
    )(*own)


def add_rows(groups, got, turned_ref, sums):
    for group, ref in zip(groups, got):
        for place, (ox, oy) in enumerate(group):
            for oz in range(-2, 3):
                cell = cell_of(-ox, -oy, -oz)
                value = ref[place * 5 + oz + 2] * turned_ref[cell]
                sums[cell : cell + 1, :] = jnp.sum(value, axis=0, keepdims=True)


def near_kernel(groups, *refs):
    got = refs[: len(groups)]
    turned_ref, tau_ref, sums, flat_ref = refs[len(groups) :]
    flat_kernel(tau_ref, flat_ref)
    sums[...] = jnp.zeros_like(sums)
    add_rows(groups, got, turned_ref, sums)


def near_sums(groups, got, turned, tau):
    return pl.pallas_call(
        functools.partial(near_kernel, groups),
        out_shape=(
            jax.ShapeDtypeStruct((SUM_ROWS, LANES), f32),
            jax.ShapeDtypeStruct((DEPTH, L2 * L2), f32),
        ),
        in_specs=in_vmem(len(got) + 2),
        out_specs=tuple(in_vmem(2)),
        compiler_params=pltpu.CompilerParams(vmem_limit_bytes=8 * MIB),
        name="near_sums",
    )(*got, turned, tau)


def total_kernel(groups, *refs):
    got = refs[: len(groups)]
    turned_ref, near_ref, out_ref, rows = refs[len(groups) :]
    rows[...] = near_ref[...]
    add_rows(groups, got, turned_ref, rows)
    sums = rows[...]
    site = lax.broadcasted_iota(jnp.int32, (8, LANES), 0)
    pick = (lane_index((8, LANES)) // L2 == site).astype(f32).astype(bf16)
    high = sums.astype(bf16)
    rest = sums - high.astype(f32)
    middle = rest.astype(bf16)
    low = (rest - middle.astype(f32)).astype(bf16)
    total = lax.dot_general(
        pick,
        jnp.concatenate([high, middle, low], axis=0),
        (((1,), (1,)), ((), ())),
        preferred_element_type=f32,
    )
    total = (total[:, :SUM_ROWS] + total[:, SUM_ROWS : 2 * SUM_ROWS]) + total[:, 2 * SUM_ROWS :]
    out_ref[...] = total[:DEPTH, :WINDOW]


def total_sums(groups, got, turned, near):
    return pl.pallas_call(
        functools.partial(total_kernel, groups),
        out_shape=jax.ShapeDtypeStruct((DEPTH, WINDOW), f32),
        in_specs=in_vmem(len(got) + 2),
        out_specs=in_vmem(1)[0],
        scratch_shapes=[pltpu.VMEM((SUM_ROWS, LANES), f32)],
        compiler_params=pltpu.CompilerParams(vmem_limit_bytes=8 * MIB),
        name="total_sums",
    )(*got, turned, near)


def plane_offsets():
    return [(ox, oy) for ox in (-1, 0, 1) for oy in (-1, 0, 1)]


def cell_of(dx, dy, dz):
    return ((dx + 1) * 3 + dy + 1) * 5 + dz + 2


def plane_groups():
    counts = (lax.axis_size("gx"), lax.axis_size("gy"))
    groups = {}
    for ox, oy in plane_offsets():
        groups.setdefault((ox % counts[0], oy % counts[1]), []).append((ox, oy))
    return groups


def body(t_matrix, structure, species, members, delta_table):
    own = packed_own(
        t_matrix.reshape(DEPTH, L2 * L2),
        members.reshape(DEPTH, WINDOW),
        species.reshape(1, DEPTH),
    )
    structure = structure[0]

    below, above = shifted(own, (0, 0, 1)), shifted(own, (0, 0, -1))
    first = split_piece(0, structure)
    slabs = jnp.stack([own[:L2], below[:L2], above[:L2]])
    slabs, structure, first = lax.optimization_barrier((slabs, structure, first))
    if lax.axis_size("gx") == 2:
        sides = [shifted(slabs, (1, 0, 0)), slabs]
    else:
        sides = [shifted(slabs, (1, 0, 0)), slabs, shifted(slabs, (-1, 0, 0))]
    second = split_piece(1, structure)
    plane = jnp.stack(sides)
    plane, structure, second = lax.optimization_barrier((plane, structure, second))
    planes = [shifted(plane, (0, 1, 0)), plane, shifted(plane, (0, -1, 0))]
    third = split_piece(2, structure)
    member, delta, tile = setup(own, below, above, delta_table)
    parts = (first, second, third)
    images = first_images(parts, tile)
    near = jnp.stack(planes)

    table = plane_groups()
    stages = [
        [shift for shift in table if shift[0] != 0 and shift[1] == 0],
        [shift for shift in table if shift[0] != 0 and shift[1] != 0],
        [shift for shift in table if shift[0] == 0],
    ]
    got, local = {}, {}
    for number, stage in enumerate(stages):
        groups = [table[shift] for shift in stage]
        if number == 0:
            *tiles, column, window = first_stage(groups, parts, images, near, member, tile, delta)
        else:
            tiles = next_stage(groups, parts, column, window, tile, delta)
        if (0, 0) in stage:
            tau = tiles[-1]
        local.update(zip(stage, tiles[len(stage) :]))
        for shift, block in zip(stage, tiles):
            got[shift] = block if shift == (0, 0) else shifted(block, shift + (0,))
    shifts = list(table)
    turned = turned_tiles([table[shift] for shift in shifts], [local[shift] for shift in shifts])
    close = stages[2]
    near_rows, site_tau = near_sums(
        [table[shift] for shift in close], [got[shift] for shift in close], turned, tau
    )
    far = stages[0] + stages[1]
    pairs = total_sums(
        [table[shift] for shift in far], [got[shift] for shift in far], turned, near_rows
    )
    return (
        site_tau.reshape(1, 1, 1, DEPTH, L2 * L2),
        pairs.reshape(1, 1, DEPTH, WINDOW),
    )


def solution(mesh):
    placed = (
        P(None, "gx", "gy", "gz", None),
        P(),
        P("gx", "gy", "gz"),
        P("gx", "gy", "gz", None),
        P(),
    )
    return jax.shard_map(
        body,
        mesh=mesh,
        in_specs=placed,
        out_specs=(P(None, "gx", "gy", "gz", None), P("gx", "gy", "gz", None)),
        check_vma=False,
    )
```

```python
import functools

import jax
import jax.numpy as jnp
import numpy as np
from jax import lax
from jax.experimental import pallas as pl
from jax.experimental.pallas import tpu as pltpu
from jax.sharding import PartitionSpec as P


L2 = 32
WINDOW = 45
ITERS = 4
SPECIES = 4
DEPTH = 4
LANES = DEPTH * L2
ROWS = WINDOW * L2
CENTRE = WINDOW // 2
SUM_ROWS = 48
PACK_ROWS = L2 + 8
PIECES = 3
PIECE = WINDOW // PIECES
PIECE_ROWS = PIECE * L2
SPLIT_STEPS = 3
CHUNK = 15
MESH_AXES = ("gx", "gy", "gz")


bf16 = jnp.bfloat16
f32 = jnp.float32
MIB = 1 << 20


def shifted(x, shift):
    sizes = [lax.axis_size(axis) for axis in MESH_AXES]
    pairs = []
    for source in np.ndindex(*sizes):
        target = [(i + d) % n for i, d, n in zip(source, shift, sizes)]
        pairs.append(
            (int(np.ravel_multi_index(source, sizes)), int(np.ravel_multi_index(target, sizes)))
        )
    return lax.ppermute(x, MESH_AXES, pairs)


def in_vmem(count):
    return [pl.BlockSpec(memory_space=pltpu.VMEM)] * count


def in_hbm(x):
    return pltpu.with_memory_space_constraint(x, pltpu.HBM)


def halves(x):
    high = x.astype(bf16)
    return high, (x - high.astype(f32)).astype(bf16)


def lane_index(shape):
    return lax.broadcasted_iota(jnp.int32, shape, len(shape) - 1)


def tile_kernel(flat_ref, tile_ref):
    row = lax.broadcasted_iota(jnp.int32, (DEPTH, LANES), 0)
    diagonal = lane_index((DEPTH, LANES)) // L2 == row
    for j in range(L2 // DEPTH):
        part = flat_ref[:, j * LANES : (j + 1) * LANES]
        rolled = [part] + [pltpu.roll(part, m * L2, 1) for m in range(1, DEPTH)]
        for k in range(DEPTH):
            picked = jnp.zeros((DEPTH, LANES), f32)
            for m in range(DEPTH):
                picked = jnp.where(diagonal & (row == (m + k) % DEPTH), rolled[m], picked)
            a = j * DEPTH + k
            tile_ref[a : a + 1, :] = jnp.sum(picked, axis=0, keepdims=True)


def flat_kernel(tile_ref, flat_ref):
    row = lax.broadcasted_iota(jnp.int32, (DEPTH, LANES), 0)
    diagonal = lane_index((DEPTH, LANES)) // L2 == row
    for j in range(L2 // DEPTH):
        spread = []
        for k in range(DEPTH):
            a = j * DEPTH + k
            line = jnp.broadcast_to(tile_ref[a : a + 1, :], (DEPTH, LANES))
            spread.append(jnp.where(diagonal, line, 0.0))
        value = jnp.zeros((DEPTH, LANES), f32)
        for m in range(DEPTH):
            picked = jnp.zeros((DEPTH, LANES), f32)
            for k in range(DEPTH):
                picked = jnp.where(row == (k - m) % DEPTH, spread[k], picked)
            value = value + (picked if m == 0 else pltpu.roll(picked, m * L2, 1))
        flat_ref[:, j * LANES : (j + 1) * LANES] = value


def pack_kernel(flat_hbm, members_hbm, species_hbm, pack_ref, flat_ref, members_ref, species_ref, sems):
    moves = [(flat_hbm, flat_ref), (members_hbm, members_ref), (species_hbm, species_ref)]
    copies = [
        pltpu.make_async_copy(source, target, sems.at[i])
        for i, (source, target) in enumerate(moves)
    ]
    for copy in copies:
        copy.start()
    for copy in copies:
        copy.wait()
    tile_kernel(flat_ref, pack_ref)
    pack_ref[L2:, :] = jnp.full((PACK_ROWS - L2, LANES), -1.0, f32)
    pack_ref[L2 : L2 + DEPTH, :WINDOW] = members_ref[...].astype(f32)
    pack_ref[L2 + DEPTH : L2 + DEPTH + 1, :DEPTH] = species_ref[...].astype(f32)


def packed_own(flat, members, species):
    return pl.pallas_call(
        pack_kernel,
        out_shape=jax.ShapeDtypeStruct((PACK_ROWS, LANES), f32),
        in_specs=[pl.BlockSpec(memory_space=pltpu.HBM)] * 3,
        out_specs=in_vmem(1)[0],
        scratch_shapes=[
            pltpu.VMEM((DEPTH, L2 * L2), f32),
            pltpu.VMEM((DEPTH, WINDOW), jnp.int32),
            pltpu.VMEM((1, DEPTH), jnp.int32),
            pltpu.SemaphoreType.DMA((3,)),
        ],
        compiler_params=pltpu.CompilerParams(vmem_limit_bytes=4 * MIB),
        name="packed_own",
    )(in_hbm(flat), in_hbm(members), in_hbm(species))


def split_kernel(piece, structure_hbm, parts_ref, buffer, sems):
    step_rows = PIECE_ROWS // SPLIT_STEPS

    def fetch(step):
        rows = pl.ds(piece * PIECE_ROWS + step * step_rows, step_rows)
        return pltpu.make_async_copy(structure_hbm.at[rows, :], buffer.at[step], sems.at[step])

    for step in range(SPLIT_STEPS):
        fetch(step).start()
    half = L2 // 2
    for step in range(SPLIT_STEPS):
        fetch(step).wait()

        def half_cell(i, carry, step=step):
            source = pl.ds(pl.multiple_of(i * half, half), half)
            target = step * 2 * step_rows + i // 2 * 2 * L2 + i % 2 * half
            high, low = halves(buffer[step, source, :])
            parts_ref[pl.ds(pl.multiple_of(target, half), half), :] = high
            parts_ref[pl.ds(pl.multiple_of(target + L2, half), half), :] = low
            return carry

        lax.fori_loop(0, step_rows // half, half_cell, 0, unroll=2)


def split_piece(piece, structure):
    return pl.pallas_call(
        functools.partial(split_kernel, piece),
        out_shape=jax.ShapeDtypeStruct((2 * PIECE_ROWS, ROWS), bf16),
        in_specs=[pl.BlockSpec(memory_space=pltpu.HBM)],
        out_specs=in_vmem(1)[0],
        scratch_shapes=[
            pltpu.VMEM((SPLIT_STEPS, PIECE_ROWS // SPLIT_STEPS, ROWS), f32),
            pltpu.SemaphoreType.DMA((SPLIT_STEPS,)),
        ],
        compiler_params=pltpu.CompilerParams(vmem_limit_bytes=8 * MIB),
        cost_estimate=pl.CostEstimate(
            flops=MIB, bytes_accessed=4 * PIECE_ROWS * ROWS, transcendentals=0
        ),
        name="split_piece",
    )(in_hbm(structure))


def both_tiles(own, below, above):
    lane = lane_index(own.shape)
    return [own, jnp.where(lane < 2 * L2, above, below)]


def setup_kernel(own_ref, below_ref, above_ref, table_hbm, member_ref, delta_ref, tile_ref, *rest):
    table_ref, table_tile, sem = rest
    copy = pltpu.make_async_copy(table_hbm, table_ref, sem.at[0])
    copy.start()
    cells = lax.broadcasted_iota(jnp.int32, (WINDOW, LANES), 0).astype(f32)
    group = lane_index((WINDOW, LANES)) // L2
    sources = [[own_ref] * DEPTH, [above_ref, above_ref, below_ref, below_ref]]
    for half, refs in enumerate(sources):
        member = jnp.zeros((WINDOW, LANES), f32)
        for g, ref in enumerate(refs):
            found = (ref[L2 + g : L2 + g + 1, :] == cells).astype(f32)
            found = jnp.max(found, axis=1, keepdims=True)
            member = jnp.where(group == g, found, member)
        member_ref[:, half * LANES : (half + 1) * LANES] = member
    tiles = both_tiles(own_ref[:L2, :], below_ref[:L2, :], above_ref[:L2, :])
    for half, tile in enumerate(tiles):
        tile_ref[:, half * LANES : (half + 1) * LANES] = tile

    copy.wait()
    tile_kernel(table_ref, table_tile)
    table = table_tile[...]
    turns = [table] + [pltpu.roll(table, m * L2, 1) for m in range(1, SPECIES)]
    group = lane_index((L2, LANES)) // L2
    thin = lane_index((1, LANES))
    row = slice(L2 + DEPTH, L2 + DEPTH + 1)
    for half, refs in enumerate(sources):
        delta = jnp.zeros((L2, LANES), f32)
        for g, ref in enumerate(refs):
            kinds = jnp.max(jnp.where(thin == g, ref[row, :], -1.0), axis=1, keepdims=True)
            for kind in range(SPECIES):
                here = (group == g) & (kinds == kind)
                delta = jnp.where(here, turns[(g - kind) % SPECIES], delta)
        delta_ref[:, half * LANES : (half + 1) * LANES] = delta


def setup(own, below, above, table):
    return pl.pallas_call(
        setup_kernel,
        out_shape=(
            jax.ShapeDtypeStruct((WINDOW, 2 * LANES), f32),
            jax.ShapeDtypeStruct((L2, 2 * LANES), f32),
            jax.ShapeDtypeStruct((L2, 2 * LANES), f32),
        ),
        in_specs=in_vmem(3) + [pl.BlockSpec(memory_space=pltpu.HBM)],
        out_specs=tuple(in_vmem(3)),
        scratch_shapes=[
            pltpu.VMEM((SPECIES, L2 * L2), f32),
            pltpu.VMEM((L2, LANES), f32),
            pltpu.SemaphoreType.DMA((1,)),
        ],
        compiler_params=pltpu.CompilerParams(vmem_limit_bytes=4 * MIB),
        name="setup",
    )(own, below, above, in_hbm(table))


def four_products(product):
    parts = product.reshape(-1, 2, L2, 2 * LANES)
    high, low = parts[:, 0], parts[:, 1]
    return (high[..., :LANES] + high[..., LANES:]) + (low[..., :LANES] + low[..., LANES:])


def first_image_kernel(*refs):
    parts, (tile_ref, image_ref) = refs[:PIECES], refs[PIECES:]
    lane_tile = CENTRE * L2 // LANES * LANES
    before = CENTRE * L2 - lane_tile
    for half in range(2):
        lanes = slice(half * LANES, (half + 1) * LANES)
        right = jnp.concatenate(halves(tile_ref[:, lanes]), axis=1)
        right = jnp.concatenate(
            [
                jnp.zeros((before, 2 * LANES), bf16),
                right,
                jnp.zeros((LANES - before - L2, 2 * LANES), bf16),
            ],
            axis=0,
        )
        for piece, ref in enumerate(parts):
            left = ref[:, lane_tile : lane_tile + LANES]
            product = jnp.dot(left, right, preferred_element_type=f32)
            image_ref[piece * PIECE : (piece + 1) * PIECE, :, lanes] = four_products(product)


def first_images(parts, tile):
    return pl.pallas_call(
        first_image_kernel,
        out_shape=jax.ShapeDtypeStruct((WINDOW, L2, 2 * LANES), f32),
        in_specs=in_vmem(PIECES + 1),
        out_specs=in_vmem(1)[0],
        compiler_params=pltpu.CompilerParams(vmem_limit_bytes=8 * MIB),
        name="first_images",
    )(*parts, tile)


def site_blocks(tile):
    lane = lane_index((L2, LANES))
    masks = [(lane // L2 == s).astype(f32).astype(bf16) for s in range(DEPTH)]
    return jnp.concatenate([tile * mask for mask in masks], axis=0)


def moved(window, cell, half, image):
    blocks = jnp.concatenate([site_blocks(part) for part in halves(image)], axis=1)
    left = window[cell * 2 * L2 : (cell + 1) * 2 * L2, half * LANES : (half + 1) * LANES]
    return four_products(jnp.dot(left, blocks, preferred_element_type=f32))[0]


HIGH_AT = (1, 2)
LOW_AT = (0, 3)


def keep(column, place, half, value):
    rows = slice(place * L2, (place + 1) * L2)
    for at, part in zip((HIGH_AT[half], LOW_AT[half]), halves(value)):
        column[rows, at * LANES : (at + 1) * LANES] = part


def set_images(parts, cells, column, slot):
    high, low = [], []
    for cell in cells:
        ref, base = parts[cell // PIECE], cell % PIECE * 2 * L2
        high.append(ref[base : base + L2, :])
        low.append(ref[base + L2 : base + 2 * L2, :])
    high, low = jnp.concatenate(high, axis=0), jnp.concatenate(low, axis=0)
    own = jnp.dot(high, column[:, : 2 * LANES], preferred_element_type=f32)
    other = jnp.dot(high, column[:, 2 * LANES :], preferred_element_type=f32)
    both = jnp.dot(low, column[:, LANES : 3 * LANES], preferred_element_type=f32)
    shape = (len(cells), L2, LANES)
    image = own[:, :LANES] + own[:, LANES:] + both[:, :LANES]
    slot[: len(cells), :, :LANES] = image.reshape(shape)
    image = other[:, :LANES] + other[:, LANES:] + both[:, LANES:]
    slot[: len(cells), :, LANES:] = image.reshape(shape)


def window_tiles(near, cell):
    dx, dy, dz = cell // 15, cell // 5 % 3, cell % 5 - 2
    own, below, above = (near(dx, dy, i) for i in range(3))
    group = lane_index((L2, LANES)) // L2
    first, second = own, jnp.where(group < 2, above, below)
    if dz > 0:
        first = jnp.where(group < dz, above, own)
        second = jnp.where(group < dz, own, jnp.where(group < 2 + dz, above, below))
    elif dz < 0:
        first = jnp.where(group >= DEPTH + dz, below, own)
        second = jnp.where(group >= DEPTH + dz, own, jnp.where(group < 2 + dz, above, below))
    move = -dz % DEPTH * L2
    return [tile if move == 0 else pltpu.roll(tile, move, 1) for tile in (first, second)]


def set_window(window, near, member_ref, cell):
    base = cell * 2 * L2
    for half, tile in enumerate(window_tiles(near, cell)):
        lanes = slice(half * LANES, (half + 1) * LANES)
        high, low = halves(tile * member_ref[cell : cell + 1, lanes])
        window[base : base + L2, lanes] = high
        window[base + L2 : base + 2 * L2, lanes] = low


def set_column(column, window, tile_ref, cell, image):
    for half in range(2):
        lanes = slice(half * LANES, (half + 1) * LANES)
        value = moved(window, cell, half, image[:, lanes])
        if cell == CENTRE:
            value = value + tile_ref[:, lanes]
        keep(column, cell, half, value)


def early_cells():
    return [cell for cell in range(WINDOW) if cell // 5 % 3 == 1]


def early_kernel(plane_ref, member_ref, tile_ref, image_ref, column, window):
    def near(dx, dy, slab):
        return plane_ref[dx % plane_ref.shape[0], slab]

    for cell in early_cells():
        set_window(window, near, member_ref, cell)
    for cell in early_cells():
        set_column(column, window, tile_ref, cell, image_ref[cell])


def early_columns(plane, member, tile, images):
    return pl.pallas_call(
        early_kernel,
        out_shape=(
            jax.ShapeDtypeStruct((ROWS, 4 * LANES), bf16),
            jax.ShapeDtypeStruct((2 * ROWS, 2 * LANES), bf16),
        ),
        in_specs=in_vmem(4),
        out_specs=tuple(in_vmem(2)),
        compiler_params=pltpu.CompilerParams(vmem_limit_bytes=8 * MIB),
        name="early_columns",
    )(plane, member, tile, images)


def sweep_over(parts, chunks, source, use_image, slots):
    for i, chunk in enumerate(chunks):
        set_images(parts, chunk, source, slots[i % 2])
        if i > 0:
            use_image(i - 1, slots[(i - 1) % 2])
    use_image(len(chunks) - 1, slots[(len(chunks) - 1) % 2])


def delta_blocks(tile):
    high, low = (site_blocks(part) for part in halves(tile))
    return jnp.concatenate(
        [
            jnp.concatenate([high, low], axis=1),
            jnp.concatenate([high, jnp.zeros_like(high)], axis=1),
        ],
        axis=0,
    )


def last_sweep(parts, column, window, tile_ref, delta_ref, stage, sent, local, tau_ref, slots, final):
    deltas = [delta_blocks(delta_ref[:, half * LANES : (half + 1) * LANES]) for half in range(2)]
    chunks = [[cell_of(ox, oy, oz) for ox, oy in group for oz in range(-2, 3)] for group in stage]
    group_of = lane_index((L2, LANES)) // L2

    def use_image(i, slot):
        count = len(chunks[i])
        values = []
        for half in range(2):
            lanes = slice(half * LANES, (half + 1) * LANES)
            for place, cell in enumerate(chunks[i]):
                value = moved(window, cell, half, slot[place, :, lanes])
                if cell == CENTRE:
                    value = value + tile_ref[:, lanes]
                    if half == 0:
                        tau_ref[...] = value
                rows = slice(place * L2, (place + 1) * L2)
                high, low = halves(value)
                final[half, rows, :LANES] = high
                final[half, rows, LANES:] = low
            product = jnp.dot(
                final[half, : count * L2, :], deltas[half], preferred_element_type=f32
            )
            product = product[:, :LANES] + product[:, LANES:]
            values.append(product.reshape(count, L2, LANES))
        local[i][...] = values[0]
        for place, cell in enumerate(chunks[i]):
            oz = cell % 5 - 2
            value = values[0][place]
            if oz > 0:
                value = jnp.where(group_of >= DEPTH - oz, values[1][place], value)
            elif oz < 0:
                value = jnp.where(group_of < -oz, values[1][place], value)
            if oz != 0:
                value = pltpu.roll(value, oz % DEPTH * L2, 1)
            sent[i][place] = value

    sweep_over(parts, chunks, column, use_image, slots)


def first_kernel(stage, *refs):
    parts, refs = refs[:PIECES], refs[PIECES:]
    _, _, image_ref, south_ref, north_ref, member_ref, tile_ref, delta_ref = refs[:8]
    sent, local = refs[8 : 8 + len(stage)], refs[8 + len(stage) : 8 + 2 * len(stage)]
    column, window, other, slot_a, slot_b, final = refs[8 + 2 * len(stage) :]
    slots = (slot_a, slot_b)

    def near(dx, dy, slab):
        ref = south_ref if dy == 0 else north_ref
        return ref[dx % ref.shape[0], slab]

    late = [cell for cell in range(WINDOW) if cell not in early_cells()]
    for cell in late:
        set_window(window, near, member_ref, cell)
    for cell in late:
        set_column(column, window, tile_ref, cell, image_ref[cell])
    source, target = column, other
    full = [list(range(base, base + CHUNK)) for base in range(0, WINDOW, CHUNK)]
    for _ in range(1, ITERS - 1):

        def use_image(i, slot, target=target):
            for place, cell in enumerate(full[i]):
                set_column(target, window, tile_ref, cell, slot[place])

        sweep_over(parts, full, source, use_image, slots)
        source, target = target, source
    if source is not column:
        column[...] = source[...]
    last_sweep(
        parts, column, window, tile_ref, delta_ref, stage, sent, local, None, slots, final
    )


def next_kernel(stage, *refs):
    parts, refs = refs[:PIECES], refs[PIECES:]
    column, window, tile_ref, delta_ref = refs[:4]
    sent, local = refs[4 : 4 + len(stage)], refs[4 + len(stage) : 4 + 2 * len(stage)]
    rest = refs[4 + 2 * len(stage) :]
    tau_ref = rest[0] if len(rest) == 4 else None
    slot_a, slot_b, final = rest[-3:]
    last_sweep(
        parts,
        column,
        window,
        tile_ref,
        delta_ref,
        stage,
        sent,
        local,
        tau_ref,
        (slot_a, slot_b),
        final,
    )


def stage_call(kernel, stage, extra_outs, extra_scratch, operands, flops, aliases=()):
    longest = max(CHUNK, 5 * max(len(group) for group in stage))
    out_shape = [jax.ShapeDtypeStruct((5 * len(group), L2, LANES), f32) for group in stage] * 2
    out_shape += extra_outs
    return pl.pallas_call(
        functools.partial(kernel, stage),
        out_shape=tuple(out_shape),
        in_specs=in_vmem(len(operands)),
        out_specs=tuple(in_vmem(len(out_shape))),
        scratch_shapes=extra_scratch
        + [pltpu.VMEM((longest, L2, 2 * LANES), f32)] * 2
        + [pltpu.VMEM((2, longest * L2, 2 * LANES), bf16)],
        input_output_aliases={
            operand: 2 * len(stage) + i for i, operand in enumerate(aliases)
        },
        compiler_params=pltpu.CompilerParams(vmem_limit_bytes=24 * MIB),
        cost_estimate=pl.CostEstimate(flops=flops, bytes_accessed=MIB, transcendentals=0),
    )(*operands)


def first_stage(stage, parts, column, window, images, south, north, member, tile, delta):
    return stage_call(
        first_kernel,
        stage,
        [
            jax.ShapeDtypeStruct((ROWS, 4 * LANES), bf16),
            jax.ShapeDtypeStruct((2 * ROWS, 2 * LANES), bf16),
        ],
        [pltpu.VMEM((ROWS, 4 * LANES), bf16)],
        (*parts, column, window, images, south, north, member, tile, delta),
        2 * 6 * (ITERS - 2) * ROWS * ROWS * LANES,
        (PIECES, PIECES + 1),
    )


def next_stage(stage, parts, column, window, tile, delta):
    tau = [jax.ShapeDtypeStruct((L2, LANES), f32)]
    return stage_call(
        next_kernel,
        stage,
        tau if any((0, 0) in group for group in stage) else [],
        [],
        (*parts, column, window, tile, delta),
        2 * ROWS * ROWS * LANES,
    )


def find_tile(groups, refs, ox, oy, oz):
    for group, ref in zip(groups, refs):
        if (ox, oy) in group:
            return ref[group.index((ox, oy)) * 5 + oz + 2]
    raise ValueError("no tile")


def plane_offsets():
    return [(ox, oy) for ox in (-1, 0, 1) for oy in (-1, 0, 1)]


def cell_of(dx, dy, dz):
    return ((dx + 1) * 3 + dy + 1) * 5 + dz + 2


def turn_kernel(groups, *refs):
    own, out = refs[:-1], refs[-1]
    lane = lane_index((L2, LANES))

    def cell_tile(cell):
        cell = min(cell, WINDOW - 1)
        return find_tile(groups, own, cell // 15 - 1, cell // 5 % 3 - 1, cell % 5 - 2)

    for base in range(0, WINDOW, DEPTH):
        block = jnp.concatenate([cell_tile(base + k) for k in range(DEPTH)], axis=0)
        turned = block.T
        pieces = [turned[s * L2 : (s + 1) * L2] for s in range(DEPTH)]
        for k in range(min(DEPTH, WINDOW - base)):
            value = pieces[0] if k == 0 else pltpu.roll(pieces[0], (-k % DEPTH) * L2, 1)
            for s in range(1, DEPTH):
                move = (s - k) % DEPTH
                piece = pieces[s] if move == 0 else pltpu.roll(pieces[s], move * L2, 1)
                value = jnp.where(lane // L2 == s, piece, value)
            out[base + k] = value


def turned_tiles(groups, own):
    return pl.pallas_call(
        functools.partial(turn_kernel, groups),
        out_shape=jax.ShapeDtypeStruct((WINDOW, L2, LANES), f32),
        in_specs=in_vmem(len(own)),
        out_specs=in_vmem(1)[0],
        compiler_params=pltpu.CompilerParams(vmem_limit_bytes=8 * MIB),
        cost_estimate=pl.CostEstimate(flops=MIB, bytes_accessed=2 * MIB, transcendentals=0),
        name="turned_tiles",
    )(*own)


def add_rows(groups, got, turned_ref, sums):
    for group, ref in zip(groups, got):
        for place, (ox, oy) in enumerate(group):
            for oz in range(-2, 3):
                cell = cell_of(-ox, -oy, -oz)
                value = ref[place * 5 + oz + 2] * turned_ref[cell]
                sums[cell : cell + 1, :] = jnp.sum(value, axis=0, keepdims=True)


def near_kernel(groups, *refs):
    got = refs[: len(groups)]
    turned_ref, tau_ref, sums, flat_ref = refs[len(groups) :]
    flat_kernel(tau_ref, flat_ref)
    sums[...] = jnp.zeros_like(sums)
    add_rows(groups, got, turned_ref, sums)


def near_sums(groups, got, turned, tau):
    return pl.pallas_call(
        functools.partial(near_kernel, groups),
        out_shape=(
            jax.ShapeDtypeStruct((SUM_ROWS, LANES), f32),
            jax.ShapeDtypeStruct((DEPTH, L2 * L2), f32),
        ),
        in_specs=in_vmem(len(got) + 2),
        out_specs=tuple(in_vmem(2)),
        compiler_params=pltpu.CompilerParams(vmem_limit_bytes=8 * MIB),
        name="near_sums",
    )(*got, turned, tau)


def total_kernel(groups, *refs):
    got = refs[: len(groups)]
    turned_ref, near_ref, out_ref, rows = refs[len(groups) :]
    rows[...] = near_ref[...]
    add_rows(groups, got, turned_ref, rows)
    sums = rows[...]
    site = lax.broadcasted_iota(jnp.int32, (8, LANES), 0)
    pick = (lane_index((8, LANES)) // L2 == site).astype(f32).astype(bf16)
    high = sums.astype(bf16)
    rest = sums - high.astype(f32)
    middle = rest.astype(bf16)
    low = (rest - middle.astype(f32)).astype(bf16)
    total = lax.dot_general(
        pick,
        jnp.concatenate([high, middle, low], axis=0),
        (((1,), (1,)), ((), ())),
        preferred_element_type=f32,
    )
    total = (total[:, :SUM_ROWS] + total[:, SUM_ROWS : 2 * SUM_ROWS]) + total[:, 2 * SUM_ROWS :]
    out_ref[...] = total[:DEPTH, :WINDOW]


def total_sums(groups, got, turned, near):
    return pl.pallas_call(
        functools.partial(total_kernel, groups),
        out_shape=jax.ShapeDtypeStruct((DEPTH, WINDOW), f32),
        in_specs=in_vmem(len(got) + 2),
        out_specs=in_vmem(1)[0],
        scratch_shapes=[pltpu.VMEM((SUM_ROWS, LANES), f32)],
        compiler_params=pltpu.CompilerParams(vmem_limit_bytes=8 * MIB),
        name="total_sums",
    )(*got, turned, near)


def plane_offsets():
    return [(ox, oy) for ox in (-1, 0, 1) for oy in (-1, 0, 1)]


def cell_of(dx, dy, dz):
    return ((dx + 1) * 3 + dy + 1) * 5 + dz + 2


def plane_groups():
    counts = (lax.axis_size("gx"), lax.axis_size("gy"))
    groups = {}
    for ox, oy in plane_offsets():
        groups.setdefault((ox % counts[0], oy % counts[1]), []).append((ox, oy))
    return groups


def body(t_matrix, structure, species, members, delta_table):
    own = packed_own(
        t_matrix.reshape(DEPTH, L2 * L2),
        members.reshape(DEPTH, WINDOW),
        species.reshape(1, DEPTH),
    )
    structure = structure[0]

    below, above = shifted(own, (0, 0, 1)), shifted(own, (0, 0, -1))
    first, second = split_piece(0, structure), split_piece(1, structure)
    slabs = jnp.stack([own[:L2], below[:L2], above[:L2]])
    slabs, structure, first, second = lax.optimization_barrier((slabs, structure, first, second))
    if lax.axis_size("gx") == 2:
        sides = [shifted(slabs, (1, 0, 0)), slabs]
    else:
        sides = [shifted(slabs, (1, 0, 0)), slabs, shifted(slabs, (-1, 0, 0))]
    prepared = setup(own, below, above, delta_table)
    plane = jnp.stack(sides)
    plane, structure, *prepared = lax.optimization_barrier((plane, structure, *prepared))
    member, delta, tile = prepared
    south, north = shifted(plane, (0, 1, 0)), shifted(plane, (0, -1, 0))
    parts = (first, second, split_piece(2, structure))
    images = first_images(parts, tile)
    column, window = early_columns(plane, member, tile, images)

    table = plane_groups()
    stages = [
        [shift for shift in table if shift[0] != 0 and shift[1] != 0],
        [shift for shift in table if shift[0] != 0 and shift[1] == 0],
        [shift for shift in table if shift[0] == 0 and shift[1] != 0],
        [(0, 0)],
    ]
    got, local = {}, {}
    for number, stage in enumerate(stages):
        groups = [table[shift] for shift in stage]
        if number == 0:
            *tiles, column, window = first_stage(
                groups, parts, column, window, images, south, north, member, tile, delta
            )
        else:
            tiles = next_stage(groups, parts, column, window, tile, delta)
        if (0, 0) in stage:
            tau = tiles[-1]
        local.update(zip(stage, tiles[len(stage) :]))
        for shift, block in zip(stage, tiles):
            got[shift] = block if shift == (0, 0) else shifted(block, shift + (0,))
    shifts = list(table)
    turned = turned_tiles([table[shift] for shift in shifts], [local[shift] for shift in shifts])
    near_rows, site_tau = near_sums([table[0, 0]], [got[0, 0]], turned, tau)
    far = [shift for shift in shifts if shift != (0, 0)]
    pairs = total_sums(
        [table[shift] for shift in far], [got[shift] for shift in far], turned, near_rows
    )
    return (
        site_tau.reshape(1, 1, 1, DEPTH, L2 * L2),
        pairs.reshape(1, 1, DEPTH, WINDOW),
    )


def solution(mesh):
    placed = (
        P(None, "gx", "gy", "gz", None),
        P(),
        P("gx", "gy", "gz"),
        P("gx", "gy", "gz", None),
        P(),
    )
    return jax.shard_map(
        body,
        mesh=mesh,
        in_specs=placed,
        out_specs=(P(None, "gx", "gy", "gz", None), P("gx", "gy", "gz", None)),
        check_vma=False,
    )
```

```python
import functools

import jax
import jax.numpy as jnp
import numpy as np
from jax import lax
from jax.experimental import pallas as pl
from jax.experimental.pallas import tpu as pltpu
from jax.sharding import PartitionSpec as P


L2 = 32
WINDOW = 45
ITERS = 4
SPECIES = 4
DEPTH = 4
LANES = DEPTH * L2
ROWS = WINDOW * L2
CENTRE = WINDOW // 2
SUM_ROWS = 48
PACK_ROWS = L2 + 8
PIECES = 3
PIECE = WINDOW // PIECES
PIECE_ROWS = PIECE * L2
SPLIT_STEPS = 3
CHUNK = 23
MESH_AXES = ("gx", "gy", "gz")


bf16 = jnp.bfloat16
f32 = jnp.float32
MIB = 1 << 20


def shifted(x, shift):
    sizes = [lax.axis_size(axis) for axis in MESH_AXES]
    pairs = []
    for source in np.ndindex(*sizes):
        target = [(i + d) % n for i, d, n in zip(source, shift, sizes)]
        pairs.append(
            (int(np.ravel_multi_index(source, sizes)), int(np.ravel_multi_index(target, sizes)))
        )
    return lax.ppermute(x, MESH_AXES, pairs)


def in_vmem(count):
    return [pl.BlockSpec(memory_space=pltpu.VMEM)] * count


def in_hbm(x):
    return pltpu.with_memory_space_constraint(x, pltpu.HBM)


def halves(x):
    high = x.astype(bf16)
    return high, (x - high.astype(f32)).astype(bf16)


def lane_index(shape):
    return lax.broadcasted_iota(jnp.int32, shape, len(shape) - 1)


def tile_kernel(flat_ref, tile_ref):
    row = lax.broadcasted_iota(jnp.int32, (DEPTH, LANES), 0)
    diagonal = lane_index((DEPTH, LANES)) // L2 == row
    for j in range(L2 // DEPTH):
        part = flat_ref[:, j * LANES : (j + 1) * LANES]
        rolled = [part] + [pltpu.roll(part, m * L2, 1) for m in range(1, DEPTH)]
        for k in range(DEPTH):
            picked = jnp.zeros((DEPTH, LANES), f32)
            for m in range(DEPTH):
                picked = jnp.where(diagonal & (row == (m + k) % DEPTH), rolled[m], picked)
            a = j * DEPTH + k
            tile_ref[a : a + 1, :] = jnp.sum(picked, axis=0, keepdims=True)


def flat_kernel(tile_ref, flat_ref):
    row = lax.broadcasted_iota(jnp.int32, (DEPTH, LANES), 0)
    diagonal = lane_index((DEPTH, LANES)) // L2 == row
    for j in range(L2 // DEPTH):
        spread = []
        for k in range(DEPTH):
            a = j * DEPTH + k
            line = jnp.broadcast_to(tile_ref[a : a + 1, :], (DEPTH, LANES))
            spread.append(jnp.where(diagonal, line, 0.0))
        value = jnp.zeros((DEPTH, LANES), f32)
        for m in range(DEPTH):
            picked = jnp.zeros((DEPTH, LANES), f32)
            for k in range(DEPTH):
                picked = jnp.where(row == (k - m) % DEPTH, spread[k], picked)
            value = value + (picked if m == 0 else pltpu.roll(picked, m * L2, 1))
        flat_ref[:, j * LANES : (j + 1) * LANES] = value


def pack_kernel(flat_hbm, members_hbm, species_hbm, pack_ref, flat_ref, members_ref, species_ref, sems):
    moves = [(flat_hbm, flat_ref), (members_hbm, members_ref), (species_hbm, species_ref)]
    copies = [
        pltpu.make_async_copy(source, target, sems.at[i])
        for i, (source, target) in enumerate(moves)
    ]
    for copy in copies:
        copy.start()
    for copy in copies:
        copy.wait()
    tile_kernel(flat_ref, pack_ref)
    pack_ref[L2:, :] = jnp.full((PACK_ROWS - L2, LANES), -1.0, f32)
    pack_ref[L2 : L2 + DEPTH, :WINDOW] = members_ref[...].astype(f32)
    pack_ref[L2 + DEPTH : L2 + DEPTH + 1, :DEPTH] = species_ref[...].astype(f32)


def packed_own(flat, members, species):
    return pl.pallas_call(
        pack_kernel,
        out_shape=jax.ShapeDtypeStruct((PACK_ROWS, LANES), f32),
        in_specs=[pl.BlockSpec(memory_space=pltpu.HBM)] * 3,
        out_specs=in_vmem(1)[0],
        scratch_shapes=[
            pltpu.VMEM((DEPTH, L2 * L2), f32),
            pltpu.VMEM((DEPTH, WINDOW), jnp.int32),
            pltpu.VMEM((1, DEPTH), jnp.int32),
            pltpu.SemaphoreType.DMA((3,)),
        ],
        compiler_params=pltpu.CompilerParams(vmem_limit_bytes=4 * MIB),
        name="packed_own",
    )(in_hbm(flat), in_hbm(members), in_hbm(species))


def split_kernel(piece, structure_hbm, parts_ref, buffer, sems):
    step_rows = PIECE_ROWS // SPLIT_STEPS

    def fetch(step):
        rows = pl.ds(piece * PIECE_ROWS + step * step_rows, step_rows)
        return pltpu.make_async_copy(structure_hbm.at[rows, :], buffer.at[step], sems.at[step])

    for step in range(SPLIT_STEPS):
        fetch(step).start()
    half = L2 // 2
    for step in range(SPLIT_STEPS):
        fetch(step).wait()

        def half_cell(i, carry, step=step):
            source = pl.ds(pl.multiple_of(i * half, half), half)
            target = step * 2 * step_rows + i // 2 * 2 * L2 + i % 2 * half
            high, low = halves(buffer[step, source, :])
            parts_ref[pl.ds(pl.multiple_of(target, half), half), :] = high
            parts_ref[pl.ds(pl.multiple_of(target + L2, half), half), :] = low
            return carry

        lax.fori_loop(0, step_rows // half, half_cell, 0, unroll=2)


def split_piece(piece, structure):
    return pl.pallas_call(
        functools.partial(split_kernel, piece),
        out_shape=jax.ShapeDtypeStruct((2 * PIECE_ROWS, ROWS), bf16),
        in_specs=[pl.BlockSpec(memory_space=pltpu.HBM)],
        out_specs=in_vmem(1)[0],
        scratch_shapes=[
            pltpu.VMEM((SPLIT_STEPS, PIECE_ROWS // SPLIT_STEPS, ROWS), f32),
            pltpu.SemaphoreType.DMA((SPLIT_STEPS,)),
        ],
        compiler_params=pltpu.CompilerParams(vmem_limit_bytes=8 * MIB),
        cost_estimate=pl.CostEstimate(
            flops=MIB, bytes_accessed=4 * PIECE_ROWS * ROWS, transcendentals=0
        ),
        name="split_piece",
    )(in_hbm(structure))


def both_tiles(own, below, above):
    lane = lane_index(own.shape)
    return [own, jnp.where(lane < 2 * L2, above, below)]


def setup_kernel(own_ref, below_ref, above_ref, table_hbm, member_ref, delta_ref, tile_ref, *rest):
    table_ref, table_tile, sem = rest
    copy = pltpu.make_async_copy(table_hbm, table_ref, sem.at[0])
    copy.start()
    cells = lax.broadcasted_iota(jnp.int32, (WINDOW, LANES), 0).astype(f32)
    group = lane_index((WINDOW, LANES)) // L2
    sources = [[own_ref] * DEPTH, [above_ref, above_ref, below_ref, below_ref]]
    for half, refs in enumerate(sources):
        member = jnp.zeros((WINDOW, LANES), f32)
        for g, ref in enumerate(refs):
            found = (ref[L2 + g : L2 + g + 1, :] == cells).astype(f32)
            found = jnp.max(found, axis=1, keepdims=True)
            member = jnp.where(group == g, found, member)
        member_ref[:, half * LANES : (half + 1) * LANES] = member
    tiles = both_tiles(own_ref[:L2, :], below_ref[:L2, :], above_ref[:L2, :])
    for half, tile in enumerate(tiles):
        tile_ref[:, half * LANES : (half + 1) * LANES] = tile

    copy.wait()
    tile_kernel(table_ref, table_tile)
    table = table_tile[...]
    turns = [table] + [pltpu.roll(table, m * L2, 1) for m in range(1, SPECIES)]
    group = lane_index((L2, LANES)) // L2
    thin = lane_index((1, LANES))
    row = slice(L2 + DEPTH, L2 + DEPTH + 1)
    for half, refs in enumerate(sources):
        delta = jnp.zeros((L2, LANES), f32)
        for g, ref in enumerate(refs):
            kinds = jnp.max(jnp.where(thin == g, ref[row, :], -1.0), axis=1, keepdims=True)
            for kind in range(SPECIES):
                here = (group == g) & (kinds == kind)
                delta = jnp.where(here, turns[(g - kind) % SPECIES], delta)
        delta_ref[:, half * LANES : (half + 1) * LANES] = delta


def setup(own, below, above, table):
    return pl.pallas_call(
        setup_kernel,
        out_shape=(
            jax.ShapeDtypeStruct((WINDOW, 2 * LANES), f32),
            jax.ShapeDtypeStruct((L2, 2 * LANES), f32),
            jax.ShapeDtypeStruct((L2, 2 * LANES), f32),
        ),
        in_specs=in_vmem(3) + [pl.BlockSpec(memory_space=pltpu.HBM)],
        out_specs=tuple(in_vmem(3)),
        scratch_shapes=[
            pltpu.VMEM((SPECIES, L2 * L2), f32),
            pltpu.VMEM((L2, LANES), f32),
            pltpu.SemaphoreType.DMA((1,)),
        ],
        compiler_params=pltpu.CompilerParams(vmem_limit_bytes=4 * MIB),
        name="setup",
    )(own, below, above, in_hbm(table))


def four_products(product):
    parts = product.reshape(-1, 2, L2, 2 * LANES)
    high, low = parts[:, 0], parts[:, 1]
    return (high[..., :LANES] + high[..., LANES:]) + (low[..., :LANES] + low[..., LANES:])


def first_image_kernel(*refs):
    parts, (tile_ref, image_ref) = refs[:PIECES], refs[PIECES:]
    lane_tile = CENTRE * L2 // LANES * LANES
    before = CENTRE * L2 - lane_tile
    for half in range(2):
        lanes = slice(half * LANES, (half + 1) * LANES)
        right = jnp.concatenate(halves(tile_ref[:, lanes]), axis=1)
        right = jnp.concatenate(
            [
                jnp.zeros((before, 2 * LANES), bf16),
                right,
                jnp.zeros((LANES - before - L2, 2 * LANES), bf16),
            ],
            axis=0,
        )
        for piece, ref in enumerate(parts):
            left = ref[:, lane_tile : lane_tile + LANES]
            product = jnp.dot(left, right, preferred_element_type=f32)
            image_ref[piece * PIECE : (piece + 1) * PIECE, :, lanes] = four_products(product)


def first_images(parts, tile):
    return pl.pallas_call(
        first_image_kernel,
        out_shape=jax.ShapeDtypeStruct((WINDOW, L2, 2 * LANES), f32),
        in_specs=in_vmem(PIECES + 1),
        out_specs=in_vmem(1)[0],
        compiler_params=pltpu.CompilerParams(vmem_limit_bytes=8 * MIB),
        name="first_images",
    )(*parts, tile)


def site_blocks(tile):
    lane = lane_index((L2, LANES))
    masks = [(lane // L2 == s).astype(f32).astype(bf16) for s in range(DEPTH)]
    return jnp.concatenate([tile * mask for mask in masks], axis=0)


def moved(window, cell, half, image):
    blocks = jnp.concatenate([site_blocks(part) for part in halves(image)], axis=1)
    left = window[cell * 2 * L2 : (cell + 1) * 2 * L2, half * LANES : (half + 1) * LANES]
    return four_products(jnp.dot(left, blocks, preferred_element_type=f32))[0]


HIGH_AT = (1, 2)
LOW_AT = (0, 3)


def keep(column, place, half, value):
    rows = slice(place * L2, (place + 1) * L2)
    for at, part in zip((HIGH_AT[half], LOW_AT[half]), halves(value)):
        column[rows, at * LANES : (at + 1) * LANES] = part


def set_images(parts, cells, column, slot):
    high, low = [], []
    for cell in cells:
        ref, base = parts[cell // PIECE], cell % PIECE * 2 * L2
        high.append(ref[base : base + L2, :])
        low.append(ref[base + L2 : base + 2 * L2, :])
    high, low = jnp.concatenate(high, axis=0), jnp.concatenate(low, axis=0)
    own = jnp.dot(high, column[:, : 2 * LANES], preferred_element_type=f32)
    other = jnp.dot(high, column[:, 2 * LANES :], preferred_element_type=f32)
    both = jnp.dot(low, column[:, LANES : 3 * LANES], preferred_element_type=f32)
    shape = (len(cells), L2, LANES)
    image = own[:, :LANES] + own[:, LANES:] + both[:, :LANES]
    slot[: len(cells), :, :LANES] = image.reshape(shape)
    image = other[:, :LANES] + other[:, LANES:] + both[:, LANES:]
    slot[: len(cells), :, LANES:] = image.reshape(shape)


def window_tiles(near, cell):
    dx, dy, dz = cell // 15, cell // 5 % 3, cell % 5 - 2
    own, below, above = (near(dx, dy, i) for i in range(3))
    group = lane_index((L2, LANES)) // L2
    first, second = own, jnp.where(group < 2, above, below)
    if dz > 0:
        first = jnp.where(group < dz, above, own)
        second = jnp.where(group < dz, own, jnp.where(group < 2 + dz, above, below))
    elif dz < 0:
        first = jnp.where(group >= DEPTH + dz, below, own)
        second = jnp.where(group >= DEPTH + dz, own, jnp.where(group < 2 + dz, above, below))
    move = -dz % DEPTH * L2
    return [tile if move == 0 else pltpu.roll(tile, move, 1) for tile in (first, second)]


def set_window(window, near, member_ref, cell):
    base = cell * 2 * L2
    for half, tile in enumerate(window_tiles(near, cell)):
        lanes = slice(half * LANES, (half + 1) * LANES)
        high, low = halves(tile * member_ref[cell : cell + 1, lanes])
        window[base : base + L2, lanes] = high
        window[base + L2 : base + 2 * L2, lanes] = low


def set_column(column, window, tile_ref, cell, image):
    for half in range(2):
        lanes = slice(half * LANES, (half + 1) * LANES)
        value = moved(window, cell, half, image[:, lanes])
        if cell == CENTRE:
            value = value + tile_ref[:, lanes]
        keep(column, cell, half, value)


def early_cells():
    return [cell for cell in range(WINDOW) if cell // 5 % 3 == 1]


def early_kernel(plane_ref, member_ref, tile_ref, image_ref, column, window):
    def near(dx, dy, slab):
        return plane_ref[dx % plane_ref.shape[0], slab]

    for cell in early_cells():
        set_window(window, near, member_ref, cell)
    for cell in early_cells():
        set_column(column, window, tile_ref, cell, image_ref[cell])


def early_columns(plane, member, tile, images):
    return pl.pallas_call(
        early_kernel,
        out_shape=(
            jax.ShapeDtypeStruct((ROWS, 4 * LANES), bf16),
            jax.ShapeDtypeStruct((2 * ROWS, 2 * LANES), bf16),
        ),
        in_specs=in_vmem(4),
        out_specs=tuple(in_vmem(2)),
        compiler_params=pltpu.CompilerParams(vmem_limit_bytes=8 * MIB),
        name="early_columns",
    )(plane, member, tile, images)


def sweep_over(parts, chunks, source, use_image, slots):
    for i, chunk in enumerate(chunks):
        set_images(parts, chunk, source, slots[i % 2])
        if i > 0:
            use_image(i - 1, slots[(i - 1) % 2])
    use_image(len(chunks) - 1, slots[(len(chunks) - 1) % 2])


def delta_blocks(tile):
    high, low = (site_blocks(part) for part in halves(tile))
    return jnp.concatenate(
        [
            jnp.concatenate([high, low], axis=1),
            jnp.concatenate([high, jnp.zeros_like(high)], axis=1),
        ],
        axis=0,
    )


def last_sweep(parts, column, window, tile_ref, delta_ref, stage, sent, local, tau_ref, slots, final):
    deltas = [delta_blocks(delta_ref[:, half * LANES : (half + 1) * LANES]) for half in range(2)]
    group_of = lane_index((L2, LANES)) // L2
    lines = [
        (i, place, cell_of(ox, oy, 0))
        for i, group in enumerate(stage)
        for place, (ox, oy) in enumerate(group)
    ]
    step = stage_lines(stage)
    chunks = [lines[i : i + step] for i in range(0, len(lines), step)]
    places = [(at, oz) for at in range(step) for oz in range(-2, 3)]

    def use_image(number, slot):
        chunk = chunks[number]
        values = []
        for half in range(2):
            lanes = slice(half * LANES, (half + 1) * LANES)
            work = final.at[number % 2, half]
            for row, (at, oz) in enumerate(places[: 5 * len(chunk)]):
                if half == 1 and oz == 0:
                    continue
                cell = chunk[at][2] + oz
                value = moved(window, cell, half, slot[row, :, lanes])
                if cell == CENTRE:
                    value = value + tile_ref[:, lanes]
                    tau_ref[...] = value
                high, low = halves(value)
                work[row * L2 : (row + 1) * L2, :LANES] = high
                work[row * L2 : (row + 1) * L2, LANES:] = low
            count = 5 * len(chunk)
            product = jnp.dot(work[: count * L2, :], deltas[half], preferred_element_type=f32)
            product = product[:, :LANES] + product[:, LANES:]
            values.append(product.reshape(count, L2, LANES))
        for row, (at, oz) in enumerate(places[: 5 * len(chunk)]):
            i, place, _ = chunk[at]
            value = values[0][row]
            local[i][place * 5 + oz + 2] = value
            if oz > 0:
                value = jnp.where(group_of >= DEPTH - oz, values[1][row], value)
            elif oz < 0:
                value = jnp.where(group_of < -oz, values[1][row], value)
            if oz != 0:
                value = pltpu.roll(value, oz % DEPTH * L2, 1)
            sent[i][place * 5 + oz + 2] = value

    cells = [[middle + oz for _, _, middle in chunk for oz in range(-2, 3)] for chunk in chunks]
    sweep_over(parts, cells, column, use_image, slots)


def stage_lines(stage):
    return 2 if sum(len(group) for group in stage) > 2 else 1


def first_kernel(stage, *refs):
    parts, refs = refs[:PIECES], refs[PIECES:]
    early_column, early_window, image_ref, south_ref, north_ref = refs[:5]
    member_ref, tile_ref, delta_ref = refs[5:8]
    sent, local = refs[8 : 8 + len(stage)], refs[8 + len(stage) : 8 + 2 * len(stage)]
    column, window, other, slot_a, slot_b, final = refs[8 + 2 * len(stage) :]
    slots = (slot_a, slot_b)

    def near(dx, dy, slab):
        ref = south_ref if dy == 0 else north_ref
        return ref[dx % ref.shape[0], slab]

    for cell in early_cells():
        rows = slice(cell * L2, (cell + 1) * L2)
        column[rows, :] = early_column[rows, :]
        rows = slice(cell * 2 * L2, (cell + 1) * 2 * L2)
        window[rows, :] = early_window[rows, :]
    late = [cell for cell in range(WINDOW) if cell not in early_cells()]
    for cell in late:
        set_window(window, near, member_ref, cell)
    for cell in late:
        set_column(column, window, tile_ref, cell, image_ref[cell])
    source, target = column, other
    full = [
        list(range(base, min(base + CHUNK, WINDOW))) for base in range(0, WINDOW, CHUNK)
    ]
    for _ in range(1, ITERS - 1):

        def use_image(i, slot, target=target):
            for place, cell in enumerate(full[i]):
                set_column(target, window, tile_ref, cell, slot[place])

        sweep_over(parts, full, source, use_image, slots)
        source, target = target, source
    if source is not column:
        column[...] = source[...]
    last_sweep(
        parts, column, window, tile_ref, delta_ref, stage, sent, local, None, slots, final
    )


def next_kernel(stage, *refs):
    parts, refs = refs[:PIECES], refs[PIECES:]
    column, window, tile_ref, delta_ref = refs[:4]
    sent, local = refs[4 : 4 + len(stage)], refs[4 + len(stage) : 4 + 2 * len(stage)]
    rest = refs[4 + 2 * len(stage) :]
    tau_ref = rest[0] if len(rest) == 4 else None
    slot_a, slot_b, final = rest[-3:]
    last_sweep(
        parts,
        column,
        window,
        tile_ref,
        delta_ref,
        stage,
        sent,
        local,
        tau_ref,
        (slot_a, slot_b),
        final,
    )


def stage_call(kernel, stage, extra_outs, extra_scratch, operands, flops):
    lines = stage_lines(stage)
    longest = max(CHUNK, 5 * lines)
    out_shape = [jax.ShapeDtypeStruct((5 * len(group), L2, LANES), f32) for group in stage] * 2
    out_shape += extra_outs
    return pl.pallas_call(
        functools.partial(kernel, stage),
        out_shape=tuple(out_shape),
        in_specs=in_vmem(len(operands)),
        out_specs=tuple(in_vmem(len(out_shape))),
        scratch_shapes=extra_scratch
        + [pltpu.VMEM((longest, L2, 2 * LANES), f32)] * 2
        + [pltpu.VMEM((2, 2, 5 * lines * L2, 2 * LANES), bf16)],
        compiler_params=pltpu.CompilerParams(vmem_limit_bytes=24 * MIB),
        cost_estimate=pl.CostEstimate(flops=flops, bytes_accessed=MIB, transcendentals=0),
    )(*operands)


def first_stage(stage, parts, column, window, images, south, north, member, tile, delta):
    return stage_call(
        first_kernel,
        stage,
        [
            jax.ShapeDtypeStruct((ROWS, 4 * LANES), bf16),
            jax.ShapeDtypeStruct((2 * ROWS, 2 * LANES), bf16),
        ],
        [pltpu.VMEM((ROWS, 4 * LANES), bf16)],
        (*parts, column, window, images, south, north, member, tile, delta),
        2 * 6 * (ITERS - 2) * ROWS * ROWS * LANES,
    )


def next_stage(stage, parts, column, window, tile, delta):
    tau = [jax.ShapeDtypeStruct((L2, LANES), f32)]
    return stage_call(
        next_kernel,
        stage,
        tau if any((0, 0) in group for group in stage) else [],
        [],
        (*parts, column, window, tile, delta),
        2 * ROWS * ROWS * LANES,
    )


def find_tile(groups, refs, ox, oy, oz):
    for group, ref in zip(groups, refs):
        if (ox, oy) in group:
            return ref[group.index((ox, oy)) * 5 + oz + 2]
    raise ValueError("no tile")


def plane_offsets():
    return [(ox, oy) for ox in (-1, 0, 1) for oy in (-1, 0, 1)]


def cell_of(dx, dy, dz):
    return ((dx + 1) * 3 + dy + 1) * 5 + dz + 2


def turn_kernel(groups, *refs):
    own, out = refs[:-1], refs[-1]
    lane = lane_index((L2, LANES))

    def cell_tile(cell):
        cell = min(cell, WINDOW - 1)
        return find_tile(groups, own, cell // 15 - 1, cell // 5 % 3 - 1, cell % 5 - 2)

    for base in range(0, WINDOW, DEPTH):
        block = jnp.concatenate([cell_tile(base + k) for k in range(DEPTH)], axis=0)
        turned = block.T
        pieces = [turned[s * L2 : (s + 1) * L2] for s in range(DEPTH)]
        for k in range(min(DEPTH, WINDOW - base)):
            value = pieces[0] if k == 0 else pltpu.roll(pieces[0], (-k % DEPTH) * L2, 1)
            for s in range(1, DEPTH):
                move = (s - k) % DEPTH
                piece = pieces[s] if move == 0 else pltpu.roll(pieces[s], move * L2, 1)
                value = jnp.where(lane // L2 == s, piece, value)
            out[base + k] = value


def turned_tiles(groups, own):
    return pl.pallas_call(
        functools.partial(turn_kernel, groups),
        out_shape=jax.ShapeDtypeStruct((WINDOW, L2, LANES), f32),
        in_specs=in_vmem(len(own)),
        out_specs=in_vmem(1)[0],
        compiler_params=pltpu.CompilerParams(vmem_limit_bytes=8 * MIB),
        cost_estimate=pl.CostEstimate(flops=MIB, bytes_accessed=2 * MIB, transcendentals=0),
        name="turned_tiles",
    )(*own)


def add_rows(groups, got, turned_ref, sums):
    for group, ref in zip(groups, got):
        for place, (ox, oy) in enumerate(group):
            for oz in range(-2, 3):
                cell = cell_of(-ox, -oy, -oz)
                value = ref[place * 5 + oz + 2] * turned_ref[cell]
                sums[cell : cell + 1, :] = jnp.sum(value, axis=0, keepdims=True)


def near_kernel(groups, *refs):
    got = refs[: len(groups)]
    turned_ref, tau_ref, sums, flat_ref = refs[len(groups) :]
    flat_kernel(tau_ref, flat_ref)
    sums[...] = jnp.zeros_like(sums)
    add_rows(groups, got, turned_ref, sums)


def near_sums(groups, got, turned, tau):
    return pl.pallas_call(
        functools.partial(near_kernel, groups),
        out_shape=(
            jax.ShapeDtypeStruct((SUM_ROWS, LANES), f32),
            jax.ShapeDtypeStruct((DEPTH, L2 * L2), f32),
        ),
        in_specs=in_vmem(len(got) + 2),
        out_specs=tuple(in_vmem(2)),
        compiler_params=pltpu.CompilerParams(vmem_limit_bytes=8 * MIB),
        name="near_sums",
    )(*got, turned, tau)


def total_kernel(groups, *refs):
    got = refs[: len(groups)]
    turned_ref, near_ref, out_ref, rows = refs[len(groups) :]
    rows[...] = near_ref[...]
    add_rows(groups, got, turned_ref, rows)
    sums = rows[...]
    site = lax.broadcasted_iota(jnp.int32, (8, LANES), 0)
    pick = (lane_index((8, LANES)) // L2 == site).astype(f32).astype(bf16)
    high = sums.astype(bf16)
    rest = sums - high.astype(f32)
    middle = rest.astype(bf16)
    low = (rest - middle.astype(f32)).astype(bf16)
    total = lax.dot_general(
        pick,
        jnp.concatenate([high, middle, low], axis=0),
        (((1,), (1,)), ((), ())),
        preferred_element_type=f32,
    )
    total = (total[:, :SUM_ROWS] + total[:, SUM_ROWS : 2 * SUM_ROWS]) + total[:, 2 * SUM_ROWS :]
    out_ref[...] = total[:DEPTH, :WINDOW]


def total_sums(groups, got, turned, near):
    return pl.pallas_call(
        functools.partial(total_kernel, groups),
        out_shape=jax.ShapeDtypeStruct((DEPTH, WINDOW), f32),
        in_specs=in_vmem(len(got) + 2),
        out_specs=in_vmem(1)[0],
        scratch_shapes=[pltpu.VMEM((SUM_ROWS, LANES), f32)],
        compiler_params=pltpu.CompilerParams(vmem_limit_bytes=8 * MIB),
        name="total_sums",
    )(*got, turned, near)


def plane_offsets():
    return [(ox, oy) for ox in (-1, 0, 1) for oy in (-1, 0, 1)]


def cell_of(dx, dy, dz):
    return ((dx + 1) * 3 + dy + 1) * 5 + dz + 2


def plane_groups():
    counts = (lax.axis_size("gx"), lax.axis_size("gy"))
    groups = {}
    for ox, oy in plane_offsets():
        groups.setdefault((ox % counts[0], oy % counts[1]), []).append((ox, oy))
    return groups


def body(t_matrix, structure, species, members, delta_table):
    own = packed_own(
        t_matrix.reshape(DEPTH, L2 * L2),
        members.reshape(DEPTH, WINDOW),
        species.reshape(1, DEPTH),
    )
    structure = structure[0]

    below, above = shifted(own, (0, 0, 1)), shifted(own, (0, 0, -1))
    first, second = split_piece(0, structure), split_piece(1, structure)
    slabs = jnp.stack([own[:L2], below[:L2], above[:L2]])
    slabs, structure, first, second = lax.optimization_barrier((slabs, structure, first, second))
    if lax.axis_size("gx") == 2:
        sides = [shifted(slabs, (1, 0, 0)), slabs]
    else:
        sides = [shifted(slabs, (1, 0, 0)), slabs, shifted(slabs, (-1, 0, 0))]
    prepared = setup(own, below, above, delta_table)
    plane = jnp.stack(sides)
    plane, structure, *prepared = lax.optimization_barrier((plane, structure, *prepared))
    member, delta, tile = prepared
    south, north = shifted(plane, (0, 1, 0)), shifted(plane, (0, -1, 0))
    parts = (first, second, split_piece(2, structure))
    images = first_images(parts, tile)
    column, window = early_columns(plane, member, tile, images)

    table = plane_groups()
    stages = [
        [shift for shift in table if shift[0] != 0 and shift[1] == 0],
        [shift for shift in table if shift[0] != 0 and shift[1] != 0],
        [shift for shift in table if shift[0] == 0 and shift[1] != 0],
        [(0, 0)],
    ]
    got, local = {}, {}
    for number, stage in enumerate(stages):
        groups = [table[shift] for shift in stage]
        if number == 0:
            *tiles, column, window = first_stage(
                groups, parts, column, window, images, south, north, member, tile, delta
            )
        else:
            tiles = next_stage(groups, parts, column, window, tile, delta)
        if (0, 0) in stage:
            tau = tiles[-1]
        local.update(zip(stage, tiles[len(stage) :]))
        for shift, block in zip(stage, tiles):
            got[shift] = block if shift == (0, 0) else shifted(block, shift + (0,))
    shifts = list(table)
    turned = turned_tiles([table[shift] for shift in shifts], [local[shift] for shift in shifts])
    near_rows, site_tau = near_sums([table[0, 0]], [got[0, 0]], turned, tau)
    far = [shift for shift in shifts if shift != (0, 0)]
    pairs = total_sums(
        [table[shift] for shift in far], [got[shift] for shift in far], turned, near_rows
    )
    return (
        site_tau.reshape(1, 1, 1, DEPTH, L2 * L2),
        pairs.reshape(1, 1, DEPTH, WINDOW),
    )


def solution(mesh):
    placed = (
        P(None, "gx", "gy", "gz", None),
        P(),
        P("gx", "gy", "gz"),
        P("gx", "gy", "gz", None),
        P(),
    )
    return jax.shard_map(
        body,
        mesh=mesh,
        in_specs=placed,
        out_specs=(P(None, "gx", "gy", "gz", None), P("gx", "gy", "gz", None)),
        check_vma=False,
    )
```

```python
import functools

import jax
import jax.numpy as jnp
import numpy as np
from jax import lax
from jax.experimental import pallas as pl
from jax.experimental.pallas import tpu as pltpu
from jax.sharding import PartitionSpec as P


L2 = 32
WINDOW = 45
ITERS = 4
SPECIES = 4
DEPTH = 4
LANES = DEPTH * L2
ROWS = WINDOW * L2
CENTRE = WINDOW // 2
SUM_ROWS = 48
PACK_ROWS = L2 + 8
PIECES = 1
PIECE = WINDOW // PIECES
PIECE_ROWS = PIECE * L2
SPLIT_STEPS = 9
CHUNK = 23
MESH_AXES = ("gx", "gy", "gz")


bf16 = jnp.bfloat16
f32 = jnp.float32
MIB = 1 << 20


def shifted(x, shift):
    sizes = [lax.axis_size(axis) for axis in MESH_AXES]
    pairs = []
    for source in np.ndindex(*sizes):
        target = [(i + d) % n for i, d, n in zip(source, shift, sizes)]
        pairs.append(
            (int(np.ravel_multi_index(source, sizes)), int(np.ravel_multi_index(target, sizes)))
        )
    return lax.ppermute(x, MESH_AXES, pairs)


def in_vmem(count):
    return [pl.BlockSpec(memory_space=pltpu.VMEM)] * count


def in_hbm(x):
    return pltpu.with_memory_space_constraint(x, pltpu.HBM)


def halves(x):
    high = x.astype(bf16)
    return high, (x - high.astype(f32)).astype(bf16)


def lane_index(shape):
    return lax.broadcasted_iota(jnp.int32, shape, len(shape) - 1)


def tile_kernel(flat_ref, tile_ref):
    row = lax.broadcasted_iota(jnp.int32, (DEPTH, LANES), 0)
    diagonal = lane_index((DEPTH, LANES)) // L2 == row
    for j in range(L2 // DEPTH):
        part = flat_ref[:, j * LANES : (j + 1) * LANES]
        rolled = [part] + [pltpu.roll(part, m * L2, 1) for m in range(1, DEPTH)]
        for k in range(DEPTH):
            picked = jnp.zeros((DEPTH, LANES), f32)
            for m in range(DEPTH):
                picked = jnp.where(diagonal & (row == (m + k) % DEPTH), rolled[m], picked)
            a = j * DEPTH + k
            tile_ref[a : a + 1, :] = jnp.sum(picked, axis=0, keepdims=True)


def flat_kernel(tile_ref, flat_ref):
    row = lax.broadcasted_iota(jnp.int32, (DEPTH, LANES), 0)
    diagonal = lane_index((DEPTH, LANES)) // L2 == row
    for j in range(L2 // DEPTH):
        spread = []
        for k in range(DEPTH):
            a = j * DEPTH + k
            line = jnp.broadcast_to(tile_ref[a : a + 1, :], (DEPTH, LANES))
            spread.append(jnp.where(diagonal, line, 0.0))
        value = jnp.zeros((DEPTH, LANES), f32)
        for m in range(DEPTH):
            picked = jnp.zeros((DEPTH, LANES), f32)
            for k in range(DEPTH):
                picked = jnp.where(row == (k - m) % DEPTH, spread[k], picked)
            value = value + (picked if m == 0 else pltpu.roll(picked, m * L2, 1))
        flat_ref[:, j * LANES : (j + 1) * LANES] = value


def pack_kernel(flat_hbm, members_hbm, species_hbm, pack_ref, flat_ref, members_ref, species_ref, sems):
    moves = [(flat_hbm, flat_ref), (members_hbm, members_ref), (species_hbm, species_ref)]
    copies = [
        pltpu.make_async_copy(source, target, sems.at[i])
        for i, (source, target) in enumerate(moves)
    ]
    for copy in copies:
        copy.start()
    for copy in copies:
        copy.wait()
    tile_kernel(flat_ref, pack_ref)
    pack_ref[L2:, :] = jnp.full((PACK_ROWS - L2, LANES), -1.0, f32)
    pack_ref[L2 : L2 + DEPTH, :WINDOW] = members_ref[...].astype(f32)
    pack_ref[L2 + DEPTH : L2 + DEPTH + 1, :DEPTH] = species_ref[...].astype(f32)


def packed_own(flat, members, species):
    return pl.pallas_call(
        pack_kernel,
        out_shape=jax.ShapeDtypeStruct((PACK_ROWS, LANES), f32),
        in_specs=[pl.BlockSpec(memory_space=pltpu.HBM)] * 3,
        out_specs=in_vmem(1)[0],
        scratch_shapes=[
            pltpu.VMEM((DEPTH, L2 * L2), f32),
            pltpu.VMEM((DEPTH, WINDOW), jnp.int32),
            pltpu.VMEM((1, DEPTH), jnp.int32),
            pltpu.SemaphoreType.DMA((3,)),
        ],
        compiler_params=pltpu.CompilerParams(vmem_limit_bytes=4 * MIB),
        name="packed_own",
    )(in_hbm(flat), in_hbm(members), in_hbm(species))


def split_kernel(piece, structure_hbm, parts_ref, buffer, sems):
    step_rows = PIECE_ROWS // SPLIT_STEPS

    def fetch(step):
        rows = pl.ds(piece * PIECE_ROWS + step * step_rows, step_rows)
        return pltpu.make_async_copy(structure_hbm.at[rows, :], buffer.at[step], sems.at[step])

    for step in range(SPLIT_STEPS):
        fetch(step).start()
    half = L2 // 2
    for step in range(SPLIT_STEPS):
        fetch(step).wait()

        def half_cell(i, carry, step=step):
            source = pl.ds(pl.multiple_of(i * half, half), half)
            target = step * 2 * step_rows + i // 2 * 2 * L2 + i % 2 * half
            high, low = halves(buffer[step, source, :])
            parts_ref[pl.ds(pl.multiple_of(target, half), half), :] = high
            parts_ref[pl.ds(pl.multiple_of(target + L2, half), half), :] = low
            return carry

        lax.fori_loop(0, step_rows // half, half_cell, 0, unroll=2)


def split_piece(piece, structure):
    return pl.pallas_call(
        functools.partial(split_kernel, piece),
        out_shape=jax.ShapeDtypeStruct((2 * PIECE_ROWS, ROWS), bf16),
        in_specs=[pl.BlockSpec(memory_space=pltpu.HBM)],
        out_specs=in_vmem(1)[0],
        scratch_shapes=[
            pltpu.VMEM((SPLIT_STEPS, PIECE_ROWS // SPLIT_STEPS, ROWS), f32),
            pltpu.SemaphoreType.DMA((SPLIT_STEPS,)),
        ],
        compiler_params=pltpu.CompilerParams(vmem_limit_bytes=12 * MIB),
        cost_estimate=pl.CostEstimate(
            flops=MIB, bytes_accessed=4 * PIECE_ROWS * ROWS, transcendentals=0
        ),
        name="split_piece",
    )(in_hbm(structure))


def both_tiles(own, below, above):
    lane = lane_index(own.shape)
    return [own, jnp.where(lane < 2 * L2, above, below)]


def setup_kernel(own_ref, below_ref, above_ref, table_hbm, member_ref, delta_ref, tile_ref, *rest):
    table_ref, table_tile, sem = rest
    copy = pltpu.make_async_copy(table_hbm, table_ref, sem.at[0])
    copy.start()
    cells = lax.broadcasted_iota(jnp.int32, (WINDOW, LANES), 0).astype(f32)
    group = lane_index((WINDOW, LANES)) // L2
    sources = [[own_ref] * DEPTH, [above_ref, above_ref, below_ref, below_ref]]
    for half, refs in enumerate(sources):
        member = jnp.zeros((WINDOW, LANES), f32)
        for g, ref in enumerate(refs):
            found = (ref[L2 + g : L2 + g + 1, :] == cells).astype(f32)
            found = jnp.max(found, axis=1, keepdims=True)
            member = jnp.where(group == g, found, member)
        member_ref[:, half * LANES : (half + 1) * LANES] = member
    tiles = both_tiles(own_ref[:L2, :], below_ref[:L2, :], above_ref[:L2, :])
    for half, tile in enumerate(tiles):
        tile_ref[:, half * LANES : (half + 1) * LANES] = tile

    copy.wait()
    tile_kernel(table_ref, table_tile)
    table = table_tile[...]
    turns = [table] + [pltpu.roll(table, m * L2, 1) for m in range(1, SPECIES)]
    group = lane_index((L2, LANES)) // L2
    thin = lane_index((1, LANES))
    row = slice(L2 + DEPTH, L2 + DEPTH + 1)
    for half, refs in enumerate(sources):
        delta = jnp.zeros((L2, LANES), f32)
        for g, ref in enumerate(refs):
            kinds = jnp.max(jnp.where(thin == g, ref[row, :], -1.0), axis=1, keepdims=True)
            for kind in range(SPECIES):
                here = (group == g) & (kinds == kind)
                delta = jnp.where(here, turns[(g - kind) % SPECIES], delta)
        delta_ref[:, half * LANES : (half + 1) * LANES] = delta


def setup(own, below, above, table):
    return pl.pallas_call(
        setup_kernel,
        out_shape=(
            jax.ShapeDtypeStruct((WINDOW, 2 * LANES), f32),
            jax.ShapeDtypeStruct((L2, 2 * LANES), f32),
            jax.ShapeDtypeStruct((L2, 2 * LANES), f32),
        ),
        in_specs=in_vmem(3) + [pl.BlockSpec(memory_space=pltpu.HBM)],
        out_specs=tuple(in_vmem(3)),
        scratch_shapes=[
            pltpu.VMEM((SPECIES, L2 * L2), f32),
            pltpu.VMEM((L2, LANES), f32),
            pltpu.SemaphoreType.DMA((1,)),
        ],
        compiler_params=pltpu.CompilerParams(vmem_limit_bytes=4 * MIB),
        name="setup",
    )(own, below, above, in_hbm(table))


def four_products(product):
    parts = product.reshape(-1, 2, L2, 2 * LANES)
    high, low = parts[:, 0], parts[:, 1]
    return (high[..., :LANES] + high[..., LANES:]) + (low[..., :LANES] + low[..., LANES:])


def first_image_kernel(*refs):
    parts, (tile_ref, image_ref) = refs[:PIECES], refs[PIECES:]
    lane_tile = CENTRE * L2 // LANES * LANES
    before = CENTRE * L2 - lane_tile
    for half in range(2):
        lanes = slice(half * LANES, (half + 1) * LANES)
        right = jnp.concatenate(halves(tile_ref[:, lanes]), axis=1)
        right = jnp.concatenate(
            [
                jnp.zeros((before, 2 * LANES), bf16),
                right,
                jnp.zeros((LANES - before - L2, 2 * LANES), bf16),
            ],
            axis=0,
        )
        for piece, ref in enumerate(parts):
            left = ref[:, lane_tile : lane_tile + LANES]
            product = jnp.dot(left, right, preferred_element_type=f32)
            image_ref[piece * PIECE : (piece + 1) * PIECE, :, lanes] = four_products(product)


def first_images(parts, tile):
    return pl.pallas_call(
        first_image_kernel,
        out_shape=jax.ShapeDtypeStruct((WINDOW, L2, 2 * LANES), f32),
        in_specs=in_vmem(PIECES + 1),
        out_specs=in_vmem(1)[0],
        compiler_params=pltpu.CompilerParams(vmem_limit_bytes=8 * MIB),
        name="first_images",
    )(*parts, tile)


def site_blocks(tile):
    lane = lane_index((L2, LANES))
    masks = [(lane // L2 == s).astype(f32).astype(bf16) for s in range(DEPTH)]
    return jnp.concatenate([tile * mask for mask in masks], axis=0)


def moved(window, cell, half, image):
    blocks = jnp.concatenate([site_blocks(part) for part in halves(image)], axis=1)
    left = window[cell * 2 * L2 : (cell + 1) * 2 * L2, half * LANES : (half + 1) * LANES]
    return four_products(jnp.dot(left, blocks, preferred_element_type=f32))[0]


HIGH_AT = (1, 2)
LOW_AT = (0, 3)


def keep(column, place, half, value):
    rows = slice(place * L2, (place + 1) * L2)
    for at, part in zip((HIGH_AT[half], LOW_AT[half]), halves(value)):
        column[rows, at * LANES : (at + 1) * LANES] = part


def set_images(parts, cells, column, slot):
    high, low = [], []
    for cell in cells:
        ref, base = parts[cell // PIECE], cell % PIECE * 2 * L2
        high.append(ref[base : base + L2, :])
        low.append(ref[base + L2 : base + 2 * L2, :])
    high, low = jnp.concatenate(high, axis=0), jnp.concatenate(low, axis=0)
    own = jnp.dot(high, column[:, : 2 * LANES], preferred_element_type=f32)
    other = jnp.dot(high, column[:, 2 * LANES :], preferred_element_type=f32)
    both = jnp.dot(low, column[:, LANES : 3 * LANES], preferred_element_type=f32)
    shape = (len(cells), L2, LANES)
    image = own[:, :LANES] + own[:, LANES:] + both[:, :LANES]
    slot[: len(cells), :, :LANES] = image.reshape(shape)
    image = other[:, :LANES] + other[:, LANES:] + both[:, LANES:]
    slot[: len(cells), :, LANES:] = image.reshape(shape)


def window_tiles(near, cell):
    dx, dy, dz = cell // 15, cell // 5 % 3, cell % 5 - 2
    own, below, above = (near(dx, dy, i) for i in range(3))
    group = lane_index((L2, LANES)) // L2
    first, second = own, jnp.where(group < 2, above, below)
    if dz > 0:
        first = jnp.where(group < dz, above, own)
        second = jnp.where(group < dz, own, jnp.where(group < 2 + dz, above, below))
    elif dz < 0:
        first = jnp.where(group >= DEPTH + dz, below, own)
        second = jnp.where(group >= DEPTH + dz, own, jnp.where(group < 2 + dz, above, below))
    move = -dz % DEPTH * L2
    return [tile if move == 0 else pltpu.roll(tile, move, 1) for tile in (first, second)]


def set_window(window, near, member_ref, cell):
    base = cell * 2 * L2
    for half, tile in enumerate(window_tiles(near, cell)):
        lanes = slice(half * LANES, (half + 1) * LANES)
        high, low = halves(tile * member_ref[cell : cell + 1, lanes])
        window[base : base + L2, lanes] = high
        window[base + L2 : base + 2 * L2, lanes] = low


def set_column(column, window, tile_ref, cell, image):
    for half in range(2):
        lanes = slice(half * LANES, (half + 1) * LANES)
        value = moved(window, cell, half, image[:, lanes])
        if cell == CENTRE:
            value = value + tile_ref[:, lanes]
        keep(column, cell, half, value)


def early_cells():
    return [cell for cell in range(WINDOW) if cell // 15 == 1 or cell // 5 % 3 == 1]


def near_slabs(own_ref, middle_refs, side_refs):
    def near(dx, dy, slab):
        if dx == 1:
            return own_ref[slab] if dy == 1 else middle_refs[dy // 2][slab]
        ref = side_refs[dy]
        return ref[dx // 2 % ref.shape[0], slab]

    return near


def early_kernel(
    own_ref, south_ref, north_ref, side_ref, member_ref, tile_ref, image_ref, column, window
):
    near = near_slabs(own_ref, (south_ref, north_ref), (None, side_ref, None))
    for cell in early_cells():
        set_window(window, near, member_ref, cell)
    for cell in early_cells():
        set_column(column, window, tile_ref, cell, image_ref[cell])


def early_columns(*operands):
    return pl.pallas_call(
        early_kernel,
        out_shape=(
            jax.ShapeDtypeStruct((ROWS, 4 * LANES), bf16),
            jax.ShapeDtypeStruct((2 * ROWS, 2 * LANES), bf16),
        ),
        in_specs=in_vmem(len(operands)),
        out_specs=tuple(in_vmem(2)),
        compiler_params=pltpu.CompilerParams(vmem_limit_bytes=8 * MIB),
        name="early_columns",
    )(*operands)


def sweep_over(parts, chunks, source, use_image, slots):
    for i, chunk in enumerate(chunks):
        set_images(parts, chunk, source, slots[i % 2])
        if i > 0:
            use_image(i - 1, slots[(i - 1) % 2])
    use_image(len(chunks) - 1, slots[(len(chunks) - 1) % 2])


def delta_blocks(tile):
    high, low = (site_blocks(part) for part in halves(tile))
    return jnp.concatenate(
        [
            jnp.concatenate([high, low], axis=1),
            jnp.concatenate([high, jnp.zeros_like(high)], axis=1),
        ],
        axis=0,
    )


def last_sweep(parts, column, window, tile_ref, delta_ref, stage, sent, local, tau_ref, slots, final):
    deltas = [delta_blocks(delta_ref[:, half * LANES : (half + 1) * LANES]) for half in range(2)]
    group_of = lane_index((L2, LANES)) // L2
    lines = [
        (i, place, cell_of(ox, oy, 0))
        for i, group in enumerate(stage)
        for place, (ox, oy) in enumerate(group)
    ]
    step = stage_lines(stage)
    chunks = [lines[i : i + step] for i in range(0, len(lines), step)]
    places = [(at, oz) for at in range(step) for oz in range(-2, 3)]

    def use_image(number, slot):
        chunk = chunks[number]
        values = []
        for half in range(2):
            lanes = slice(half * LANES, (half + 1) * LANES)
            work = final.at[number % 2, half]
            for row, (at, oz) in enumerate(places[: 5 * len(chunk)]):
                if half == 1 and oz == 0:
                    continue
                cell = chunk[at][2] + oz
                value = moved(window, cell, half, slot[row, :, lanes])
                if cell == CENTRE:
                    value = value + tile_ref[:, lanes]
                    tau_ref[...] = value
                high, low = halves(value)
                work[row * L2 : (row + 1) * L2, :LANES] = high
                work[row * L2 : (row + 1) * L2, LANES:] = low
            count = 5 * len(chunk)
            product = jnp.dot(work[: count * L2, :], deltas[half], preferred_element_type=f32)
            product = product[:, :LANES] + product[:, LANES:]
            values.append(product.reshape(count, L2, LANES))
        for row, (at, oz) in enumerate(places[: 5 * len(chunk)]):
            i, place, _ = chunk[at]
            value = values[0][row]
            local[i][place * 5 + oz + 2] = value
            if oz > 0:
                value = jnp.where(group_of >= DEPTH - oz, values[1][row], value)
            elif oz < 0:
                value = jnp.where(group_of < -oz, values[1][row], value)
            if oz != 0:
                value = pltpu.roll(value, oz % DEPTH * L2, 1)
            sent[i][place * 5 + oz + 2] = value

    cells = [[middle + oz for _, _, middle in chunk for oz in range(-2, 3)] for chunk in chunks]
    sweep_over(parts, cells, column, use_image, slots)


def stage_lines(stage):
    return 2 if sum(len(group) for group in stage) > 2 else 1


def first_kernel(stage, *refs):
    parts, refs = refs[:PIECES], refs[PIECES:]
    early_column, early_window, image_ref, south_ref, north_ref = refs[:5]
    member_ref, tile_ref, delta_ref = refs[5:8]
    sent, local = refs[8 : 8 + len(stage)], refs[8 + len(stage) : 8 + 2 * len(stage)]
    column, window, other, slot_a, slot_b, final = refs[8 + 2 * len(stage) :]
    slots = (slot_a, slot_b)

    near = near_slabs(None, None, (south_ref, None, north_ref))
    for cell in early_cells():
        rows = slice(cell * L2, (cell + 1) * L2)
        column[rows, :] = early_column[rows, :]
        rows = slice(cell * 2 * L2, (cell + 1) * 2 * L2)
        window[rows, :] = early_window[rows, :]
    late = [cell for cell in range(WINDOW) if cell not in early_cells()]
    for cell in late:
        set_window(window, near, member_ref, cell)
    for cell in late:
        set_column(column, window, tile_ref, cell, image_ref[cell])
    source, target = column, other
    full = [
        list(range(base, min(base + CHUNK, WINDOW))) for base in range(0, WINDOW, CHUNK)
    ]
    for _ in range(1, ITERS - 1):

        def use_image(i, slot, target=target):
            for place, cell in enumerate(full[i]):
                set_column(target, window, tile_ref, cell, slot[place])

        sweep_over(parts, full, source, use_image, slots)
        source, target = target, source
    if source is not column:
        column[...] = source[...]
    last_sweep(
        parts, column, window, tile_ref, delta_ref, stage, sent, local, None, slots, final
    )


def next_kernel(stage, *refs):
    parts, refs = refs[:PIECES], refs[PIECES:]
    column, window, tile_ref, delta_ref = refs[:4]
    sent, local = refs[4 : 4 + len(stage)], refs[4 + len(stage) : 4 + 2 * len(stage)]
    rest = refs[4 + 2 * len(stage) :]
    tau_ref = rest[0] if len(rest) == 4 else None
    slot_a, slot_b, final = rest[-3:]
    last_sweep(
        parts,
        column,
        window,
        tile_ref,
        delta_ref,
        stage,
        sent,
        local,
        tau_ref,
        (slot_a, slot_b),
        final,
    )


def stage_call(kernel, stage, extra_outs, extra_scratch, operands, flops):
    lines = stage_lines(stage)
    longest = max(CHUNK, 5 * lines)
    out_shape = [jax.ShapeDtypeStruct((5 * len(group), L2, LANES), f32) for group in stage] * 2
    out_shape += extra_outs
    return pl.pallas_call(
        functools.partial(kernel, stage),
        out_shape=tuple(out_shape),
        in_specs=in_vmem(len(operands)),
        out_specs=tuple(in_vmem(len(out_shape))),
        scratch_shapes=extra_scratch
        + [pltpu.VMEM((longest, L2, 2 * LANES), f32)] * 2
        + [pltpu.VMEM((2, 2, 5 * lines * L2, 2 * LANES), bf16)],
        compiler_params=pltpu.CompilerParams(vmem_limit_bytes=24 * MIB),
        cost_estimate=pl.CostEstimate(flops=flops, bytes_accessed=MIB, transcendentals=0),
    )(*operands)


def first_stage(stage, parts, column, window, images, south, north, member, tile, delta):
    return stage_call(
        first_kernel,
        stage,
        [
            jax.ShapeDtypeStruct((ROWS, 4 * LANES), bf16),
            jax.ShapeDtypeStruct((2 * ROWS, 2 * LANES), bf16),
        ],
        [pltpu.VMEM((ROWS, 4 * LANES), bf16)],
        (*parts, column, window, images, south, north, member, tile, delta),
        2 * 6 * (ITERS - 2) * ROWS * ROWS * LANES,
    )


def next_stage(stage, parts, column, window, tile, delta):
    tau = [jax.ShapeDtypeStruct((L2, LANES), f32)]
    return stage_call(
        next_kernel,
        stage,
        tau if any((0, 0) in group for group in stage) else [],
        [],
        (*parts, column, window, tile, delta),
        2 * ROWS * ROWS * LANES,
    )


def find_tile(groups, refs, ox, oy, oz):
    for group, ref in zip(groups, refs):
        if (ox, oy) in group:
            return ref[group.index((ox, oy)) * 5 + oz + 2]
    raise ValueError("no tile")


def plane_offsets():
    return [(ox, oy) for ox in (-1, 0, 1) for oy in (-1, 0, 1)]


def cell_of(dx, dy, dz):
    return ((dx + 1) * 3 + dy + 1) * 5 + dz + 2


def turn_kernel(groups, *refs):
    own, out = refs[:-1], refs[-1]
    lane = lane_index((L2, LANES))

    def cell_tile(cell):
        cell = min(cell, WINDOW - 1)
        return find_tile(groups, own, cell // 15 - 1, cell // 5 % 3 - 1, cell % 5 - 2)

    for base in range(0, WINDOW, DEPTH):
        block = jnp.concatenate([cell_tile(base + k) for k in range(DEPTH)], axis=0)
        turned = block.T
        pieces = [turned[s * L2 : (s + 1) * L2] for s in range(DEPTH)]
        for k in range(min(DEPTH, WINDOW - base)):
            value = pieces[0] if k == 0 else pltpu.roll(pieces[0], (-k % DEPTH) * L2, 1)
            for s in range(1, DEPTH):
                move = (s - k) % DEPTH
                piece = pieces[s] if move == 0 else pltpu.roll(pieces[s], move * L2, 1)
                value = jnp.where(lane // L2 == s, piece, value)
            out[base + k] = value


def turned_tiles(groups, own):
    return pl.pallas_call(
        functools.partial(turn_kernel, groups),
        out_shape=jax.ShapeDtypeStruct((WINDOW, L2, LANES), f32),
        in_specs=in_vmem(len(own)),
        out_specs=in_vmem(1)[0],
        compiler_params=pltpu.CompilerParams(vmem_limit_bytes=8 * MIB),
        cost_estimate=pl.CostEstimate(flops=MIB, bytes_accessed=2 * MIB, transcendentals=0),
        name="turned_tiles",
    )(*own)


def add_rows(groups, got, turned_ref, sums):
    for group, ref in zip(groups, got):
        for place, (ox, oy) in enumerate(group):
            for oz in range(-2, 3):
                cell = cell_of(-ox, -oy, -oz)
                value = ref[place * 5 + oz + 2] * turned_ref[cell]
                sums[cell : cell + 1, :] = jnp.sum(value, axis=0, keepdims=True)


def near_kernel(groups, *refs):
    got = refs[: len(groups)]
    turned_ref, tau_ref, sums, flat_ref = refs[len(groups) :]
    flat_kernel(tau_ref, flat_ref)
    sums[...] = jnp.zeros_like(sums)
    add_rows(groups, got, turned_ref, sums)


def near_sums(groups, got, turned, tau):
    return pl.pallas_call(
        functools.partial(near_kernel, groups),
        out_shape=(
            jax.ShapeDtypeStruct((SUM_ROWS, LANES), f32),
            jax.ShapeDtypeStruct((DEPTH, L2 * L2), f32),
        ),
        in_specs=in_vmem(len(got) + 2),
        out_specs=tuple(in_vmem(2)),
        compiler_params=pltpu.CompilerParams(vmem_limit_bytes=8 * MIB),
        name="near_sums",
    )(*got, turned, tau)


def total_kernel(groups, *refs):
    got = refs[: len(groups)]
    turned_ref, near_ref, out_ref, rows = refs[len(groups) :]
    rows[...] = near_ref[...]
    add_rows(groups, got, turned_ref, rows)
    sums = rows[...]
    site = lax.broadcasted_iota(jnp.int32, (8, LANES), 0)
    pick = (lane_index((8, LANES)) // L2 == site).astype(f32).astype(bf16)
    high = sums.astype(bf16)
    rest = sums - high.astype(f32)
    middle = rest.astype(bf16)
    low = (rest - middle.astype(f32)).astype(bf16)
    total = lax.dot_general(
        pick,
        jnp.concatenate([high, middle, low], axis=0),
        (((1,), (1,)), ((), ())),
        preferred_element_type=f32,
    )
    total = (total[:, :SUM_ROWS] + total[:, SUM_ROWS : 2 * SUM_ROWS]) + total[:, 2 * SUM_ROWS :]
    out_ref[...] = total[:DEPTH, :WINDOW]


def total_sums(groups, got, turned, near):
    return pl.pallas_call(
        functools.partial(total_kernel, groups),
        out_shape=jax.ShapeDtypeStruct((DEPTH, WINDOW), f32),
        in_specs=in_vmem(len(got) + 2),
        out_specs=in_vmem(1)[0],
        scratch_shapes=[pltpu.VMEM((SUM_ROWS, LANES), f32)],
        compiler_params=pltpu.CompilerParams(vmem_limit_bytes=8 * MIB),
        name="total_sums",
    )(*got, turned, near)


def plane_offsets():
    return [(ox, oy) for ox in (-1, 0, 1) for oy in (-1, 0, 1)]


def cell_of(dx, dy, dz):
    return ((dx + 1) * 3 + dy + 1) * 5 + dz + 2


def plane_groups():
    counts = (lax.axis_size("gx"), lax.axis_size("gy"))
    groups = {}
    for ox, oy in plane_offsets():
        groups.setdefault((ox % counts[0], oy % counts[1]), []).append((ox, oy))
    return groups


def body(t_matrix, structure, species, members, delta_table):
    own = packed_own(
        t_matrix.reshape(DEPTH, L2 * L2),
        members.reshape(DEPTH, WINDOW),
        species.reshape(1, DEPTH),
    )
    structure = structure[0]

    below, above = shifted(own, (0, 0, 1)), shifted(own, (0, 0, -1))
    parts = split_piece(0, structure)
    slabs = jnp.stack([own[:L2], below[:L2], above[:L2]])
    slabs, parts = lax.optimization_barrier((slabs, parts))
    parts = (parts,)
    sides = shifted(slabs, (1, 0, 0))[None]
    if lax.axis_size("gx") > 2:
        sides = jnp.stack([sides[0], shifted(slabs, (-1, 0, 0))])
    south, north = shifted(slabs, (0, 1, 0)), shifted(slabs, (0, -1, 0))
    prepared = setup(own, below, above, delta_table)
    sides, *prepared = lax.optimization_barrier((sides, *prepared))
    member, delta, tile = prepared
    side_south, side_north = shifted(sides, (0, 1, 0)), shifted(sides, (0, -1, 0))
    images = first_images(parts, tile)
    column, window = early_columns(slabs, south, north, sides, member, tile, images)

    table = plane_groups()
    stages = [
        [shift for shift in table if shift[0] != 0 and shift[1] == 0],
        [shift for shift in table if shift[0] != 0 and shift[1] != 0],
        [shift for shift in table if shift[0] == 0 and shift[1] != 0],
        [(0, 0)],
    ]
    got, local = {}, {}
    for number, stage in enumerate(stages):
        groups = [table[shift] for shift in stage]
        if number == 0:
            *tiles, column, window = first_stage(
                groups, parts, column, window, images, side_south, side_north, member, tile, delta
            )
        else:
            tiles = next_stage(groups, parts, column, window, tile, delta)
        if (0, 0) in stage:
            tau = tiles[-1]
        local.update(zip(stage, tiles[len(stage) :]))
        for shift, block in zip(stage, tiles):
            got[shift] = block if shift == (0, 0) else shifted(block, shift + (0,))
    shifts = list(table)
    turned = turned_tiles([table[shift] for shift in shifts], [local[shift] for shift in shifts])
    near_rows, site_tau = near_sums([table[0, 0]], [got[0, 0]], turned, tau)
    far = [shift for shift in shifts if shift != (0, 0)]
    pairs = total_sums(
        [table[shift] for shift in far], [got[shift] for shift in far], turned, near_rows
    )
    return (
        site_tau.reshape(1, 1, 1, DEPTH, L2 * L2),
        pairs.reshape(1, 1, DEPTH, WINDOW),
    )


def solution(mesh):
    placed = (
        P(None, "gx", "gy", "gz", None),
        P(),
        P("gx", "gy", "gz"),
        P("gx", "gy", "gz", None),
        P(),
    )
    return jax.shard_map(
        body,
        mesh=mesh,
        in_specs=placed,
        out_specs=(P(None, "gx", "gy", "gz", None), P("gx", "gy", "gz", None)),
        check_vma=False,
    )
```

```python
import functools

import jax
import jax.numpy as jnp
import numpy as np
from jax import lax
from jax.experimental import pallas as pl
from jax.experimental.pallas import tpu as pltpu
from jax.sharding import PartitionSpec as P


L2 = 32
WINDOW = 45
ITERS = 4
SPECIES = 4
DEPTH = 4
LANES = DEPTH * L2
ROWS = WINDOW * L2
CENTRE = WINDOW // 2
SUM_ROWS = 48
PACK_ROWS = L2 + 8
PIECES = 1
PIECE = WINDOW // PIECES
PIECE_ROWS = PIECE * L2
SPLIT_STEPS = 9
CHUNK = 23
MESH_AXES = ("gx", "gy", "gz")


bf16 = jnp.bfloat16
f32 = jnp.float32
MIB = 1 << 20


def shifted(x, shift):
    sizes = [lax.axis_size(axis) for axis in MESH_AXES]
    pairs = []
    for source in np.ndindex(*sizes):
        target = [(i + d) % n for i, d, n in zip(source, shift, sizes)]
        pairs.append(
            (int(np.ravel_multi_index(source, sizes)), int(np.ravel_multi_index(target, sizes)))
        )
    return lax.ppermute(x, MESH_AXES, pairs)


def in_vmem(count):
    return [pl.BlockSpec(memory_space=pltpu.VMEM)] * count


def in_hbm(x):
    return pltpu.with_memory_space_constraint(x, pltpu.HBM)


def halves(x):
    high = x.astype(bf16)
    return high, (x - high.astype(f32)).astype(bf16)


def lane_index(shape):
    return lax.broadcasted_iota(jnp.int32, shape, len(shape) - 1)


def tile_kernel(flat_ref, tile_ref):
    row = lax.broadcasted_iota(jnp.int32, (DEPTH, LANES), 0)
    diagonal = lane_index((DEPTH, LANES)) // L2 == row
    for j in range(L2 // DEPTH):
        part = flat_ref[:, j * LANES : (j + 1) * LANES]
        rolled = [part] + [pltpu.roll(part, m * L2, 1) for m in range(1, DEPTH)]
        for k in range(DEPTH):
            picked = jnp.zeros((DEPTH, LANES), f32)
            for m in range(DEPTH):
                picked = jnp.where(diagonal & (row == (m + k) % DEPTH), rolled[m], picked)
            a = j * DEPTH + k
            tile_ref[a : a + 1, :] = jnp.sum(picked, axis=0, keepdims=True)


def flat_kernel(tile_ref, flat_ref):
    row = lax.broadcasted_iota(jnp.int32, (DEPTH, LANES), 0)
    diagonal = lane_index((DEPTH, LANES)) // L2 == row
    for j in range(L2 // DEPTH):
        spread = []
        for k in range(DEPTH):
            a = j * DEPTH + k
            line = jnp.broadcast_to(tile_ref[a : a + 1, :], (DEPTH, LANES))
            spread.append(jnp.where(diagonal, line, 0.0))
        value = jnp.zeros((DEPTH, LANES), f32)
        for m in range(DEPTH):
            picked = jnp.zeros((DEPTH, LANES), f32)
            for k in range(DEPTH):
                picked = jnp.where(row == (k - m) % DEPTH, spread[k], picked)
            value = value + (picked if m == 0 else pltpu.roll(picked, m * L2, 1))
        flat_ref[:, j * LANES : (j + 1) * LANES] = value


def pack_kernel(flat_hbm, members_hbm, species_hbm, pack_ref, flat_ref, members_ref, species_ref, sems):
    moves = [(flat_hbm, flat_ref), (members_hbm, members_ref), (species_hbm, species_ref)]
    copies = [
        pltpu.make_async_copy(source, target, sems.at[i])
        for i, (source, target) in enumerate(moves)
    ]
    for copy in copies:
        copy.start()
    for copy in copies:
        copy.wait()
    tile_kernel(flat_ref, pack_ref)
    pack_ref[L2:, :] = jnp.full((PACK_ROWS - L2, LANES), -1.0, f32)
    pack_ref[L2 : L2 + DEPTH, :WINDOW] = members_ref[...].astype(f32)
    pack_ref[L2 + DEPTH : L2 + DEPTH + 1, :DEPTH] = species_ref[...].astype(f32)


def packed_own(flat, members, species):
    return pl.pallas_call(
        pack_kernel,
        out_shape=jax.ShapeDtypeStruct((PACK_ROWS, LANES), f32),
        in_specs=[pl.BlockSpec(memory_space=pltpu.HBM)] * 3,
        out_specs=in_vmem(1)[0],
        scratch_shapes=[
            pltpu.VMEM((DEPTH, L2 * L2), f32),
            pltpu.VMEM((DEPTH, WINDOW), jnp.int32),
            pltpu.VMEM((1, DEPTH), jnp.int32),
            pltpu.SemaphoreType.DMA((3,)),
        ],
        compiler_params=pltpu.CompilerParams(vmem_limit_bytes=4 * MIB),
        name="packed_own",
    )(in_hbm(flat), in_hbm(members), in_hbm(species))


def split_kernel(piece, structure_hbm, parts_ref, buffer, sems):
    step_rows = PIECE_ROWS // SPLIT_STEPS

    def fetch(step):
        rows = pl.ds(piece * PIECE_ROWS + step * step_rows, step_rows)
        return pltpu.make_async_copy(structure_hbm.at[rows, :], buffer.at[step], sems.at[step])

    for step in range(SPLIT_STEPS):
        fetch(step).start()
    half = L2 // 2
    for step in range(SPLIT_STEPS):
        fetch(step).wait()

        def half_cell(i, carry, step=step):
            source = pl.ds(pl.multiple_of(i * half, half), half)
            target = step * 2 * step_rows + i // 2 * 2 * L2 + i % 2 * half
            high, low = halves(buffer[step, source, :])
            parts_ref[pl.ds(pl.multiple_of(target, half), half), :] = high
            parts_ref[pl.ds(pl.multiple_of(target + L2, half), half), :] = low
            return carry

        lax.fori_loop(0, step_rows // half, half_cell, 0, unroll=2)


def split_piece(piece, structure):
    return pl.pallas_call(
        functools.partial(split_kernel, piece),
        out_shape=jax.ShapeDtypeStruct((2 * PIECE_ROWS, ROWS), bf16),
        in_specs=[pl.BlockSpec(memory_space=pltpu.HBM)],
        out_specs=in_vmem(1)[0],
        scratch_shapes=[
            pltpu.VMEM((SPLIT_STEPS, PIECE_ROWS // SPLIT_STEPS, ROWS), f32),
            pltpu.SemaphoreType.DMA((SPLIT_STEPS,)),
        ],
        compiler_params=pltpu.CompilerParams(vmem_limit_bytes=12 * MIB),
        cost_estimate=pl.CostEstimate(
            flops=MIB, bytes_accessed=4 * PIECE_ROWS * ROWS, transcendentals=0
        ),
        name="split_piece",
    )(in_hbm(structure))


def both_tiles(own, below, above):
    lane = lane_index(own.shape)
    return [own, jnp.where(lane < 2 * L2, above, below)]


def setup_kernel(own_ref, below_ref, above_ref, table_hbm, member_ref, delta_ref, tile_ref, *rest):
    table_ref, table_tile, sem = rest
    copy = pltpu.make_async_copy(table_hbm, table_ref, sem.at[0])
    copy.start()
    cells = lax.broadcasted_iota(jnp.int32, (WINDOW, LANES), 0).astype(f32)
    group = lane_index((WINDOW, LANES)) // L2
    sources = [[own_ref] * DEPTH, [above_ref, above_ref, below_ref, below_ref]]
    for half, refs in enumerate(sources):
        member = jnp.zeros((WINDOW, LANES), f32)
        for g, ref in enumerate(refs):
            found = (ref[L2 + g : L2 + g + 1, :] == cells).astype(f32)
            found = jnp.max(found, axis=1, keepdims=True)
            member = jnp.where(group == g, found, member)
        member_ref[:, half * LANES : (half + 1) * LANES] = member
    tiles = both_tiles(own_ref[:L2, :], below_ref[:L2, :], above_ref[:L2, :])
    for half, tile in enumerate(tiles):
        tile_ref[:, half * LANES : (half + 1) * LANES] = tile

    copy.wait()
    tile_kernel(table_ref, table_tile)
    table = table_tile[...]
    turns = [table] + [pltpu.roll(table, m * L2, 1) for m in range(1, SPECIES)]
    group = lane_index((L2, LANES)) // L2
    thin = lane_index((1, LANES))
    row = slice(L2 + DEPTH, L2 + DEPTH + 1)
    for half, refs in enumerate(sources):
        delta = jnp.zeros((L2, LANES), f32)
        for g, ref in enumerate(refs):
            kinds = jnp.max(jnp.where(thin == g, ref[row, :], -1.0), axis=1, keepdims=True)
            for kind in range(SPECIES):
                here = (group == g) & (kinds == kind)
                delta = jnp.where(here, turns[(g - kind) % SPECIES], delta)
        delta_ref[:, half * LANES : (half + 1) * LANES] = delta


def setup(own, below, above, table):
    return pl.pallas_call(
        setup_kernel,
        out_shape=(
            jax.ShapeDtypeStruct((WINDOW, 2 * LANES), f32),
            jax.ShapeDtypeStruct((L2, 2 * LANES), f32),
            jax.ShapeDtypeStruct((L2, 2 * LANES), f32),
        ),
        in_specs=in_vmem(3) + [pl.BlockSpec(memory_space=pltpu.HBM)],
        out_specs=tuple(in_vmem(3)),
        scratch_shapes=[
            pltpu.VMEM((SPECIES, L2 * L2), f32),
            pltpu.VMEM((L2, LANES), f32),
            pltpu.SemaphoreType.DMA((1,)),
        ],
        compiler_params=pltpu.CompilerParams(vmem_limit_bytes=4 * MIB),
        name="setup",
    )(own, below, above, in_hbm(table))


def three_products(product):
    parts = product.reshape(-1, 2, L2, 2 * LANES)
    high, low = parts[:, 0], parts[:, 1]
    return (high[..., :LANES] + high[..., LANES:]) + low[..., :LANES]


def first_image_kernel(*refs):
    parts, (tile_ref, image_ref) = refs[:PIECES], refs[PIECES:]
    lane_tile = CENTRE * L2 // LANES * LANES
    before = CENTRE * L2 - lane_tile
    for half in range(2):
        lanes = slice(half * LANES, (half + 1) * LANES)
        right = jnp.concatenate(halves(tile_ref[:, lanes]), axis=1)
        right = jnp.concatenate(
            [
                jnp.zeros((before, 2 * LANES), bf16),
                right,
                jnp.zeros((LANES - before - L2, 2 * LANES), bf16),
            ],
            axis=0,
        )
        for piece, ref in enumerate(parts):
            left = ref[:, lane_tile : lane_tile + LANES]
            product = jnp.dot(left, right, preferred_element_type=f32)
            image_ref[piece * PIECE : (piece + 1) * PIECE, :, lanes] = three_products(product)


def first_images(parts, tile):
    return pl.pallas_call(
        first_image_kernel,
        out_shape=jax.ShapeDtypeStruct((WINDOW, L2, 2 * LANES), f32),
        in_specs=in_vmem(PIECES + 1),
        out_specs=in_vmem(1)[0],
        compiler_params=pltpu.CompilerParams(vmem_limit_bytes=8 * MIB),
        name="first_images",
    )(*parts, tile)


def site_blocks(tile):
    lane = lane_index((L2, LANES))
    masks = [(lane // L2 == s).astype(f32).astype(bf16) for s in range(DEPTH)]
    return jnp.concatenate([tile * mask for mask in masks], axis=0)


def moved(window, cell, half, image):
    blocks = jnp.concatenate([site_blocks(part) for part in halves(image)], axis=1)
    left = window[cell * 2 * L2 : (cell + 1) * 2 * L2, half * LANES : (half + 1) * LANES]
    return three_products(jnp.dot(left, blocks, preferred_element_type=f32))[0]


HIGH_AT = (1, 2)
LOW_AT = (0, 3)


def keep(column, place, half, value):
    rows = slice(place * L2, (place + 1) * L2)
    for at, part in zip((HIGH_AT[half], LOW_AT[half]), halves(value)):
        column[rows, at * LANES : (at + 1) * LANES] = part


def lane_runs(early):
    per_tile = LANES // L2
    runs = []
    for start in range(0, WINDOW, per_tile):
        cells = range(start, min(start + per_tile, WINDOW))
        if (len(cells) == per_tile and all(c in early_cells() for c in cells)) != early:
            continue
        low, high = cells[0] * L2, (cells[-1] + 1) * L2
        if runs and runs[-1][1] == low:
            runs[-1][1] = high
        else:
            runs.append([low, high])
    return runs


def joined(pieces, axis):
    return pieces[0] if len(pieces) == 1 else jnp.concatenate(pieces, axis=axis)


def set_images(parts, cells, column, slot, runs=((0, ROWS),), start=None):
    def rows_of(base):
        return joined([ref[base : base + L2, low:high] for low, high in runs], 1)

    def lanes_of(first, last):
        return joined([column[low:high, first:last] for low, high in runs], 0)

    high, low = [], []
    for cell in cells:
        ref, base = parts[cell // PIECE], cell % PIECE * 2 * L2
        high.append(rows_of(base))
        low.append(rows_of(base + L2))
    high, low = jnp.concatenate(high, axis=0), jnp.concatenate(low, axis=0)
    own = jnp.dot(high, lanes_of(0, 2 * LANES), preferred_element_type=f32)
    other = jnp.dot(high, lanes_of(2 * LANES, 4 * LANES), preferred_element_type=f32)
    both = jnp.dot(low, lanes_of(LANES, 3 * LANES), preferred_element_type=f32)
    shape = (len(cells), L2, LANES)
    own = own[:, :LANES] + own[:, LANES:] + both[:, :LANES]
    other = other[:, :LANES] + other[:, LANES:] + both[:, LANES:]
    for at, image in enumerate((own, other)):
        image = image.reshape(shape)
        lanes = slice(at * LANES, (at + 1) * LANES)
        if start is not None:
            image = image + start[cells[0] : cells[-1] + 1, :, lanes]
        slot[: len(cells), :, lanes] = image


def window_tiles(near, cell):
    dx, dy, dz = cell // 15, cell // 5 % 3, cell % 5 - 2
    own, below, above = (near(dx, dy, i) for i in range(3))
    group = lane_index((L2, LANES)) // L2
    first, second = own, jnp.where(group < 2, above, below)
    if dz > 0:
        first = jnp.where(group < dz, above, own)
        second = jnp.where(group < dz, own, jnp.where(group < 2 + dz, above, below))
    elif dz < 0:
        first = jnp.where(group >= DEPTH + dz, below, own)
        second = jnp.where(group >= DEPTH + dz, own, jnp.where(group < 2 + dz, above, below))
    move = -dz % DEPTH * L2
    return [tile if move == 0 else pltpu.roll(tile, move, 1) for tile in (first, second)]


def set_window(window, near, member_ref, cell):
    base = cell * 2 * L2
    for half, tile in enumerate(window_tiles(near, cell)):
        lanes = slice(half * LANES, (half + 1) * LANES)
        high, low = halves(tile * member_ref[cell : cell + 1, lanes])
        window[base : base + L2, lanes] = high
        window[base + L2 : base + 2 * L2, lanes] = low


def set_column(column, window, tile_ref, cell, image):
    for half in range(2):
        lanes = slice(half * LANES, (half + 1) * LANES)
        value = moved(window, cell, half, image[:, lanes])
        if cell == CENTRE:
            value = value + tile_ref[:, lanes]
        keep(column, cell, half, value)


def early_cells():
    return [cell for cell in range(WINDOW) if cell // 15 == 1 or cell // 5 % 3 == 1]


def near_slabs(own_ref, middle_refs, side_refs):
    def near(dx, dy, slab):
        if dx == 1:
            return own_ref[slab] if dy == 1 else middle_refs[dy // 2][slab]
        ref = side_refs[dy]
        return ref[dx // 2 % ref.shape[0], slab]

    return near


def sweep_chunks():
    return [list(range(base, min(base + CHUNK, WINDOW))) for base in range(0, WINDOW, CHUNK)]


def early_kernel(parts_count, *refs):
    parts, refs = refs[:parts_count], refs[parts_count:]
    own_ref, south_ref, north_ref, side_ref, member_ref, tile_ref, image_ref = refs[:7]
    column, window, start = refs[7:]
    near = near_slabs(own_ref, (south_ref, north_ref), (None, side_ref, None))
    for cell in early_cells():
        set_window(window, near, member_ref, cell)
    for cell in early_cells():
        set_column(column, window, tile_ref, cell, image_ref[cell])
    for cells in sweep_chunks():
        part = start.at[cells[0] : cells[-1] + 1]
        set_images(parts, cells, column, part, lane_runs(True))


def early_columns(parts, *operands):
    operands = (*parts, *operands)
    return pl.pallas_call(
        functools.partial(early_kernel, len(parts)),
        out_shape=(
            jax.ShapeDtypeStruct((ROWS, 4 * LANES), bf16),
            jax.ShapeDtypeStruct((2 * ROWS, 2 * LANES), bf16),
            jax.ShapeDtypeStruct((WINDOW, L2, 2 * LANES), f32),
        ),
        in_specs=in_vmem(len(operands)),
        out_specs=tuple(in_vmem(3)),
        compiler_params=pltpu.CompilerParams(vmem_limit_bytes=8 * MIB),
        name="early_columns",
    )(*operands)


def sweep_over(parts, chunks, source, use_image, slots, **options):
    for i, chunk in enumerate(chunks):
        set_images(parts, chunk, source, slots[i % 2], **options)
        if i > 0:
            use_image(i - 1, slots[(i - 1) % 2])
    use_image(len(chunks) - 1, slots[(len(chunks) - 1) % 2])


def delta_blocks(tile):
    high, low = (site_blocks(part) for part in halves(tile))
    return jnp.concatenate(
        [
            jnp.concatenate([high, low], axis=1),
            jnp.concatenate([high, jnp.zeros_like(high)], axis=1),
        ],
        axis=0,
    )


def last_sweep(parts, column, window, tile_ref, delta_ref, stage, sent, local, tau_ref, slots, final):
    deltas = [delta_blocks(delta_ref[:, half * LANES : (half + 1) * LANES]) for half in range(2)]
    group_of = lane_index((L2, LANES)) // L2
    lines = [
        (i, place, cell_of(ox, oy, 0))
        for i, group in enumerate(stage)
        for place, (ox, oy) in enumerate(group)
    ]
    step = stage_lines(stage)
    chunks = [lines[i : i + step] for i in range(0, len(lines), step)]
    places = [(at, oz) for at in range(step) for oz in range(-2, 3)]

    def use_image(number, slot):
        chunk = chunks[number]
        values = []
        for half in range(2):
            lanes = slice(half * LANES, (half + 1) * LANES)
            work = final.at[number % 2, half]
            for row, (at, oz) in enumerate(places[: 5 * len(chunk)]):
                if half == 1 and oz == 0:
                    continue
                cell = chunk[at][2] + oz
                value = moved(window, cell, half, slot[row, :, lanes])
                if cell == CENTRE:
                    value = value + tile_ref[:, lanes]
                    tau_ref[...] = value
                high, low = halves(value)
                work[row * L2 : (row + 1) * L2, :LANES] = high
                work[row * L2 : (row + 1) * L2, LANES:] = low
            count = 5 * len(chunk)
            product = jnp.dot(work[: count * L2, :], deltas[half], preferred_element_type=f32)
            product = product[:, :LANES] + product[:, LANES:]
            values.append(product.reshape(count, L2, LANES))
        for row, (at, oz) in enumerate(places[: 5 * len(chunk)]):
            i, place, _ = chunk[at]
            value = values[0][row]
            local[i][place * 5 + oz + 2] = value
            if oz > 0:
                value = jnp.where(group_of >= DEPTH - oz, values[1][row], value)
            elif oz < 0:
                value = jnp.where(group_of < -oz, values[1][row], value)
            if oz != 0:
                value = pltpu.roll(value, oz % DEPTH * L2, 1)
            sent[i][place * 5 + oz + 2] = value

    cells = [[middle + oz for _, _, middle in chunk for oz in range(-2, 3)] for chunk in chunks]
    sweep_over(parts, cells, column, use_image, slots)


def stage_lines(stage):
    return 2 if sum(len(group) for group in stage) > 2 else 1


def first_kernel(stage, *refs):
    parts, refs = refs[:PIECES], refs[PIECES:]
    early_column, early_window, start, image_ref, south_ref, north_ref = refs[:6]
    member_ref, tile_ref, delta_ref = refs[6:9]
    sent, local = refs[9 : 9 + len(stage)], refs[9 + len(stage) : 9 + 2 * len(stage)]
    column, window, other, slot_a, slot_b, final = refs[9 + 2 * len(stage) :]
    slots = (slot_a, slot_b)

    near = near_slabs(None, None, (south_ref, None, north_ref))
    for cell in early_cells():
        rows = slice(cell * L2, (cell + 1) * L2)
        column[rows, :] = early_column[rows, :]
        rows = slice(cell * 2 * L2, (cell + 1) * 2 * L2)
        window[rows, :] = early_window[rows, :]
    late = [cell for cell in range(WINDOW) if cell not in early_cells()]
    for cell in late:
        set_window(window, near, member_ref, cell)
    for cell in late:
        set_column(column, window, tile_ref, cell, image_ref[cell])
    source, target = column, other
    full = sweep_chunks()
    for sweep in range(1, ITERS - 1):

        def use_image(i, slot, target=target):
            for place, cell in enumerate(full[i]):
                set_column(target, window, tile_ref, cell, slot[place])

        if sweep == 1:
            options = dict(runs=lane_runs(False), start=start)
        else:
            options = {}
        sweep_over(parts, full, source, use_image, slots, **options)
        source, target = target, source
    if source is not column:
        column[...] = source[...]
    last_sweep(
        parts, column, window, tile_ref, delta_ref, stage, sent, local, None, slots, final
    )


def next_kernel(stage, *refs):
    parts, refs = refs[:PIECES], refs[PIECES:]
    column, window, tile_ref, delta_ref = refs[:4]
    sent, local = refs[4 : 4 + len(stage)], refs[4 + len(stage) : 4 + 2 * len(stage)]
    rest = refs[4 + 2 * len(stage) :]
    tau_ref = rest[0] if len(rest) == 4 else None
    slot_a, slot_b, final = rest[-3:]
    last_sweep(
        parts,
        column,
        window,
        tile_ref,
        delta_ref,
        stage,
        sent,
        local,
        tau_ref,
        (slot_a, slot_b),
        final,
    )


def stage_call(kernel, stage, extra_outs, extra_scratch, operands, flops):
    lines = stage_lines(stage)
    longest = max(CHUNK, 5 * lines)
    out_shape = [jax.ShapeDtypeStruct((5 * len(group), L2, LANES), f32) for group in stage] * 2
    out_shape += extra_outs
    return pl.pallas_call(
        functools.partial(kernel, stage),
        out_shape=tuple(out_shape),
        in_specs=in_vmem(len(operands)),
        out_specs=tuple(in_vmem(len(out_shape))),
        scratch_shapes=extra_scratch
        + [pltpu.VMEM((longest, L2, 2 * LANES), f32)] * 2
        + [pltpu.VMEM((2, 2, 5 * lines * L2, 2 * LANES), bf16)],
        compiler_params=pltpu.CompilerParams(vmem_limit_bytes=24 * MIB),
        cost_estimate=pl.CostEstimate(flops=flops, bytes_accessed=MIB, transcendentals=0),
    )(*operands)


def first_stage(stage, parts, *operands):
    return stage_call(
        first_kernel,
        stage,
        [
            jax.ShapeDtypeStruct((ROWS, 4 * LANES), bf16),
            jax.ShapeDtypeStruct((2 * ROWS, 2 * LANES), bf16),
        ],
        [pltpu.VMEM((ROWS, 4 * LANES), bf16)],
        (*parts, *operands),
        2 * 6 * (ITERS - 2) * ROWS * ROWS * LANES,
    )


def next_stage(stage, parts, column, window, tile, delta):
    tau = [jax.ShapeDtypeStruct((L2, LANES), f32)]
    return stage_call(
        next_kernel,
        stage,
        tau if any((0, 0) in group for group in stage) else [],
        [],
        (*parts, column, window, tile, delta),
        2 * ROWS * ROWS * LANES,
    )


def find_tile(groups, refs, ox, oy, oz):
    for group, ref in zip(groups, refs):
        if (ox, oy) in group:
            return ref[group.index((ox, oy)) * 5 + oz + 2]
    raise ValueError("no tile")


def plane_offsets():
    return [(ox, oy) for ox in (-1, 0, 1) for oy in (-1, 0, 1)]


def cell_of(dx, dy, dz):
    return ((dx + 1) * 3 + dy + 1) * 5 + dz + 2


def turn_kernel(groups, *refs):
    own, out = refs[:-1], refs[-1]
    lane = lane_index((L2, LANES))

    def cell_tile(cell):
        cell = min(cell, WINDOW - 1)
        return find_tile(groups, own, cell // 15 - 1, cell // 5 % 3 - 1, cell % 5 - 2)

    for base in range(0, WINDOW, DEPTH):
        block = jnp.concatenate([cell_tile(base + k) for k in range(DEPTH)], axis=0)
        turned = block.T
        pieces = [turned[s * L2 : (s + 1) * L2] for s in range(DEPTH)]
        for k in range(min(DEPTH, WINDOW - base)):
            value = pieces[0] if k == 0 else pltpu.roll(pieces[0], (-k % DEPTH) * L2, 1)
            for s in range(1, DEPTH):
                move = (s - k) % DEPTH
                piece = pieces[s] if move == 0 else pltpu.roll(pieces[s], move * L2, 1)
                value = jnp.where(lane // L2 == s, piece, value)
            out[base + k] = value


def turned_tiles(groups, own):
    return pl.pallas_call(
        functools.partial(turn_kernel, groups),
        out_shape=jax.ShapeDtypeStruct((WINDOW, L2, LANES), f32),
        in_specs=in_vmem(len(own)),
        out_specs=in_vmem(1)[0],
        compiler_params=pltpu.CompilerParams(vmem_limit_bytes=8 * MIB),
        cost_estimate=pl.CostEstimate(flops=MIB, bytes_accessed=2 * MIB, transcendentals=0),
        name="turned_tiles",
    )(*own)


def add_rows(groups, got, turned_ref, sums):
    for group, ref in zip(groups, got):
        for place, (ox, oy) in enumerate(group):
            for oz in range(-2, 3):
                cell = cell_of(-ox, -oy, -oz)
                value = ref[place * 5 + oz + 2] * turned_ref[cell]
                sums[cell : cell + 1, :] = jnp.sum(value, axis=0, keepdims=True)


def near_kernel(groups, *refs):
    got = refs[: len(groups)]
    turned_ref, tau_ref, sums, flat_ref = refs[len(groups) :]
    flat_kernel(tau_ref, flat_ref)
    sums[...] = jnp.zeros_like(sums)
    add_rows(groups, got, turned_ref, sums)


def near_sums(groups, got, turned, tau):
    return pl.pallas_call(
        functools.partial(near_kernel, groups),
        out_shape=(
            jax.ShapeDtypeStruct((SUM_ROWS, LANES), f32),
            jax.ShapeDtypeStruct((DEPTH, L2 * L2), f32),
        ),
        in_specs=in_vmem(len(got) + 2),
        out_specs=tuple(in_vmem(2)),
        compiler_params=pltpu.CompilerParams(vmem_limit_bytes=8 * MIB),
        name="near_sums",
    )(*got, turned, tau)


def total_kernel(groups, *refs):
    got = refs[: len(groups)]
    turned_ref, near_ref, out_ref, rows = refs[len(groups) :]
    rows[...] = near_ref[...]
    add_rows(groups, got, turned_ref, rows)
    sums = rows[...]
    site = lax.broadcasted_iota(jnp.int32, (8, LANES), 0)
    pick = (lane_index((8, LANES)) // L2 == site).astype(f32).astype(bf16)
    high = sums.astype(bf16)
    rest = sums - high.astype(f32)
    middle = rest.astype(bf16)
    low = (rest - middle.astype(f32)).astype(bf16)
    total = lax.dot_general(
        pick,
        jnp.concatenate([high, middle, low], axis=0),
        (((1,), (1,)), ((), ())),
        preferred_element_type=f32,
    )
    total = (total[:, :SUM_ROWS] + total[:, SUM_ROWS : 2 * SUM_ROWS]) + total[:, 2 * SUM_ROWS :]
    out_ref[...] = total[:DEPTH, :WINDOW]


def total_sums(groups, got, turned, near):
    return pl.pallas_call(
        functools.partial(total_kernel, groups),
        out_shape=jax.ShapeDtypeStruct((DEPTH, WINDOW), f32),
        in_specs=in_vmem(len(got) + 2),
        out_specs=in_vmem(1)[0],
        scratch_shapes=[pltpu.VMEM((SUM_ROWS, LANES), f32)],
        compiler_params=pltpu.CompilerParams(vmem_limit_bytes=8 * MIB),
        name="total_sums",
    )(*got, turned, near)


def plane_offsets():
    return [(ox, oy) for ox in (-1, 0, 1) for oy in (-1, 0, 1)]


def cell_of(dx, dy, dz):
    return ((dx + 1) * 3 + dy + 1) * 5 + dz + 2


def plane_groups():
    counts = (lax.axis_size("gx"), lax.axis_size("gy"))
    groups = {}
    for ox, oy in plane_offsets():
        groups.setdefault((ox % counts[0], oy % counts[1]), []).append((ox, oy))
    return groups


def body(t_matrix, structure, species, members, delta_table):
    own = packed_own(
        t_matrix.reshape(DEPTH, L2 * L2),
        members.reshape(DEPTH, WINDOW),
        species.reshape(1, DEPTH),
    )
    structure = structure[0]

    below, above = shifted(own, (0, 0, 1)), shifted(own, (0, 0, -1))
    parts = split_piece(0, structure)
    slabs = jnp.stack([own[:L2], below[:L2], above[:L2]])
    slabs, parts = lax.optimization_barrier((slabs, parts))
    parts = (parts,)
    sides = shifted(slabs, (1, 0, 0))[None]
    if lax.axis_size("gx") > 2:
        sides = jnp.stack([sides[0], shifted(slabs, (-1, 0, 0))])
    south, north = shifted(slabs, (0, 1, 0)), shifted(slabs, (0, -1, 0))
    prepared = setup(own, below, above, delta_table)
    sides, *prepared = lax.optimization_barrier((sides, *prepared))
    member, delta, tile = prepared
    side_south, side_north = shifted(sides, (0, 1, 0)), shifted(sides, (0, -1, 0))
    images = first_images(parts, tile)
    early = early_columns(parts, slabs, south, north, sides, member, tile, images)

    table = plane_groups()
    stages = [
        [shift for shift in table if shift[0] != 0 and shift[1] == 0],
        [shift for shift in table if shift[0] != 0 and shift[1] == 1],
        [shift for shift in table if shift[0] == 0 and shift[1] != 0],
        [shift for shift in table if shift[0] != 0 and shift[1] > 1],
        [(0, 0)],
    ]
    got, local = {}, {}
    for number, stage in enumerate(stages):
        groups = [table[shift] for shift in stage]
        if number == 0:
            *tiles, column, window = first_stage(
                groups, parts, *early, images, side_south, side_north, member, tile, delta
            )
        else:
            tiles = next_stage(groups, parts, column, window, tile, delta)
        if (0, 0) in stage:
            tau = tiles[-1]
        local.update(zip(stage, tiles[len(stage) :]))
        for shift, block in zip(stage, tiles):
            got[shift] = block if shift == (0, 0) else shifted(block, shift + (0,))
    shifts = list(table)
    turned = turned_tiles([table[shift] for shift in shifts], [local[shift] for shift in shifts])
    near_rows, site_tau = near_sums([table[0, 0]], [got[0, 0]], turned, tau)
    far = [shift for shift in shifts if shift != (0, 0)]
    pairs = total_sums(
        [table[shift] for shift in far], [got[shift] for shift in far], turned, near_rows
    )
    return (
        site_tau.reshape(1, 1, 1, DEPTH, L2 * L2),
        pairs.reshape(1, 1, DEPTH, WINDOW),
    )


def solution(mesh):
    placed = (
        P(None, "gx", "gy", "gz", None),
        P(),
        P("gx", "gy", "gz"),
        P("gx", "gy", "gz", None),
        P(),
    )
    return jax.shard_map(
        body,
        mesh=mesh,
        in_specs=placed,
        out_specs=(P(None, "gx", "gy", "gz", None), P("gx", "gy", "gz", None)),
        check_vma=False,
    )
```

```python
import functools

import jax
import jax.numpy as jnp
import numpy as np
from jax import lax
from jax.experimental import pallas as pl
from jax.experimental.pallas import tpu as pltpu
from jax.sharding import PartitionSpec as P


L2 = 32
WINDOW = 45
ITERS = 4
SPECIES = 4
DEPTH = 4
LANES = DEPTH * L2
ROWS = WINDOW * L2
CENTRE = WINDOW // 2
SUM_ROWS = 48
PACK_ROWS = L2 + 8
PIECES = 1
PIECE = WINDOW // PIECES
PIECE_ROWS = PIECE * L2
SPLIT_STEPS = 9
CHUNK = 23
MESH_AXES = ("gx", "gy", "gz")

PLAN = (("x",), ("xy+", "y+"), ("xy-", "y-"), ("own",))


bf16 = jnp.bfloat16
f32 = jnp.float32
MIB = 1 << 20


def shifted(x, shift):
    sizes = [lax.axis_size(axis) for axis in MESH_AXES]
    pairs = []
    for source in np.ndindex(*sizes):
        target = [(i + d) % n for i, d, n in zip(source, shift, sizes)]
        pairs.append(
            (int(np.ravel_multi_index(source, sizes)), int(np.ravel_multi_index(target, sizes)))
        )
    return lax.ppermute(x, MESH_AXES, pairs)


def in_vmem(count):
    return [pl.BlockSpec(memory_space=pltpu.VMEM)] * count


def in_hbm(x):
    return pltpu.with_memory_space_constraint(x, pltpu.HBM)


def halves(x):
    high = x.astype(bf16)
    return high, (x - high.astype(f32)).astype(bf16)


def lane_index(shape):
    return lax.broadcasted_iota(jnp.int32, shape, len(shape) - 1)


def tile_kernel(flat_ref, tile_ref):
    row = lax.broadcasted_iota(jnp.int32, (DEPTH, LANES), 0)
    diagonal = lane_index((DEPTH, LANES)) // L2 == row
    for j in range(L2 // DEPTH):
        part = flat_ref[:, j * LANES : (j + 1) * LANES]
        rolled = [part] + [pltpu.roll(part, m * L2, 1) for m in range(1, DEPTH)]
        for k in range(DEPTH):
            picked = jnp.zeros((DEPTH, LANES), f32)
            for m in range(DEPTH):
                picked = jnp.where(diagonal & (row == (m + k) % DEPTH), rolled[m], picked)
            a = j * DEPTH + k
            tile_ref[a : a + 1, :] = jnp.sum(picked, axis=0, keepdims=True)


def flat_kernel(tile_ref, flat_ref):
    row = lax.broadcasted_iota(jnp.int32, (DEPTH, LANES), 0)
    diagonal = lane_index((DEPTH, LANES)) // L2 == row
    for j in range(L2 // DEPTH):
        spread = []
        for k in range(DEPTH):
            a = j * DEPTH + k
            line = jnp.broadcast_to(tile_ref[a : a + 1, :], (DEPTH, LANES))
            spread.append(jnp.where(diagonal, line, 0.0))
        value = jnp.zeros((DEPTH, LANES), f32)
        for m in range(DEPTH):
            picked = jnp.zeros((DEPTH, LANES), f32)
            for k in range(DEPTH):
                picked = jnp.where(row == (k - m) % DEPTH, spread[k], picked)
            value = value + (picked if m == 0 else pltpu.roll(picked, m * L2, 1))
        flat_ref[:, j * LANES : (j + 1) * LANES] = value


def pack_kernel(flat_hbm, members_hbm, species_hbm, pack_ref, flat_ref, members_ref, species_ref, sems):
    moves = [(flat_hbm, flat_ref), (members_hbm, members_ref), (species_hbm, species_ref)]
    copies = [
        pltpu.make_async_copy(source, target, sems.at[i])
        for i, (source, target) in enumerate(moves)
    ]
    for copy in copies:
        copy.start()
    for copy in copies:
        copy.wait()
    tile_kernel(flat_ref, pack_ref)
    pack_ref[L2:, :] = jnp.full((PACK_ROWS - L2, LANES), -1.0, f32)
    pack_ref[L2 : L2 + DEPTH, :WINDOW] = members_ref[...].astype(f32)
    pack_ref[L2 + DEPTH : L2 + DEPTH + 1, :DEPTH] = species_ref[...].astype(f32)


def packed_own(flat, members, species):
    return pl.pallas_call(
        pack_kernel,
        out_shape=jax.ShapeDtypeStruct((PACK_ROWS, LANES), f32),
        in_specs=[pl.BlockSpec(memory_space=pltpu.HBM)] * 3,
        out_specs=in_vmem(1)[0],
        scratch_shapes=[
            pltpu.VMEM((DEPTH, L2 * L2), f32),
            pltpu.VMEM((DEPTH, WINDOW), jnp.int32),
            pltpu.VMEM((1, DEPTH), jnp.int32),
            pltpu.SemaphoreType.DMA((3,)),
        ],
        compiler_params=pltpu.CompilerParams(vmem_limit_bytes=4 * MIB),
        name="packed_own",
    )(in_hbm(flat), in_hbm(members), in_hbm(species))


def split_kernel(piece, structure_hbm, parts_ref, buffer, sems):
    step_rows = PIECE_ROWS // SPLIT_STEPS

    def fetch(step):
        rows = pl.ds(piece * PIECE_ROWS + step * step_rows, step_rows)
        return pltpu.make_async_copy(structure_hbm.at[rows, :], buffer.at[step], sems.at[step])

    for step in range(SPLIT_STEPS):
        fetch(step).start()
    half = L2 // 2
    for step in range(SPLIT_STEPS):
        fetch(step).wait()

        def half_cell(i, carry, step=step):
            source = pl.ds(pl.multiple_of(i * half, half), half)
            target = step * 2 * step_rows + i // 2 * 2 * L2 + i % 2 * half
            high, low = halves(buffer[step, source, :])
            parts_ref[pl.ds(pl.multiple_of(target, half), half), :] = high
            parts_ref[pl.ds(pl.multiple_of(target + L2, half), half), :] = low
            return carry

        lax.fori_loop(0, step_rows // half, half_cell, 0, unroll=2)


def split_piece(piece, structure):
    return pl.pallas_call(
        functools.partial(split_kernel, piece),
        out_shape=jax.ShapeDtypeStruct((2 * PIECE_ROWS, ROWS), bf16),
        in_specs=[pl.BlockSpec(memory_space=pltpu.HBM)],
        out_specs=in_vmem(1)[0],
        scratch_shapes=[
            pltpu.VMEM((SPLIT_STEPS, PIECE_ROWS // SPLIT_STEPS, ROWS), f32),
            pltpu.SemaphoreType.DMA((SPLIT_STEPS,)),
        ],
        compiler_params=pltpu.CompilerParams(vmem_limit_bytes=12 * MIB),
        cost_estimate=pl.CostEstimate(
            flops=MIB, bytes_accessed=4 * PIECE_ROWS * ROWS, transcendentals=0
        ),
        name="split_piece",
    )(in_hbm(structure))


def both_tiles(own, below, above):
    lane = lane_index(own.shape)
    return [own, jnp.where(lane < 2 * L2, above, below)]


def setup_kernel(own_ref, below_ref, above_ref, table_hbm, member_ref, delta_ref, tile_ref, *rest):
    table_ref, table_tile, sem = rest
    copy = pltpu.make_async_copy(table_hbm, table_ref, sem.at[0])
    copy.start()
    cells = lax.broadcasted_iota(jnp.int32, (WINDOW, LANES), 0).astype(f32)
    group = lane_index((WINDOW, LANES)) // L2
    sources = [[own_ref] * DEPTH, [above_ref, above_ref, below_ref, below_ref]]
    for half, refs in enumerate(sources):
        member = jnp.zeros((WINDOW, LANES), f32)
        for g, ref in enumerate(refs):
            found = (ref[L2 + g : L2 + g + 1, :] == cells).astype(f32)
            found = jnp.max(found, axis=1, keepdims=True)
            member = jnp.where(group == g, found, member)
        member_ref[:, half * LANES : (half + 1) * LANES] = member
    tiles = both_tiles(own_ref[:L2, :], below_ref[:L2, :], above_ref[:L2, :])
    for half, tile in enumerate(tiles):
        tile_ref[:, half * LANES : (half + 1) * LANES] = tile

    copy.wait()
    tile_kernel(table_ref, table_tile)
    table = table_tile[...]
    turns = [table] + [pltpu.roll(table, m * L2, 1) for m in range(1, SPECIES)]
    group = lane_index((L2, LANES)) // L2
    thin = lane_index((1, LANES))
    row = slice(L2 + DEPTH, L2 + DEPTH + 1)
    for half, refs in enumerate(sources):
        delta = jnp.zeros((L2, LANES), f32)
        for g, ref in enumerate(refs):
            kinds = jnp.max(jnp.where(thin == g, ref[row, :], -1.0), axis=1, keepdims=True)
            for kind in range(SPECIES):
                here = (group == g) & (kinds == kind)
                delta = jnp.where(here, turns[(g - kind) % SPECIES], delta)
        delta_ref[:, half * LANES : (half + 1) * LANES] = delta


def setup(own, below, above, table):
    return pl.pallas_call(
        setup_kernel,
        out_shape=(
            jax.ShapeDtypeStruct((WINDOW, 2 * LANES), f32),
            jax.ShapeDtypeStruct((L2, 2 * LANES), f32),
            jax.ShapeDtypeStruct((L2, 2 * LANES), f32),
        ),
        in_specs=in_vmem(3) + [pl.BlockSpec(memory_space=pltpu.HBM)],
        out_specs=tuple(in_vmem(3)),
        scratch_shapes=[
            pltpu.VMEM((SPECIES, L2 * L2), f32),
            pltpu.VMEM((L2, LANES), f32),
            pltpu.SemaphoreType.DMA((1,)),
        ],
        compiler_params=pltpu.CompilerParams(vmem_limit_bytes=4 * MIB),
        name="setup",
    )(own, below, above, in_hbm(table))


def three_products(product):
    parts = product.reshape(-1, 2, L2, 2 * LANES)
    high, low = parts[:, 0], parts[:, 1]
    return (high[..., :LANES] + high[..., LANES:]) + low[..., :LANES]


def first_image_kernel(*refs):
    parts, (tile_ref, image_ref) = refs[:PIECES], refs[PIECES:]
    lane_tile = CENTRE * L2 // LANES * LANES
    before = CENTRE * L2 - lane_tile
    for half in range(2):
        lanes = slice(half * LANES, (half + 1) * LANES)
        right = jnp.concatenate(halves(tile_ref[:, lanes]), axis=1)
        right = jnp.concatenate(
            [
                jnp.zeros((before, 2 * LANES), bf16),
                right,
                jnp.zeros((LANES - before - L2, 2 * LANES), bf16),
            ],
            axis=0,
        )
        for piece, ref in enumerate(parts):
            left = ref[:, lane_tile : lane_tile + LANES]
            product = jnp.dot(left, right, preferred_element_type=f32)
            image_ref[piece * PIECE : (piece + 1) * PIECE, :, lanes] = three_products(product)


def first_images(parts, tile):
    return pl.pallas_call(
        first_image_kernel,
        out_shape=jax.ShapeDtypeStruct((WINDOW, L2, 2 * LANES), f32),
        in_specs=in_vmem(PIECES + 1),
        out_specs=in_vmem(1)[0],
        compiler_params=pltpu.CompilerParams(vmem_limit_bytes=8 * MIB),
        name="first_images",
    )(*parts, tile)


def site_blocks(tile):
    lane = lane_index((L2, LANES))
    masks = [(lane // L2 == s).astype(f32).astype(bf16) for s in range(DEPTH)]
    return jnp.concatenate([tile * mask for mask in masks], axis=0)


def moved(window, cell, half, image):
    blocks = jnp.concatenate([site_blocks(part) for part in halves(image)], axis=1)
    left = window[cell * 2 * L2 : (cell + 1) * 2 * L2, half * LANES : (half + 1) * LANES]
    return three_products(jnp.dot(left, blocks, preferred_element_type=f32))[0]


HIGH_AT = (1, 2)
LOW_AT = (0, 3)


def keep(column, place, half, value):
    rows = slice(place * L2, (place + 1) * L2)
    for at, part in zip((HIGH_AT[half], LOW_AT[half]), halves(value)):
        column[rows, at * LANES : (at + 1) * LANES] = part


def lane_runs(early):
    per_tile = LANES // L2
    runs = []
    for start in range(0, WINDOW, per_tile):
        cells = range(start, min(start + per_tile, WINDOW))
        if (len(cells) == per_tile and all(c in early_cells() for c in cells)) != early:
            continue
        low, high = cells[0] * L2, (cells[-1] + 1) * L2
        if runs and runs[-1][1] == low:
            runs[-1][1] = high
        else:
            runs.append([low, high])
    return runs


def joined(pieces, axis):
    return pieces[0] if len(pieces) == 1 else jnp.concatenate(pieces, axis=axis)


def set_images(parts, cells, column, slot, runs=((0, ROWS),), start=None):
    def rows_of(base):
        return joined([ref[base : base + L2, low:high] for low, high in runs], 1)

    def lanes_of(first, last):
        return joined([column[low:high, first:last] for low, high in runs], 0)

    high, low = [], []
    for cell in cells:
        ref, base = parts[cell // PIECE], cell % PIECE * 2 * L2
        high.append(rows_of(base))
        low.append(rows_of(base + L2))
    high, low = jnp.concatenate(high, axis=0), jnp.concatenate(low, axis=0)
    own = jnp.dot(high, lanes_of(0, 2 * LANES), preferred_element_type=f32)
    other = jnp.dot(high, lanes_of(2 * LANES, 4 * LANES), preferred_element_type=f32)
    both = jnp.dot(low, lanes_of(LANES, 3 * LANES), preferred_element_type=f32)
    shape = (len(cells), L2, LANES)
    own = own[:, :LANES] + own[:, LANES:] + both[:, :LANES]
    other = other[:, :LANES] + other[:, LANES:] + both[:, LANES:]
    for at, image in enumerate((own, other)):
        image = image.reshape(shape)
        lanes = slice(at * LANES, (at + 1) * LANES)
        if start is not None:
            image = image + start[cells[0] : cells[-1] + 1, :, lanes]
        slot[: len(cells), :, lanes] = image


def window_tiles(near, cell):
    dx, dy, dz = cell // 15, cell // 5 % 3, cell % 5 - 2
    own, below, above = (near(dx, dy, i) for i in range(3))
    group = lane_index((L2, LANES)) // L2
    first, second = own, jnp.where(group < 2, above, below)
    if dz > 0:
        first = jnp.where(group < dz, above, own)
        second = jnp.where(group < dz, own, jnp.where(group < 2 + dz, above, below))
    elif dz < 0:
        first = jnp.where(group >= DEPTH + dz, below, own)
        second = jnp.where(group >= DEPTH + dz, own, jnp.where(group < 2 + dz, above, below))
    move = -dz % DEPTH * L2
    return [tile if move == 0 else pltpu.roll(tile, move, 1) for tile in (first, second)]


def set_window(window, near, member_ref, cell):
    base = cell * 2 * L2
    for half, tile in enumerate(window_tiles(near, cell)):
        lanes = slice(half * LANES, (half + 1) * LANES)
        high, low = halves(tile * member_ref[cell : cell + 1, lanes])
        window[base : base + L2, lanes] = high
        window[base + L2 : base + 2 * L2, lanes] = low


def set_column(column, window, tile_ref, cell, image):
    for half in range(2):
        lanes = slice(half * LANES, (half + 1) * LANES)
        value = moved(window, cell, half, image[:, lanes])
        if cell == CENTRE:
            value = value + tile_ref[:, lanes]
        keep(column, cell, half, value)


def early_cells():
    return [cell for cell in range(WINDOW) if cell // 15 == 1 or cell // 5 % 3 == 1]


def near_slabs(own_ref, middle_refs, side_refs):
    def near(dx, dy, slab):
        if dx == 1:
            return own_ref[slab] if dy == 1 else middle_refs[dy // 2][slab]
        ref = side_refs[dy]
        return ref[dx // 2 % ref.shape[0], slab]

    return near


def sweep_chunks():
    return [list(range(base, min(base + CHUNK, WINDOW))) for base in range(0, WINDOW, CHUNK)]


def early_kernel(parts_count, *refs):
    parts, refs = refs[:parts_count], refs[parts_count:]
    own_ref, south_ref, north_ref, side_ref, member_ref, tile_ref, image_ref = refs[:7]
    column, window, start = refs[7:]
    near = near_slabs(own_ref, (south_ref, north_ref), (None, side_ref, None))
    for cell in early_cells():
        set_window(window, near, member_ref, cell)
    for cell in early_cells():
        set_column(column, window, tile_ref, cell, image_ref[cell])
    for cells in sweep_chunks():
        part = start.at[cells[0] : cells[-1] + 1]
        set_images(parts, cells, column, part, lane_runs(True))


def early_columns(parts, *operands):
    operands = (*parts, *operands)
    return pl.pallas_call(
        functools.partial(early_kernel, len(parts)),
        out_shape=(
            jax.ShapeDtypeStruct((ROWS, 4 * LANES), bf16),
            jax.ShapeDtypeStruct((2 * ROWS, 2 * LANES), bf16),
            jax.ShapeDtypeStruct((WINDOW, L2, 2 * LANES), f32),
        ),
        in_specs=in_vmem(len(operands)),
        out_specs=tuple(in_vmem(3)),
        compiler_params=pltpu.CompilerParams(vmem_limit_bytes=8 * MIB),
        name="early_columns",
    )(*operands)


def sweep_over(parts, chunks, source, use_image, slots, **options):
    for i, chunk in enumerate(chunks):
        set_images(parts, chunk, source, slots[i % 2], **options)
        if i > 0:
            use_image(i - 1, slots[(i - 1) % 2])
    use_image(len(chunks) - 1, slots[(len(chunks) - 1) % 2])


def delta_blocks(tile):
    high, low = (site_blocks(part) for part in halves(tile))
    return jnp.concatenate(
        [
            jnp.concatenate([high, low], axis=1),
            jnp.concatenate([high, jnp.zeros_like(high)], axis=1),
        ],
        axis=0,
    )


def last_sweep(parts, column, window, tile_ref, delta_ref, stage, sent, local, tau_ref, slots, final):
    deltas = [delta_blocks(delta_ref[:, half * LANES : (half + 1) * LANES]) for half in range(2)]
    group_of = lane_index((L2, LANES)) // L2
    lines = [
        (i, place, cell_of(ox, oy, 0))
        for i, group in enumerate(stage)
        for place, (ox, oy) in enumerate(group)
    ]
    step = stage_lines(stage)
    chunks = [lines[i : i + step] for i in range(0, len(lines), step)]
    places = [(at, oz) for at in range(step) for oz in range(-2, 3)]

    def use_image(number, slot):
        chunk = chunks[number]
        values = []
        for half in range(2):
            lanes = slice(half * LANES, (half + 1) * LANES)
            work = final.at[number % 2, half]
            for row, (at, oz) in enumerate(places[: 5 * len(chunk)]):
                if half == 1 and oz == 0:
                    continue
                cell = chunk[at][2] + oz
                value = moved(window, cell, half, slot[row, :, lanes])
                if cell == CENTRE:
                    value = value + tile_ref[:, lanes]
                    tau_ref[...] = value
                high, low = halves(value)
                work[row * L2 : (row + 1) * L2, :LANES] = high
                work[row * L2 : (row + 1) * L2, LANES:] = low
            count = 5 * len(chunk)
            product = jnp.dot(work[: count * L2, :], deltas[half], preferred_element_type=f32)
            product = product[:, :LANES] + product[:, LANES:]
            values.append(product.reshape(count, L2, LANES))
        for row, (at, oz) in enumerate(places[: 5 * len(chunk)]):
            i, place, _ = chunk[at]
            value = values[0][row]
            local[i][place * 5 + oz + 2] = value
            if oz > 0:
                value = jnp.where(group_of >= DEPTH - oz, values[1][row], value)
            elif oz < 0:
                value = jnp.where(group_of < -oz, values[1][row], value)
            if oz != 0:
                value = pltpu.roll(value, oz % DEPTH * L2, 1)
            sent[i][place * 5 + oz + 2] = value

    cells = [[middle + oz for _, _, middle in chunk for oz in range(-2, 3)] for chunk in chunks]
    sweep_over(parts, cells, column, use_image, slots)


def stage_lines(stage):
    return 2 if sum(len(group) for group in stage) > 2 else 1


def first_kernel(stage, *refs):
    parts, refs = refs[:PIECES], refs[PIECES:]
    early_column, early_window, start, image_ref, south_ref, north_ref = refs[:6]
    member_ref, tile_ref, delta_ref = refs[6:9]
    sent, local = refs[9 : 9 + len(stage)], refs[9 + len(stage) : 9 + 2 * len(stage)]
    column, window, other, slot_a, slot_b, final = refs[9 + 2 * len(stage) :]
    slots = (slot_a, slot_b)

    near = near_slabs(None, None, (south_ref, None, north_ref))
    for cell in early_cells():
        rows = slice(cell * L2, (cell + 1) * L2)
        column[rows, :] = early_column[rows, :]
        rows = slice(cell * 2 * L2, (cell + 1) * 2 * L2)
        window[rows, :] = early_window[rows, :]
    late = [cell for cell in range(WINDOW) if cell not in early_cells()]
    for cell in late:
        set_window(window, near, member_ref, cell)
    for cell in late:
        set_column(column, window, tile_ref, cell, image_ref[cell])
    source, target = column, other
    full = sweep_chunks()
    for sweep in range(1, ITERS - 1):

        def use_image(i, slot, target=target):
            for place, cell in enumerate(full[i]):
                set_column(target, window, tile_ref, cell, slot[place])

        if sweep == 1:
            options = dict(runs=lane_runs(False), start=start)
        else:
            options = {}
        sweep_over(parts, full, source, use_image, slots, **options)
        source, target = target, source
    if source is not column:
        column[...] = source[...]
    last_sweep(
        parts, column, window, tile_ref, delta_ref, stage, sent, local, None, slots, final
    )


def next_kernel(stage, *refs):
    parts, refs = refs[:PIECES], refs[PIECES:]
    column, window, tile_ref, delta_ref = refs[:4]
    sent, local = refs[4 : 4 + len(stage)], refs[4 + len(stage) : 4 + 2 * len(stage)]
    rest = refs[4 + 2 * len(stage) :]
    tau_ref = rest[0] if len(rest) == 4 else None
    slot_a, slot_b, final = rest[-3:]
    last_sweep(
        parts,
        column,
        window,
        tile_ref,
        delta_ref,
        stage,
        sent,
        local,
        tau_ref,
        (slot_a, slot_b),
        final,
    )


def stage_call(kernel, stage, extra_outs, extra_scratch, operands, flops):
    lines = stage_lines(stage)
    longest = max(CHUNK, 5 * lines)
    out_shape = [jax.ShapeDtypeStruct((5 * len(group), L2, LANES), f32) for group in stage] * 2
    out_shape += extra_outs
    return pl.pallas_call(
        functools.partial(kernel, stage),
        out_shape=tuple(out_shape),
        in_specs=in_vmem(len(operands)),
        out_specs=tuple(in_vmem(len(out_shape))),
        scratch_shapes=extra_scratch
        + [pltpu.VMEM((longest, L2, 2 * LANES), f32)] * 2
        + [pltpu.VMEM((2, 2, 5 * lines * L2, 2 * LANES), bf16)],
        compiler_params=pltpu.CompilerParams(vmem_limit_bytes=24 * MIB),
        cost_estimate=pl.CostEstimate(flops=flops, bytes_accessed=MIB, transcendentals=0),
    )(*operands)


def first_stage(stage, parts, *operands):
    return stage_call(
        first_kernel,
        stage,
        [
            jax.ShapeDtypeStruct((ROWS, 4 * LANES), bf16),
            jax.ShapeDtypeStruct((2 * ROWS, 2 * LANES), bf16),
        ],
        [pltpu.VMEM((ROWS, 4 * LANES), bf16)],
        (*parts, *operands),
        2 * 6 * (ITERS - 2) * ROWS * ROWS * LANES,
    )


def next_stage(stage, parts, column, window, tile, delta):
    tau = [jax.ShapeDtypeStruct((L2, LANES), f32)]
    return stage_call(
        next_kernel,
        stage,
        tau if any((0, 0) in group for group in stage) else [],
        [],
        (*parts, column, window, tile, delta),
        2 * ROWS * ROWS * LANES,
    )


def find_tile(groups, refs, ox, oy, oz):
    for group, ref in zip(groups, refs):
        if (ox, oy) in group:
            return ref[group.index((ox, oy)) * 5 + oz + 2]
    raise ValueError("no tile")


def plane_offsets():
    return [(ox, oy) for ox in (-1, 0, 1) for oy in (-1, 0, 1)]


def cell_of(dx, dy, dz):
    return ((dx + 1) * 3 + dy + 1) * 5 + dz + 2


def turn_kernel(groups, *refs):
    own, out = refs[:-1], refs[-1]
    lane = lane_index((L2, LANES))

    def cell_tile(cell):
        cell = min(cell, WINDOW - 1)
        return find_tile(groups, own, cell // 15 - 1, cell // 5 % 3 - 1, cell % 5 - 2)

    for base in range(0, WINDOW, DEPTH):
        block = jnp.concatenate([cell_tile(base + k) for k in range(DEPTH)], axis=0)
        turned = block.T
        pieces = [turned[s * L2 : (s + 1) * L2] for s in range(DEPTH)]
        for k in range(min(DEPTH, WINDOW - base)):
            value = pieces[0] if k == 0 else pltpu.roll(pieces[0], (-k % DEPTH) * L2, 1)
            for s in range(1, DEPTH):
                move = (s - k) % DEPTH
                piece = pieces[s] if move == 0 else pltpu.roll(pieces[s], move * L2, 1)
                value = jnp.where(lane // L2 == s, piece, value)
            out[base + k] = value


def turned_tiles(groups, own):
    return pl.pallas_call(
        functools.partial(turn_kernel, groups),
        out_shape=jax.ShapeDtypeStruct((WINDOW, L2, LANES), f32),
        in_specs=in_vmem(len(own)),
        out_specs=in_vmem(1)[0],
        compiler_params=pltpu.CompilerParams(vmem_limit_bytes=8 * MIB),
        cost_estimate=pl.CostEstimate(flops=MIB, bytes_accessed=2 * MIB, transcendentals=0),
        name="turned_tiles",
    )(*own)


def add_rows(groups, got, turned_ref, sums):
    for group, ref in zip(groups, got):
        for place, (ox, oy) in enumerate(group):
            for oz in range(-2, 3):
                cell = cell_of(-ox, -oy, -oz)
                value = ref[place * 5 + oz + 2] * turned_ref[cell]
                sums[cell : cell + 1, :] = jnp.sum(value, axis=0, keepdims=True)


def near_kernel(groups, *refs):
    got = refs[: len(groups)]
    turned_ref, tau_ref, sums, flat_ref = refs[len(groups) :]
    flat_kernel(tau_ref, flat_ref)
    sums[...] = jnp.zeros_like(sums)
    add_rows(groups, got, turned_ref, sums)


def near_sums(groups, got, turned, tau):
    return pl.pallas_call(
        functools.partial(near_kernel, groups),
        out_shape=(
            jax.ShapeDtypeStruct((SUM_ROWS, LANES), f32),
            jax.ShapeDtypeStruct((DEPTH, L2 * L2), f32),
        ),
        in_specs=in_vmem(len(got) + 2),
        out_specs=tuple(in_vmem(2)),
        compiler_params=pltpu.CompilerParams(vmem_limit_bytes=8 * MIB),
        name="near_sums",
    )(*got, turned, tau)


def total_kernel(groups, *refs):
    got = refs[: len(groups)]
    turned_ref, near_ref, out_ref, rows = refs[len(groups) :]
    rows[...] = near_ref[...]
    add_rows(groups, got, turned_ref, rows)
    sums = rows[...]
    site = lax.broadcasted_iota(jnp.int32, (8, LANES), 0)
    pick = (lane_index((8, LANES)) // L2 == site).astype(f32).astype(bf16)
    high = sums.astype(bf16)
    rest = sums - high.astype(f32)
    middle = rest.astype(bf16)
    low = (rest - middle.astype(f32)).astype(bf16)
    total = lax.dot_general(
        pick,
        jnp.concatenate([high, middle, low], axis=0),
        (((1,), (1,)), ((), ())),
        preferred_element_type=f32,
    )
    total = (total[:, :SUM_ROWS] + total[:, SUM_ROWS : 2 * SUM_ROWS]) + total[:, 2 * SUM_ROWS :]
    out_ref[...] = total[:DEPTH, :WINDOW]


def total_sums(groups, got, turned, near):
    return pl.pallas_call(
        functools.partial(total_kernel, groups),
        out_shape=jax.ShapeDtypeStruct((DEPTH, WINDOW), f32),
        in_specs=in_vmem(len(got) + 2),
        out_specs=in_vmem(1)[0],
        scratch_shapes=[pltpu.VMEM((SUM_ROWS, LANES), f32)],
        compiler_params=pltpu.CompilerParams(vmem_limit_bytes=8 * MIB),
        name="total_sums",
    )(*got, turned, near)


def plane_offsets():
    return [(ox, oy) for ox in (-1, 0, 1) for oy in (-1, 0, 1)]


def cell_of(dx, dy, dz):
    return ((dx + 1) * 3 + dy + 1) * 5 + dz + 2


def kind_of(shift):
    if shift == (0, 0):
        return "own"
    if shift[1] == 0:
        return "x"
    return ("y" if shift[0] == 0 else "xy") + ("+" if shift[1] == 1 else "-")


def plane_groups():
    counts = (lax.axis_size("gx"), lax.axis_size("gy"))
    groups = {}
    for ox, oy in plane_offsets():
        groups.setdefault((ox % counts[0], oy % counts[1]), []).append((ox, oy))
    return groups


def body(t_matrix, structure, species, members, delta_table):
    own = packed_own(
        t_matrix.reshape(DEPTH, L2 * L2),
        members.reshape(DEPTH, WINDOW),
        species.reshape(1, DEPTH),
    )
    structure = structure[0]

    below, above = shifted(own, (0, 0, 1)), shifted(own, (0, 0, -1))
    parts = split_piece(0, structure)
    slabs = jnp.stack([own[:L2], below[:L2], above[:L2]])
    slabs, parts = lax.optimization_barrier((slabs, parts))
    parts = (parts,)
    sides = shifted(slabs, (1, 0, 0))[None]
    if lax.axis_size("gx") > 2:
        sides = jnp.stack([sides[0], shifted(slabs, (-1, 0, 0))])
    south, north = shifted(slabs, (0, 1, 0)), shifted(slabs, (0, -1, 0))
    prepared = setup(own, below, above, delta_table)
    sides, *prepared = lax.optimization_barrier((sides, *prepared))
    member, delta, tile = prepared
    side_south, side_north = shifted(sides, (0, 1, 0)), shifted(sides, (0, -1, 0))
    images = first_images(parts, tile)
    early = early_columns(parts, slabs, south, north, sides, member, tile, images)

    table = plane_groups()
    stages = [[shift for shift in table if kind_of(shift) in kinds] for kinds in PLAN]
    got, local = {}, {}
    for number, stage in enumerate(stages):
        groups = [table[shift] for shift in stage]
        if number == 0:
            *tiles, column, window = first_stage(
                groups, parts, *early, images, side_south, side_north, member, tile, delta
            )
        else:
            tiles = next_stage(groups, parts, column, window, tile, delta)
        if (0, 0) in stage:
            tau = tiles[-1]
        local.update(zip(stage, tiles[len(stage) :]))
        for shift, block in zip(stage, tiles):
            got[shift] = block if shift == (0, 0) else shifted(block, shift + (0,))
    shifts = list(table)
    turned = turned_tiles([table[shift] for shift in shifts], [local[shift] for shift in shifts])
    near_rows, site_tau = near_sums([table[0, 0]], [got[0, 0]], turned, tau)
    far = [shift for shift in shifts if shift != (0, 0)]
    pairs = total_sums(
        [table[shift] for shift in far], [got[shift] for shift in far], turned, near_rows
    )
    return (
        site_tau.reshape(1, 1, 1, DEPTH, L2 * L2),
        pairs.reshape(1, 1, DEPTH, WINDOW),
    )


def solution(mesh):
    placed = (
        P(None, "gx", "gy", "gz", None),
        P(),
        P("gx", "gy", "gz"),
        P("gx", "gy", "gz", None),
        P(),
    )
    return jax.shard_map(
        body,
        mesh=mesh,
        in_specs=placed,
        out_specs=(P(None, "gx", "gy", "gz", None), P("gx", "gy", "gz", None)),
        check_vma=False,
    )
```
